32 devices in a mesh: pt: 8 (over y, x, core), md: 4 (over z).
Axes of the slice: x: 2, y: 2, z: 4, core: 2. Of those that a mesh axis runs over, the one named last changes fastest.
Arguments:
- grid_index: int32 [3, 8192], P(None, 'pt'), may hold values from 0 to 255, as said below
- wavenumbers: int32 [3, 32768], P(None, 'md'), may hold values from -16 to 15, as said below
- test_block: int32 [32768, 256], P('md'), may hold values from -64 to 63
- slab_counts: int32 [8], P('pt'), may hold values from 1 to 1024, as said below
Outputs:
- adjoint_sketch: float32 [32768, 512], P(('md', 'pt'))
The draws below stay inside these ranges and needn't reach their ends.
Inputs may be any that keep to these rules, and one draw needn't show every extreme that they name: Each slab's live points are its first slab_counts slots; in every draw one slab is full with 1024. `grid_index`: every slot's point lies in the ball of radius 256 // 2 - 1 about the grid cell (128, 128, 128). `wavenumbers`: the columns are the 32 x 32 x 32 tensor grid of wavenumber triples, each exactly once, in some order.
All inputs are finite; a program needn't handle non-finite values.
Results may differ from the reference program's by a relative error of at most 0.002.
Values may be sent and summed in bfloat16 or wider, within the bound.
A program may use at most 192 MiB of HBM per device.

```python
import math
import jax
import jax.numpy as jnp
from jax import lax

KAXIS = 32
M = 32768
R = 256
G = 256
PERIOD = 512
CAP = 1024
P_SIZE = 8192
N_PT = 8


def draw_slab_counts(key, part):
    slab_index = jnp.arange(N_PT, dtype=jnp.int32)
    distance = jnp.abs(2 * slab_index + 1 - N_PT)
    nominal = CAP - distance * (3 * CAP // 4) // N_PT
    jitter = jax.random.randint(jax.random.fold_in(key, 1), (N_PT,), 0, CAP // 8 + 1)
    counts = jnp.maximum(nominal - jitter, CAP // 8)
    full_slab = jax.random.randint(jax.random.fold_in(key, 2), (), N_PT // 4, N_PT - N_PT // 4)
    return jnp.where(slab_index == full_slab, CAP, counts).astype(jnp.int32)


def draw_grid_index(key, part):
    middle = G // 2
    radius = G // 2 - 1
    candidates = jax.random.randint(jax.random.fold_in(key, 11), (8, 3, P_SIZE), 0, G).astype(jnp.int32)
    offsets = candidates - middle
    inside = (jnp.sum(offsets * offsets, axis=1) <= radius * radius).astype(jnp.int32)
    chosen = jnp.argmax(inside, axis=0).astype(jnp.int32)
    picked = jnp.take_along_axis(candidates, jnp.broadcast_to(chosen[None, None, :], (1, 3, P_SIZE)), axis=0)[0]
    fallback = candidates[0] // 2 + G // 4
    found = jnp.max(inside, axis=0) > 0
    return jnp.where(found[None, :], picked, fallback).astype(jnp.int32)


def draw_wavenumbers(key, part):
    order = jax.random.permutation(jax.random.fold_in(key, 21), M).astype(jnp.int32)
    rows = jnp.stack([order // (KAXIS * KAXIS), order // KAXIS % KAXIS, order % KAXIS], axis=0)
    return (rows - KAXIS // 2).astype(jnp.int32)


def with_ends(entries, own_key, low, high):
    longest = entries.shape.index(max(entries.shape))
    spots = []
    for shift in (0, 1):
        where = [jax.random.randint(jax.random.fold_in(own_key, axis), (), 0, length) for axis, length in enumerate(entries.shape)]
        where[longest] = (where[longest] + shift) % entries.shape[longest]
        spots.append(tuple(where))
    return entries.at[spots[0]].set(low).at[spots[1]].set(high)


def setup_inputs(seed: int = 0) -> dict:
    seeds = jax.random.split(jax.random.key(seed), 5)
    grid_index = draw_grid_index(jax.random.fold_in(seeds[4], 71), 0)
    wavenumbers = draw_wavenumbers(jax.random.fold_in(seeds[4], 71), 0)
    test_block = with_ends(jax.random.randint(seeds[2], (M, R), -64, 64), jax.random.fold_in(seeds[2], 1), -64, 63).astype(jnp.int32)
    slab_counts = draw_slab_counts(jax.random.fold_in(seeds[4], 71), 0)
    return {"grid_index": grid_index, "wavenumbers": wavenumbers, "test_block": test_block, "slab_counts": slab_counts}


def phase_pair(coords, wave_cols, in_use):
    turns = coords[0][:, None] * wave_cols[0][None, :] + coords[1][:, None] * wave_cols[1][None, :] + coords[2][:, None] * wave_cols[2][None, :]
    turns = jnp.mod(turns, PERIOD).astype(jnp.int32)
    angles = turns.astype(jnp.float32) * (2.0 * math.pi / PERIOD)
    tile_re = jnp.where(in_use[:, None], jnp.cos(angles), 0.0).astype(jnp.bfloat16)
    tile_im = jnp.where(in_use[:, None], jnp.sin(angles), 0.0).astype(jnp.bfloat16)
    return (tile_re, tile_im)

def reference(grid_index, wavenumbers, test_block, slab_counts):
    block = min(512, CAP)
    block_count = P_SIZE // block
    slots = jnp.arange(P_SIZE, dtype=jnp.int32)
    live_rows = slots % CAP < slab_counts[slots // CAP]
    test_float = test_block.astype(jnp.float32)
    hp = lax.Precision.HIGHEST
    y_scale = 1.0 / (32.0 * math.sqrt(M))
    w_scale = 1.0 / math.sqrt(P_SIZE)

    def tiles_of(step_index):
        first = (step_index * block).astype(jnp.int32)
        coords = lax.dynamic_slice(grid_index, (jnp.int32(0), first), (3, block))
        in_use = lax.dynamic_slice_in_dim(live_rows, first, block, 0)
        return phase_pair(coords, wavenumbers, in_use)

    def sketch_block(step_index):
        tile_re, tile_im = tiles_of(step_index)
        part_re = jnp.dot(tile_re.astype(jnp.float32), test_float, precision=hp)
        part_im = jnp.dot(tile_im.astype(jnp.float32), test_float, precision=hp)
        return (jnp.concatenate([part_re, part_im], axis=1) * y_scale).astype(jnp.bfloat16)
    sketch = lax.map(sketch_block, jnp.arange(block_count, dtype=jnp.int32)).reshape(P_SIZE, 2 * R)

    def adjoint_step(summed, step_index):
        tile_re, tile_im = tiles_of(step_index)
        rows = lax.dynamic_slice_in_dim(sketch, (step_index * block).astype(jnp.int32), block, 0).astype(jnp.float32)
        from_re = jnp.dot(tile_re.astype(jnp.float32).T, rows, precision=hp)
        from_im = jnp.dot(tile_im.astype(jnp.float32).T, rows, precision=hp)
        piece = jnp.concatenate([from_re[:, :R] + from_im[:, R:], from_re[:, R:] - from_im[:, :R]], axis=1)
        return (summed + piece, None)
    summed, unused = lax.scan(adjoint_step, jnp.zeros((M, 2 * R), jnp.float32), jnp.arange(block_count, dtype=jnp.int32))
    return summed * w_scale
```

```python
import functools
import math

import jax
import jax.numpy as jnp
from jax import lax
from jax.experimental import pallas as pl
from jax.experimental.pallas import tpu as pltpu
from jax.sharding import PartitionSpec as P

M = 32768
PERIOD = 512
DEPTH = 128
TILE = 256
STRIP = 32
SKETCH = (2048, 512, 512)
MARKS = (10, 11, 13, 15, 17, 20, 23, 26, 29)
BLOCK = 128
CHUNK = 512
ROWS = 640
MAKES = (3, 3, 3, 3, 2, 2, 2, 2)

S = (4.4428679, -7.3074434, 3.59478791, -0.78437358)
C = (1.41420408, -6.97764202, 5.71523797, -1.72834735)


def phases(whole_turns):
    r = whole_turns - jnp.round(whole_turns)
    z = r * r
    s = (((S[3] * z + S[2]) * z + S[1]) * z + S[0]) * r
    c = ((C[3] * z + C[2]) * z + C[1]) * z + C[0]
    return 1.0 - s * s, s * c


def sketch_kernel(
    dtype, count_ref, points_ref, waves_ref, test_ref, result_ref, turns_ref, lhs_ref, out_ref, cast_ref
):
    width, tile, step = test_ref.shape[1], turns_ref.shape[1], test_ref.shape[0]
    chunk = turns_ref.shape[2]

    @pl.when(pl.program_id(0) == 0)
    def _():
        out_ref[...] = jnp.zeros_like(out_ref)

    cast_ref[...] = test_ref[...].astype(jnp.float32).astype(jnp.bfloat16)

    def block(index, carry):
        first = pl.multiple_of(index * tile, tile)
        for k in range(step // chunk):
            cols = pl.ds(k * chunk, chunk)
            turns_ref[k] = jnp.dot(
                points_ref[pl.ds(first, tile), :], waves_ref[:, cols], preferred_element_type=jnp.float32
            )
            for j in range(tile // STRIP):
                re, im = phases(turns_ref[k, pl.ds(j * STRIP, STRIP), :])
                lhs_ref[pl.ds(j * STRIP, STRIP), cols] = re.astype(jnp.bfloat16)
                lhs_ref[pl.ds(tile + j * STRIP, STRIP), cols] = im.astype(jnp.bfloat16)
        total = jnp.dot(lhs_ref[...], cast_ref[...], preferred_element_type=jnp.float32)
        out_ref[pl.ds(first, tile), pl.ds(0, width)] += total[:tile]
        out_ref[pl.ds(first, tile), pl.ds(width, width)] += total[tile:]
        return carry

    lax.fori_loop(0, (count_ref[0] + tile - 1) // tile, block, 0)

    @pl.when(pl.program_id(0) == pl.num_programs(0) - 1)
    def _():
        slot = lax.broadcasted_iota(jnp.int32, out_ref.shape, 0)
        result_ref[...] = jnp.where(slot < count_ref[0], out_ref[...], 0.0).astype(dtype)


def adjoint_kernel(scale, counts_ref, waves_ref, points_ref, sketch_ref, out_ref, turns_ref, lhs_ref, rhs_ref):
    modes, width = out_ref.shape[0], sketch_ref.shape[1] // 2
    slab = pl.program_id(0)

    @pl.when(slab == 0)
    def _():
        out_ref[...] = jnp.zeros_like(out_ref)

    def block(index, carry):
        first = pl.multiple_of(index * TILE, TILE)
        rhs_ref[pl.ds(0, TILE), :] = sketch_ref[pl.ds(first, TILE), :]
        rhs_ref[pl.ds(TILE, TILE), pl.ds(0, width)] = sketch_ref[pl.ds(first, TILE), pl.ds(width, width)]
        rhs_ref[pl.ds(TILE, TILE), pl.ds(width, width)] = -sketch_ref[pl.ds(first, TILE), pl.ds(0, width)]
        for k in range(modes // TILE):
            rows = pl.ds(k * TILE, TILE)
            turns_ref[k] = jnp.dot(
                waves_ref[rows, :], points_ref[:, pl.ds(first, TILE)], preferred_element_type=jnp.float32
            )
            for j in range(TILE // STRIP):
                re, im = phases(turns_ref[k, pl.ds(j * STRIP, STRIP), :])
                lhs_ref[k, pl.ds(j * STRIP, STRIP), pl.ds(0, TILE)] = re.astype(jnp.bfloat16)
                lhs_ref[k, pl.ds(j * STRIP, STRIP), pl.ds(TILE, TILE)] = im.astype(jnp.bfloat16)
            out_ref[rows, :] += jnp.dot(lhs_ref[k], rhs_ref[...], preferred_element_type=jnp.float32)
        return carry

    lax.fori_loop(0, (counts_ref[slab] + TILE - 1) // TILE, block, 0)

    @pl.when(slab == pl.num_programs(0) - 1)
    def _():
        out_ref[...] = out_ref[...] * scale


def product_kernel(scale, live_ref, first_ref, second_ref, upper_ref, lower_ref, out_ref, rhs_ref):
    width = upper_ref.shape[1] // 2
    step = pl.program_id(0)

    @pl.when(step == 0)
    def _():
        out_ref[...] = jnp.zeros_like(out_ref)

    @pl.when(2 * step < live_ref[0])
    def _():
        upper, lower = upper_ref[...], lower_ref[...]
        lower = jnp.where(2 * step + 1 < live_ref[0], lower, jnp.zeros_like(lower))
        for g, rows in enumerate((upper, lower)):
            rhs_ref[pl.ds(2 * g * TILE, TILE), :] = rows
            rhs_ref[pl.ds((2 * g + 1) * TILE, TILE), pl.ds(0, width)] = rows[:, width:]
            rhs_ref[pl.ds((2 * g + 1) * TILE, TILE), pl.ds(width, width)] = -rows[:, :width]
        lhs = jnp.concatenate([first_ref[0], second_ref[0]], axis=1)
        out_ref[...] += jnp.dot(lhs, rhs_ref[...], preferred_element_type=jnp.float32)

    @pl.when(step == pl.num_programs(0) - 1)
    def _():
        out_ref[...] = out_ref[...] * scale


def product(scale, live, order, phase, sketch):
    blocks, modes, _ = phase.shape
    width = sketch.shape[1]
    return pl.pallas_call(
        lambda live_ref, order_ref, *refs: product_kernel(scale, live_ref, *refs),
        out_shape=jax.ShapeDtypeStruct((modes, width), jnp.float32),
        grid_spec=pltpu.PrefetchScalarGridSpec(
            num_scalar_prefetch=2,
            grid=(blocks // 2,),
            in_specs=[
                pl.BlockSpec((1, modes, 2 * TILE), lambda b, live, order: (order[2 * b], 0, 0)),
                pl.BlockSpec((1, modes, 2 * TILE), lambda b, live, order: (order[2 * b + 1], 0, 0)),
                pl.BlockSpec((TILE, width), lambda b, live, order: (order[2 * b], 0)),
                pl.BlockSpec((TILE, width), lambda b, live, order: (order[2 * b + 1], 0)),
            ],
            out_specs=pl.BlockSpec((modes, width), lambda b, live, order: (0, 0)),
            scratch_shapes=[pltpu.VMEM((4 * TILE, width), jnp.bfloat16)],
        ),
        compiler_params=pltpu.CompilerParams(vmem_limit_bytes=30 * 2**20),
    )(live, order, phase, phase, sketch, sketch)


def gather_kernel(count_ref, grid_ref, all_ref, counts_ref, info_ref, info_out, info_in):
    pt, md = lax.axis_index("pt"), lax.axis_index("md")
    info_ref[...] = jnp.full(info_ref.shape, count_ref[0], jnp.int32)
    info_ref[pl.ds(0, 3), :] = grid_ref[...]
    barrier = pltpu.get_barrier_semaphore()
    for d in range(1, 8):
        pl.semaphore_signal(
            barrier, inc=1, device_id=((pt + d) % 8, md), device_id_type=pl.DeviceIdType.MESH
        )
    pl.semaphore_wait(barrier, 7)
    copies = []
    for d in range(1, 8):
        copy = pltpu.make_async_remote_copy(
            src_ref=info_ref, dst_ref=all_ref.at[pt], send_sem=info_out.at[d - 1], recv_sem=info_in.at[d - 1],
            device_id=((pt + d) % 8, md), device_id_type=pl.DeviceIdType.MESH,
        )
        copy.start()
        copies.append(copy)
    all_ref[pt] = info_ref[...]
    for copy in copies:
        copy.wait()
    total = jnp.int32(0)
    for slab in range(8):
        counts_ref[slab] = jnp.max(all_ref[slab, 7:8, :])
        total = total + counts_ref[slab]
    counts_ref[8] = total


def gather(count, grid_index):
    shape = (8, grid_index.shape[1])
    return pl.pallas_call(
        gather_kernel,
        out_shape=(jax.ShapeDtypeStruct((8,) + shape, jnp.int32), jax.ShapeDtypeStruct((9,), jnp.int32)),
        in_specs=[pl.BlockSpec(memory_space=pltpu.SMEM), pl.BlockSpec(memory_space=pltpu.VMEM)],
        out_specs=(pl.BlockSpec(memory_space=pltpu.VMEM), pl.BlockSpec(memory_space=pltpu.SMEM)),
        scratch_shapes=[
            pltpu.VMEM(shape, jnp.int32), pltpu.SemaphoreType.DMA((7,)), pltpu.SemaphoreType.DMA((7,))
        ],
        compiler_params=pltpu.CompilerParams(collective_id=1, has_side_effects=True),
    )(count, grid_index)


def compact_kernel(scale, counts_ref, all_ref, packed_ref, own_ref, mask_ref, wide_ref):
    slots = all_ref.shape[2]
    rows, quarter = own_ref.shape[0], mask_ref.shape[0]
    pt, md = lax.axis_index("pt"), lax.axis_index("md")
    wide_ref[...] = jnp.zeros_like(wide_ref)
    lane = lax.broadcasted_iota(jnp.int32, (8, slots + 128), 1)
    start = jnp.int32(0)
    for slab in range(all_ref.shape[0]):
        base = pl.multiple_of((start // 128) * 128, 128)
        shift = start - base
        here = pl.ds(base, slots + 128)
        wider = jnp.concatenate([all_ref[slab].astype(jnp.float32), jnp.zeros((8, 128), jnp.float32)], axis=1)
        wide_ref[:, here] = jnp.where(lane < shift, wide_ref[:, here], pltpu.roll(wider, shift, 1))
        start = start + counts_ref[slab]
    packed_ref[...] = wide_ref[:, : packed_ref.shape[1]]
    share = wide_ref[:, pl.ds(pl.multiple_of(pt * rows, 128), rows)]
    tall = jnp.concatenate([share, jnp.zeros((DEPTH - 8, rows), jnp.float32)], axis=0)
    own_ref[...] = tall.T.astype(jnp.bfloat16)
    slot = lax.broadcasted_iota(jnp.int32, mask_ref.shape, 0) + (pt * rows + md * quarter)
    mask_ref[...] = jnp.where(slot < start, scale, 0.0)


def compact(scale, counts, everyone, rows):
    slots = everyone.shape[2]
    total = 8 * rows
    return pl.pallas_call(
        functools.partial(compact_kernel, scale),
        out_shape=(
            jax.ShapeDtypeStruct((8, total), jnp.float32),
            jax.ShapeDtypeStruct((rows, DEPTH), jnp.bfloat16),
            jax.ShapeDtypeStruct((rows // 4, 128), jnp.float32),
        ),
        in_specs=[pl.BlockSpec(memory_space=pltpu.SMEM), pl.BlockSpec(memory_space=pltpu.VMEM)],
        out_specs=(pl.BlockSpec(memory_space=pltpu.VMEM),) * 3,
        scratch_shapes=[pltpu.VMEM((8, total + slots + 128), jnp.float32)],
    )(counts, everyone)


def fused_kernel(
    scale, own_ref, packed_ref, mask_ref, waves_ref, test_ref, out_ref,
    tall_ref, mine_ref, stage_ref, cast_ref, wide_waves_ref, points_ref, lhs_ref, sum_ref, part_ref, landed_ref, y_ref, phase_ref, rhs_ref,
    test_sem, sum_out, sum_in, z_out, z_in, x_out, x_in, y_out, y_in, core_out, core_in,
):
    pt, md = lax.axis_index("pt"), lax.axis_index("md")
    rows, quarter = own_ref.shape[0], mask_ref.shape[0]
    step, width = cast_ref.shape[1], cast_ref.shape[2]
    modes = mine_ref.shape[0]
    core, x, y = pt % 2, (pt // 2) % 2, pt // 4
    core_pt, x_pt, y_pt = pt + 1 - 2 * core, pt + 2 - 4 * x, pt + 4 - 8 * y
    xy_pt = x_pt + 4 - 8 * y
    inner = (md + 1) // 2 % 2
    upper = md // 2
    partner, cross = md + 1 - 2 * (md % 2), 3 - md

    def send(source, target, out_sem, in_sem, to_pt, to_md):
        copy = pltpu.make_async_remote_copy(
            src_ref=source, dst_ref=target, send_sem=out_sem, recv_sem=in_sem,
            device_id=(to_pt, to_md), device_id_type=pl.DeviceIdType.MESH,
        )
        copy.start()
        return copy

    def place(slab, part):
        return y_ref.at[pl.ds(pl.multiple_of(slab * rows + part * quarter, 32), quarter), :]

    def fetch(index):
        return pltpu.make_async_copy(
            test_ref.at[pl.ds(pl.multiple_of(index * step, step), step), :], stage_ref.at[index], test_sem.at[index]
        )

    for index in range(cast_ref.shape[0]):
        fetch(index).start()
    barrier = pltpu.get_barrier_semaphore()
    for d in range(1, 4):
        pl.semaphore_signal(
            barrier, inc=1, device_id=(pt, (md + d) % 4), device_id_type=pl.DeviceIdType.MESH
        )
    for other in (core_pt, x_pt, y_pt):
        pl.semaphore_signal(barrier, inc=1, device_id=(other, md), device_id_type=pl.DeviceIdType.MESH)

    wide_waves_ref[...] = jnp.zeros_like(wide_waves_ref)
    tall_ref[...] = jnp.zeros_like(tall_ref)
    tall_ref[pl.ds(0, 3), :] = waves_ref[...].astype(jnp.float32) * (1.0 / PERIOD)
    wide_waves_ref[pl.ds(0, 16), :] = tall_ref[...].astype(jnp.bfloat16)
    mine = tall_ref[:, pl.ds(pl.multiple_of(pt * modes, modes), modes)]
    mine = jnp.concatenate([mine, jnp.zeros((DEPTH - 16, modes), jnp.float32)], axis=0)
    mine_ref[...] = mine.T.astype(jnp.bfloat16)
    points_ref[...] = jnp.zeros_like(points_ref)
    points_ref[pl.ds(0, 16), :] = jnp.concatenate(
        [packed_ref[...], jnp.zeros_like(packed_ref)], axis=0
    ).astype(jnp.bfloat16)

    def sketch(block):
        parts = [(md + 3 - 2 * block) % 4, (md + 2 - 2 * block) % 4]
        sum_ref[...] = jnp.zeros_like(sum_ref)

        def body(index, carry):
            if block == 0:
                fetch(index).wait()
                cast_ref[index] = stage_ref[index].astype(jnp.float32).astype(jnp.bfloat16)
            for k in range(step // CHUNK):
                cols = pl.ds(pl.multiple_of(index * step + k * CHUNK, CHUNK), CHUNK)
                for g in range(2):
                    points = own_ref[pl.ds(pl.multiple_of(parts[g] * quarter, 32), quarter), :]
                    turns = jnp.dot(points, wide_waves_ref[:, cols], preferred_element_type=jnp.float32)
                    for j in range(quarter // STRIP):
                        re, im = phases(turns[j * STRIP : (j + 1) * STRIP])
                        at = g * quarter + j * STRIP
                        lhs_ref[pl.ds(at, STRIP), pl.ds(k * CHUNK, CHUNK)] = re.astype(jnp.bfloat16)
                        lhs_ref[pl.ds(2 * quarter + at, STRIP), pl.ds(k * CHUNK, CHUNK)] = im.astype(jnp.bfloat16)
            total = jnp.dot(lhs_ref[...], cast_ref[index], preferred_element_type=jnp.float32)
            sum_ref[:, pl.ds(0, width)] += total[: 2 * quarter]
            sum_ref[:, pl.ds(width, width)] += total[2 * quarter :]
            return carry

        lax.fori_loop(0, cast_ref.shape[0], body, 0)

    def reduce(slot, half):
        part_ref[slot] = sum_ref[pl.ds(half * quarter, quarter), :].astype(jnp.bfloat16)
        return send(part_ref.at[slot], landed_ref.at[slot], sum_out.at[slot], sum_in.at[slot], pt, (md + 3 - slot) % 4)

    sketch(0)
    pl.semaphore_wait(barrier, 6)
    sums = [reduce(0, 0), reduce(1, 1)]
    sketch(1)
    sums.append(reduce(2, 0))

    def make(first, last):
        def body(nth, carry):
            index = nth // 5
            index = ((x + index) % 2 + 2 * ((y + index // 2) % 2)) * 5 + nth % 5
            start = pl.multiple_of(index * 2 * BLOCK, 2 * BLOCK)
            coords = points_ref[:, pl.ds(start, 2 * BLOCK)]
            for k in range(modes // TILE):
                turns = jnp.dot(
                    mine_ref[pl.ds(k * TILE, TILE), :], coords, preferred_element_type=jnp.float32
                )
                for j in range(TILE // STRIP):
                    re, im = phases(turns[j * STRIP : (j + 1) * STRIP])
                    re, im = re.astype(jnp.bfloat16), im.astype(jnp.bfloat16)
                    at = pl.ds(k * TILE + j * STRIP, STRIP)
                    for h in range(2):
                        cols = slice(h * BLOCK, (h + 1) * BLOCK)
                        phase_ref[2 * index + h, at, pl.ds(0, BLOCK)] = re[:, cols]
                        phase_ref[2 * index + h, at, pl.ds(BLOCK, BLOCK)] = im[:, cols]
            return carry

        lax.fori_loop(first, last, body, 0)

    def multiply(first, last):
        def body(index, carry):
            slab = (core + index) % 2 + 2 * ((x + index // 2) % 2) + 4 * ((y + index // 4) % 2)
            per = rows // BLOCK
            for b in range(per):
                block = y_ref[pl.ds(pl.multiple_of(slab * rows + b * BLOCK, BLOCK), BLOCK), :]
                rhs_ref[pl.ds(2 * b * BLOCK, BLOCK), :] = block
                rhs_ref[pl.ds((2 * b + 1) * BLOCK, BLOCK), pl.ds(0, width)] = block[:, width:]
                rhs_ref[pl.ds((2 * b + 1) * BLOCK, BLOCK), pl.ds(width, width)] = -block[:, :width]
            lhs = jnp.concatenate([phase_ref[slab * per + b] for b in range(per)], axis=1)
            total = jnp.dot(lhs, rhs_ref[...], preferred_element_type=jnp.float32)
            out_ref[...] = (out_ref[...] + total) * jnp.where(index == 7, scale, 1.0)
            return carry

        lax.fori_loop(first, last, body, 0)

    out_ref[...] = jnp.zeros_like(out_ref)
    for copy in sums:
        copy.wait_recv()
    total = sum_ref[pl.ds(quarter, quarter), :]
    for d in range(3):
        total = total + landed_ref[d].astype(jnp.float32)
    own = place(pt, md)
    own[...] = (total * mask_ref[:, :1]).astype(jnp.bfloat16)

    pieces = [md, partner, upper * 3 + (1 - 2 * upper) * 2, upper * 3 + (1 - 2 * upper) * 3]
    ups = [send(own, own, z_out.at[0], z_in.at[0], pt, partner)]

    def onward(piece, slot, landing, target):
        here = place(pt, piece)
        return pltpu.make_async_remote_copy(
            src_ref=here, dst_ref=here, send_sem=z_out.at[slot], recv_sem=z_in.at[landing],
            device_id=(pt, target), device_id_type=pl.DeviceIdType.MESH,
        )

    relays = [
        onward(md, 1, 1, cross), onward(pieces[1], 2, 2, cross),
        onward(pieces[2], 3, 1, partner), onward(pieces[3], 4, 2, partner),
    ]

    def relay(index):
        @pl.when(inner == 1)
        def _():
            relays[index].start()

    def arrived(d):
        here = place(pt, pieces[d])
        pltpu.make_async_remote_copy(
            src_ref=here, dst_ref=here, send_sem=z_out.at[0], recv_sem=z_in.at[d - 1],
            device_id=(pt, partner), device_id_type=pl.DeviceIdType.MESH,
        ).wait_recv()

    marks = iter(MAKES)
    state = [0]

    def work():
        first = state[0]
        state[0] = first + next(marks)
        make(first, state[0])

    over_x, over_y, over_core = [], [], []
    for d in range(4):
        if d:
            arrived(d)
        relay(d)
        here = place(pt, pieces[d])
        over_x.append(send(here, here, x_out.at[d], x_in.at[d], x_pt, md))
        over_y.append(send(here, here, y_out.at[d], y_in.at[d], y_pt, md))
        over_core.append(send(here, here, core_out.at[d], core_in.at[d], core_pt, md))
        work()
    forward_x, forward_y = [], []
    for d in range(4):
        over_x[d].wait_recv()
        here = place(x_pt, pieces[d])
        if d < 2:
            forward_y.append(send(here, here, y_out.at[4 + d], y_in.at[4 + d], y_pt, md))
        over_core.append(send(here, here, core_out.at[4 + d], core_in.at[4 + d], core_pt, md))
        over_y[d].wait_recv()
        here = place(y_pt, pieces[d])
        if d >= 2:
            forward_x.append(send(here, here, x_out.at[2 + d], x_in.at[2 + d], x_pt, md))
        over_core.append(send(here, here, core_out.at[8 + d], core_in.at[8 + d], core_pt, md))
        work()
        if d == 2:
            for copy in over_core[:4]:
                copy.wait_recv()
            multiply(0, 2)
    for copy in over_core[4:12]:
        copy.wait_recv()
    multiply(2, 6)
    for d in range(4):
        (forward_y[d] if d < 2 else forward_x[d - 2]).wait_recv()
        here = place(xy_pt, pieces[d])
        over_core.append(send(here, here, core_out.at[12 + d], core_in.at[12 + d], core_pt, md))
    multiply(6, 7)
    for copy in over_core[12:]:
        copy.wait_recv()
    multiply(7, 8)
    for copy in sums + ups + over_x + over_y + over_core + forward_x + forward_y:
        copy.wait_send()

    @pl.when(inner == 1)
    def _():
        for copy in relays:
            copy.wait_send()


def fused(scale, own, packed, mask, waves, test_block):
    rows, modes, width = own.shape[0], waves.shape[1] // 8, test_block.shape[1]
    quarter, total, step = rows // 4, packed.shape[1], SKETCH[0]
    steps = test_block.shape[0] // step
    sems = [n for n in (3, 3, 5, 3, 6, 6, 6, 6, 16, 16)]
    return pl.pallas_call(
        functools.partial(fused_kernel, scale),
        out_shape=jax.ShapeDtypeStruct((modes, 2 * width), jnp.float32),
        in_specs=[pl.BlockSpec(memory_space=pltpu.VMEM)] * 4 + [pl.BlockSpec(memory_space=pl.ANY)],
        out_specs=pl.BlockSpec(memory_space=pltpu.VMEM),
        scratch_shapes=[
            pltpu.VMEM((16, waves.shape[1]), jnp.float32),
            pltpu.VMEM((modes, DEPTH), jnp.bfloat16),
            pltpu.VMEM((steps, step, width), jnp.int32),
            pltpu.VMEM((steps, step, width), jnp.bfloat16),
            pltpu.VMEM((DEPTH, waves.shape[1]), jnp.bfloat16),
            pltpu.VMEM((DEPTH, total), jnp.bfloat16),
            pltpu.VMEM((rows, step), jnp.bfloat16),
            pltpu.VMEM((rows // 2, 2 * width), jnp.float32),
            pltpu.VMEM((3, quarter, 2 * width), jnp.bfloat16),
            pltpu.VMEM((3, quarter, 2 * width), jnp.bfloat16),
            pltpu.VMEM((total, 2 * width), jnp.bfloat16),
            pltpu.VMEM((total // BLOCK, modes, 2 * BLOCK), jnp.bfloat16),
            pltpu.VMEM((2 * rows, 2 * width), jnp.bfloat16),
            pltpu.SemaphoreType.DMA((steps,)),
        ]
        + [pltpu.SemaphoreType.DMA((n,)) for n in sems],
        compiler_params=pltpu.CompilerParams(
            collective_id=2, has_side_effects=True, vmem_limit_bytes=58 * 2**20
        ),
    )(own, packed, mask, waves, test_block)


def padded(rows, factor):
    rows = rows.astype(jnp.float32) * factor
    return jnp.pad(rows, ((0, DEPTH - rows.shape[0]), (0, 0))).astype(jnp.bfloat16)


def sketch_part(count, points, waves, test_block, dtype):
    rows, modes, width = points.shape[0], waves.shape[1], test_block.shape[1]
    step, tile, chunk = SKETCH
    return pl.pallas_call(
        functools.partial(sketch_kernel, dtype),
        out_shape=jax.ShapeDtypeStruct((rows, 2 * width), dtype),
        grid=(modes // step,),
        in_specs=[
            pl.BlockSpec(memory_space=pltpu.SMEM),
            pl.BlockSpec((rows, DEPTH), lambda m: (0, 0)),
            pl.BlockSpec((DEPTH, step), lambda m: (0, m)),
            pl.BlockSpec((step, width), lambda m: (m, 0)),
        ],
        out_specs=pl.BlockSpec((rows, 2 * width), lambda m: (0, 0)),
        scratch_shapes=[
            pltpu.VMEM((step // chunk, tile, chunk), jnp.float32),
            pltpu.VMEM((2 * tile, step), jnp.bfloat16),
            pltpu.VMEM((rows, 2 * width), jnp.float32),
            pltpu.VMEM((step, width), jnp.bfloat16),
        ],
        compiler_params=pltpu.CompilerParams(vmem_limit_bytes=40 * 2**20),
        cost_estimate=pl.CostEstimate(
            flops=4 * rows * modes * width, bytes_accessed=4 * modes * width, transcendentals=0
        ),
    )(count, points, waves, test_block)


def adjoint_part(scale, counts, waves, points, sketch, capacity):
    modes, slots, width = waves.shape[0], points.shape[1], sketch.shape[1]
    return pl.pallas_call(
        functools.partial(adjoint_kernel, scale),
        out_shape=jax.ShapeDtypeStruct((modes, width), jnp.float32),
        grid=(slots // capacity,),
        in_specs=[
            pl.BlockSpec(memory_space=pltpu.SMEM),
            pl.BlockSpec((modes, DEPTH), lambda p: (0, 0)),
            pl.BlockSpec((DEPTH, capacity), lambda p: (0, p)),
            pl.BlockSpec((capacity, width), lambda p: (p, 0)),
        ],
        out_specs=pl.BlockSpec((modes, width), lambda p: (0, 0)),
        scratch_shapes=[
            pltpu.VMEM((modes // TILE, TILE, TILE), jnp.float32),
            pltpu.VMEM((modes // TILE, TILE, 2 * TILE), jnp.bfloat16),
            pltpu.VMEM((2 * TILE, width), jnp.bfloat16),
        ],
        compiler_params=pltpu.CompilerParams(vmem_limit_bytes=40 * 2**20),
        cost_estimate=pl.CostEstimate(
            flops=4 * modes * slots * width, bytes_accessed=2 * slots * width, transcendentals=0
        ),
    )(counts, waves, points, sketch)


def exchange_kernel(
    scale, part_ref, info_ref, waves_ref, out_ref, all_ref, phase_ref, landed_ref, points_ref, turns_ref, made_ref, made_sem,
    sum_out, sum_in, z_out, z_in, x_out, x_in, y_out, y_in, core_out, core_in, info_out, info_in,
):
    pt, md = lax.axis_index("pt"), lax.axis_index("md")
    rows = part_ref.shape[0]
    quarter = rows // 4
    core, x, y = pt % 2, (pt // 2) % 2, pt // 4
    core_pt, x_pt, y_pt = pt + 1 - 2 * core, pt + 2 - 4 * x, pt + 4 - 8 * y
    xy_pt = x_pt + 4 - 8 * y

    def send(source, target, out_sem, in_sem, to_pt, to_md):
        copy = pltpu.make_async_remote_copy(
            src_ref=source, dst_ref=target, send_sem=out_sem, recv_sem=in_sem,
            device_id=(to_pt, to_md), device_id_type=pl.DeviceIdType.MESH,
        )
        copy.start()
        return copy

    def place(slab, part):
        return out_ref.at[pl.ds(pl.multiple_of(slab * rows + part * quarter, quarter), quarter), :]

    barrier = pltpu.get_barrier_semaphore()
    for d in range(1, 4):
        pl.semaphore_signal(
            barrier, inc=1, device_id=(pt, (md + d) % 4), device_id_type=pl.DeviceIdType.MESH
        )
    for d in range(1, 8):
        pl.semaphore_signal(
            barrier, inc=1, device_id=((pt + d) % 8, md), device_id_type=pl.DeviceIdType.MESH
        )
    pl.semaphore_wait(barrier, 10)

    sums = []
    for d in (2, 1, 3):
        to = (md + d) % 4
        source = part_ref.at[pl.ds(pl.multiple_of(to * quarter, quarter), quarter), :]
        sums.append(send(source, landed_ref.at[d - 1], sum_out.at[d - 1], sum_in.at[d - 1], pt, to))
    others = [
        send(info_ref, all_ref.at[pt], info_out.at[d - 1], info_in.at[d - 1], (pt + d) % 8, md)
        for d in range(1, 8)
    ]
    all_ref[pt] = info_ref[...]
    for copy in others:
        copy.wait_recv()
    points_ref[...] = jnp.zeros_like(points_ref)
    for slab in range(8):
        points_ref[pl.ds(0, 8), pl.ds(slab * rows, rows)] = all_ref[slab].astype(jnp.float32)

    def keep(index):
        slot = index % 2
        return pltpu.make_async_copy(made_ref.at[slot], phase_ref.at[index], made_sem.at[slot])

    def make(first, last):
        def body(index, carry):
            slot = index % 2
            start = pl.multiple_of(index * TILE, TILE)
            coords = points_ref[:, pl.ds(start, TILE)].astype(jnp.bfloat16)

            if first >= 2:
                keep(index - 2).wait()
            for k in range(waves_ref.shape[0] // TILE):
                turns_ref[k] = jnp.dot(
                    waves_ref[pl.ds(k * TILE, TILE), :], coords, preferred_element_type=jnp.float32
                )
                for j in range(TILE // STRIP):
                    re, im = phases(turns_ref[k, pl.ds(j * STRIP, STRIP), :])
                    at = pl.ds(k * TILE + j * STRIP, STRIP)
                    made_ref[slot, at, pl.ds(0, TILE)] = re.astype(jnp.bfloat16)
                    made_ref[slot, at, pl.ds(TILE, TILE)] = im.astype(jnp.bfloat16)
            keep(index).start()
            return carry

        lax.fori_loop(first, last, body, 0)

    make(0, 2)
    make(2, MARKS[0])
    for copy in sums:
        copy.wait_recv()
    total = part_ref[pl.ds(pl.multiple_of(md * quarter, quarter), quarter), :].astype(jnp.float32)
    for d in range(3):
        total = total + landed_ref[d].astype(jnp.float32)
    place(pt, md)[...] = (total * scale).astype(jnp.bfloat16)

    own = place(pt, md)
    ups = [send(own, own, z_out.at[d - 1], z_in.at[d - 1], pt, (md + d) % 4) for d in (1, 2, 3)]
    pieces = [md, (md + 3) % 4, (md + 2) % 4, (md + 1) % 4]
    over_x, over_y, over_core = [], [], []
    for d in range(4):
        if d:
            ups[d - 1].wait_recv()
        here = place(pt, pieces[d])
        over_x.append(send(here, here, x_out.at[d], x_in.at[d], x_pt, md))
        over_y.append(send(here, here, y_out.at[d], y_in.at[d], y_pt, md))
        over_core.append(send(here, here, core_out.at[d], core_in.at[d], core_pt, md))
        make(MARKS[d], MARKS[d + 1])
    forward_x, forward_y = [], []
    for d in range(4):
        over_x[d].wait_recv()
        here = place(x_pt, pieces[d])
        if d < 2:
            forward_y.append(send(here, here, y_out.at[4 + d], y_in.at[4 + d], y_pt, md))
        over_core.append(send(here, here, core_out.at[4 + d], core_in.at[4 + d], core_pt, md))
        over_y[d].wait_recv()
        here = place(y_pt, pieces[d])
        if d >= 2:
            forward_x.append(send(here, here, x_out.at[2 + d], x_in.at[2 + d], x_pt, md))
        over_core.append(send(here, here, core_out.at[8 + d], core_in.at[8 + d], core_pt, md))
        make(MARKS[4 + d], MARKS[5 + d])
    for d in range(4):
        (forward_y[d] if d < 2 else forward_x[d - 2]).wait_recv()
        here = place(xy_pt, pieces[d])
        over_core.append(send(here, here, core_out.at[12 + d], core_in.at[12 + d], core_pt, md))
    make(MARKS[8], phase_ref.shape[0])
    keep(phase_ref.shape[0] - 2).wait()
    keep(phase_ref.shape[0] - 1).wait()
    for copy in over_core:
        copy.wait_recv()
    for copy in sums + others + ups + over_x + over_y + over_core + forward_x + forward_y:
        copy.wait_send()


def exchange(scale, part, info, waves):
    rows, width = part.shape
    modes = waves.shape[0]
    sems = [n for n in (3, 3, 6, 6, 16, 7) for _ in range(2)]
    return pl.pallas_call(
        functools.partial(exchange_kernel, scale),
        out_shape=(
            jax.ShapeDtypeStruct((8 * rows, width), jnp.bfloat16),
            jax.ShapeDtypeStruct((8,) + info.shape, info.dtype),
            jax.ShapeDtypeStruct((8 * rows // TILE, modes, 2 * TILE), jnp.bfloat16),
        ),
        in_specs=[pl.BlockSpec(memory_space=pltpu.VMEM)] * 3,
        out_specs=(pl.BlockSpec(memory_space=pltpu.VMEM),) * 2 + (pl.BlockSpec(memory_space=pl.ANY),),
        scratch_shapes=[
            pltpu.VMEM((3, rows // 4, width), jnp.bfloat16),
            pltpu.VMEM((DEPTH, 8 * rows), jnp.float32),
            pltpu.VMEM((modes // TILE, TILE, TILE), jnp.float32),
            pltpu.VMEM((2, modes, 2 * TILE), jnp.bfloat16),
            pltpu.SemaphoreType.DMA((2,)),
        ]
        + [pltpu.SemaphoreType.DMA((n,)) for n in sems],
        compiler_params=pltpu.CompilerParams(
            collective_id=0, has_side_effects=True, vmem_limit_bytes=32 * 2**20
        ),
    )(part, info, waves)


def per_device(grid_index, wavenumbers, test_block, slab_counts):
    capacity = grid_index.shape[1]
    n_pt, n_md = lax.axis_size("pt"), lax.axis_size("md")
    y_scale = 1.0 / (32.0 * math.sqrt(M))
    w_scale = 1.0 / math.sqrt(capacity * n_pt)
    own = wavenumbers.shape[1] // n_pt
    first = lax.axis_index("pt") * own

    def as_given():
        points = padded(grid_index, 1.0)
        waves = padded(wavenumbers, 1.0 / PERIOD)
        mine = lax.dynamic_slice_in_dim(waves, first, own, 1)
        part = sketch_part(slab_counts, points.T, waves, test_block, jnp.bfloat16)
        info = jnp.concatenate(
            [grid_index, jnp.broadcast_to(slab_counts[:, None], (5, capacity))], axis=0
        )
        sketch, gathered, phase = exchange(y_scale, part, info, mine.T)
        per_slab = (gathered[:, 3, 0] + TILE - 1) // TILE
        ends = jnp.sum(jnp.where(jnp.arange(8)[:, None] <= jnp.arange(8)[None, :], per_slab[:, None], 0), axis=0)
        nth = jnp.minimum(jnp.arange(phase.shape[0], dtype=jnp.int32), ends[7] - 1)
        past = (ends[None, :] <= nth[:, None]).astype(jnp.int32)
        slab = jnp.sum(past, axis=1)
        order = slab * (capacity // TILE) + nth - jnp.sum(past * per_slab[None, :], axis=1)
        return product(w_scale, ends[7:], order.astype(jnp.int32), phase, sketch)

    if (n_pt, n_md) == (8, 4):
        everyone, counts = gather(slab_counts, grid_index)

        def packed_rows():
            packed, share, mask = compact(y_scale, counts, everyone, ROWS)
            return fused(w_scale, share, packed, mask, wavenumbers, test_block)

        return lax.cond(counts[8] <= 8 * ROWS, packed_rows, as_given)
    points = padded(grid_index, 1.0)
    waves = padded(wavenumbers, 1.0 / PERIOD)
    mine = lax.dynamic_slice_in_dim(waves, first, own, 1)
    counts = lax.all_gather(slab_counts, "pt", tiled=True)
    all_points = lax.all_gather(grid_index, "pt", axis=1, tiled=True)
    part = sketch_part(slab_counts, points.T, waves, test_block, jnp.float32)
    share = lax.psum_scatter(part, "md", scatter_dimension=0, tiled=True)
    share = (share * y_scale).astype(jnp.bfloat16)
    sketch = lax.all_gather(share, ("pt", "md"), tiled=True)
    return adjoint_part(w_scale, counts, mine.T, padded(all_points, 1.0), sketch, capacity)


def solution(mesh):
    placed = (P(None, "pt"), P(None, "md"), P("md", None), P("pt"))
    return jax.shard_map(
        per_device, mesh=mesh, in_specs=placed, out_specs=P(("md", "pt"), None), check_vma=False
    )
```

```python
import functools
import math

import jax
import jax.numpy as jnp
from jax import lax
from jax.experimental import pallas as pl
from jax.experimental.pallas import tpu as pltpu
from jax.sharding import PartitionSpec as P

M = 32768
PERIOD = 512
DEPTH = 128
TILE = 256
STRIP = 32
SKETCH = (2048, 512, 512)
MARKS = (10, 11, 13, 15, 17, 20, 23, 26, 29)
BLOCK = 128
CHUNK = 512
CHUNKS = ((0, 256), (256, 256), (512, 128))
LARGEST = 256

S = (7.3193808, -3.6889591, 22.557636)
C = (4.03692, -3.305112, 12.524202, 1.7281804)


def phases(whole_turns):
    r = whole_turns - jnp.round(whole_turns)
    z = r * r
    y = z * z
    s = ((y + S[0]) * (z + S[1]) + S[2]) * r
    c = ((y + C[0]) * (z + C[1]) + C[2]) * C[3]
    return 1.0 - s * s, s * c


def sketch_kernel(
    dtype, count_ref, points_ref, waves_ref, test_ref, result_ref, turns_ref, lhs_ref, out_ref, cast_ref
):
    width, tile, step = test_ref.shape[1], turns_ref.shape[1], test_ref.shape[0]
    chunk = turns_ref.shape[2]

    @pl.when(pl.program_id(0) == 0)
    def _():
        out_ref[...] = jnp.zeros_like(out_ref)

    cast_ref[...] = test_ref[...].astype(jnp.float32).astype(jnp.bfloat16)

    def block(index, carry):
        first = pl.multiple_of(index * tile, tile)
        for k in range(step // chunk):
            cols = pl.ds(k * chunk, chunk)
            turns_ref[k] = jnp.dot(
                points_ref[pl.ds(first, tile), :], waves_ref[:, cols], preferred_element_type=jnp.float32
            )
            for j in range(tile // STRIP):
                re, im = phases(turns_ref[k, pl.ds(j * STRIP, STRIP), :])
                lhs_ref[pl.ds(j * STRIP, STRIP), cols] = re.astype(jnp.bfloat16)
                lhs_ref[pl.ds(tile + j * STRIP, STRIP), cols] = im.astype(jnp.bfloat16)
        total = jnp.dot(lhs_ref[...], cast_ref[...], preferred_element_type=jnp.float32)
        out_ref[pl.ds(first, tile), pl.ds(0, width)] += total[:tile]
        out_ref[pl.ds(first, tile), pl.ds(width, width)] += total[tile:]
        return carry

    lax.fori_loop(0, (count_ref[0] + tile - 1) // tile, block, 0)

    @pl.when(pl.program_id(0) == pl.num_programs(0) - 1)
    def _():
        slot = lax.broadcasted_iota(jnp.int32, out_ref.shape, 0)
        result_ref[...] = jnp.where(slot < count_ref[0], out_ref[...], 0.0).astype(dtype)


def adjoint_kernel(scale, counts_ref, waves_ref, points_ref, sketch_ref, out_ref, turns_ref, lhs_ref, rhs_ref):
    modes, width = out_ref.shape[0], sketch_ref.shape[1] // 2
    slab = pl.program_id(0)

    @pl.when(slab == 0)
    def _():
        out_ref[...] = jnp.zeros_like(out_ref)

    def block(index, carry):
        first = pl.multiple_of(index * TILE, TILE)
        rhs_ref[pl.ds(0, TILE), :] = sketch_ref[pl.ds(first, TILE), :]
        rhs_ref[pl.ds(TILE, TILE), pl.ds(0, width)] = sketch_ref[pl.ds(first, TILE), pl.ds(width, width)]
        rhs_ref[pl.ds(TILE, TILE), pl.ds(width, width)] = -sketch_ref[pl.ds(first, TILE), pl.ds(0, width)]
        for k in range(modes // TILE):
            rows = pl.ds(k * TILE, TILE)
            turns_ref[k] = jnp.dot(
                waves_ref[rows, :], points_ref[:, pl.ds(first, TILE)], preferred_element_type=jnp.float32
            )
            for j in range(TILE // STRIP):
                re, im = phases(turns_ref[k, pl.ds(j * STRIP, STRIP), :])
                lhs_ref[k, pl.ds(j * STRIP, STRIP), pl.ds(0, TILE)] = re.astype(jnp.bfloat16)
                lhs_ref[k, pl.ds(j * STRIP, STRIP), pl.ds(TILE, TILE)] = im.astype(jnp.bfloat16)
            out_ref[rows, :] += jnp.dot(lhs_ref[k], rhs_ref[...], preferred_element_type=jnp.float32)
        return carry

    lax.fori_loop(0, (counts_ref[slab] + TILE - 1) // TILE, block, 0)

    @pl.when(slab == pl.num_programs(0) - 1)
    def _():
        out_ref[...] = out_ref[...] * scale


def product_kernel(scale, live_ref, first_ref, second_ref, upper_ref, lower_ref, out_ref, rhs_ref):
    width = upper_ref.shape[1] // 2
    step = pl.program_id(0)

    @pl.when(step == 0)
    def _():
        out_ref[...] = jnp.zeros_like(out_ref)

    @pl.when(2 * step < live_ref[0])
    def _():
        upper, lower = upper_ref[...], lower_ref[...]
        lower = jnp.where(2 * step + 1 < live_ref[0], lower, jnp.zeros_like(lower))
        for g, rows in enumerate((upper, lower)):
            rhs_ref[pl.ds(2 * g * TILE, TILE), :] = rows
            rhs_ref[pl.ds((2 * g + 1) * TILE, TILE), pl.ds(0, width)] = rows[:, width:]
            rhs_ref[pl.ds((2 * g + 1) * TILE, TILE), pl.ds(width, width)] = -rows[:, :width]
        lhs = jnp.concatenate([first_ref[0], second_ref[0]], axis=1)
        out_ref[...] += jnp.dot(lhs, rhs_ref[...], preferred_element_type=jnp.float32)

    @pl.when(step == pl.num_programs(0) - 1)
    def _():
        out_ref[...] = out_ref[...] * scale


def product(scale, live, order, phase, sketch):
    blocks, modes, _ = phase.shape
    width = sketch.shape[1]
    return pl.pallas_call(
        lambda live_ref, order_ref, *refs: product_kernel(scale, live_ref, *refs),
        out_shape=jax.ShapeDtypeStruct((modes, width), jnp.float32),
        grid_spec=pltpu.PrefetchScalarGridSpec(
            num_scalar_prefetch=2,
            grid=(blocks // 2,),
            in_specs=[
                pl.BlockSpec((1, modes, 2 * TILE), lambda b, live, order: (order[2 * b], 0, 0)),
                pl.BlockSpec((1, modes, 2 * TILE), lambda b, live, order: (order[2 * b + 1], 0, 0)),
                pl.BlockSpec((TILE, width), lambda b, live, order: (order[2 * b], 0)),
                pl.BlockSpec((TILE, width), lambda b, live, order: (order[2 * b + 1], 0)),
            ],
            out_specs=pl.BlockSpec((modes, width), lambda b, live, order: (0, 0)),
            scratch_shapes=[pltpu.VMEM((4 * TILE, width), jnp.bfloat16)],
        ),
        compiler_params=pltpu.CompilerParams(vmem_limit_bytes=30 * 2**20),
    )(live, order, phase, phase, sketch, sketch)


def gather_kernel(limit, count_ref, grid_ref, all_ref, counts_ref, fits_ref, info_ref, info_out, info_in):
    pt, md = lax.axis_index("pt"), lax.axis_index("md")
    barrier = pltpu.get_barrier_semaphore()
    for d in range(1, 8):
        pl.semaphore_signal(
            barrier, inc=1, device_id=((pt + d) % 8, md), device_id_type=pl.DeviceIdType.MESH
        )
    blocks = grid_ref.shape[1] // 128
    lines = [grid_ref[d : d + 1, j * 128 : (j + 1) * 128] for d in range(3) for j in range(blocks)]
    lines += [jnp.full((1, 128), count_ref[0] // 32, jnp.int32), jnp.full((1, 128), count_ref[0] % 32, jnp.int32)]
    lines += [jnp.zeros((info_ref.shape[0] - len(lines), 128), jnp.int32)]
    info_ref[...] = jnp.concatenate(lines, axis=0).astype(jnp.float32).astype(jnp.bfloat16)
    pl.semaphore_wait(barrier, 7)
    copies = []
    for d in range(1, 8):
        copy = pltpu.make_async_remote_copy(
            src_ref=info_ref, dst_ref=all_ref.at[pt], send_sem=info_out.at[d - 1], recv_sem=info_in.at[d - 1],
            device_id=((pt + d) % 8, md), device_id_type=pl.DeviceIdType.MESH,
        )
        copy.start()
        copies.append(copy)
    all_ref[pt] = info_ref[...]
    for copy in copies:
        copy.wait()
    digits = [all_ref[slab, 16:32, :].astype(jnp.float32) for slab in range(8)]
    counts = [jnp.max(digit[8:9] * 32.0 + digit[9:10]).astype(jnp.int32) for digit in digits]
    for slab in range(8):
        counts_ref[slab] = counts[slab]
    fits_ref[0] = jnp.where(sum(counts) <= limit, 1, 0)


def gather(count, grid_index, limit):
    shape = (32, 128)
    return pl.pallas_call(
        functools.partial(gather_kernel, limit),
        out_shape=(
            jax.ShapeDtypeStruct((8,) + shape, jnp.bfloat16),
            jax.ShapeDtypeStruct((8,), jnp.int32),
            jax.ShapeDtypeStruct((1,), jnp.int32),
        ),
        in_specs=[pl.BlockSpec(memory_space=pltpu.SMEM), pl.BlockSpec(memory_space=pltpu.VMEM)],
        out_specs=(pl.BlockSpec(memory_space=pltpu.VMEM),) + (pl.BlockSpec(memory_space=pltpu.SMEM),) * 2,
        scratch_shapes=[
            pltpu.VMEM(shape, jnp.bfloat16), pltpu.SemaphoreType.DMA((7,)), pltpu.SemaphoreType.DMA((7,))
        ],
        compiler_params=pltpu.CompilerParams(collective_id=1, has_side_effects=True),
    )(count, grid_index)


def compact_kernel(scale, counts_ref, all_ref, packed_ref, own_ref, mask_ref, wide_ref, line_ref):
    slots = line_ref.shape[1] - 128
    rows = own_ref.shape[0]
    pt, md = lax.axis_index("pt"), lax.axis_index("md")
    wide_ref[...] = jnp.zeros_like(wide_ref)
    line_ref[...] = jnp.zeros_like(line_ref)
    lane = lax.broadcasted_iota(jnp.int32, line_ref.shape, 1)
    start = jnp.int32(0)
    for slab in range(all_ref.shape[0]):
        base = pl.multiple_of((start // 128) * 128, 128)
        shift = start - base
        here = pl.ds(base, slots + 128)
        lines = all_ref[slab].astype(jnp.float32)
        for j in range(slots // 128):
            for d in range(3):
                at = d * (slots // 128) + j
                line_ref[d : d + 1, j * 128 : (j + 1) * 128] = lines[at : at + 1]
        wide_ref[:, here] = jnp.where(lane < shift, wide_ref[:, here], pltpu.roll(line_ref[...], shift, 1))
        start = start + counts_ref[slab]
    packed_ref[...] = wide_ref[:, : packed_ref.shape[1]]
    share = wide_ref[:, pl.ds(pl.multiple_of(pt * rows, 128), rows)]
    tall = jnp.concatenate([share, jnp.zeros((DEPTH - 8, rows), jnp.float32)], axis=0)
    own_ref[...] = tall.T.astype(jnp.bfloat16)
    slot = lax.broadcasted_iota(jnp.int32, mask_ref.shape[1:], 0) + pt * rows
    for c, (base, size) in enumerate(CHUNKS):
        mask_ref[c] = jnp.where(slot + base + md * (size // 4) < start, scale, 0.0)


def compact(scale, counts, everyone, slots):
    rows = sum(size for _, size in CHUNKS)
    total = 8 * rows
    return pl.pallas_call(
        functools.partial(compact_kernel, scale),
        out_shape=(
            jax.ShapeDtypeStruct((8, total), jnp.float32),
            jax.ShapeDtypeStruct((rows, DEPTH), jnp.bfloat16),
            jax.ShapeDtypeStruct((len(CHUNKS), LARGEST // 4, 128), jnp.float32),
        ),
        in_specs=[pl.BlockSpec(memory_space=pltpu.SMEM), pl.BlockSpec(memory_space=pltpu.VMEM)],
        out_specs=(pl.BlockSpec(memory_space=pltpu.VMEM),) * 3,
        scratch_shapes=[
            pltpu.VMEM((8, total + slots + 128), jnp.float32), pltpu.VMEM((8, slots + 128), jnp.float32)
        ],
    )(counts, everyone)


def fused_kernel(
    scale, own_ref, packed_ref, mask_ref, waves_ref, test_ref, out_ref,
    tall_ref, mine_ref, stage_ref, cast_ref, wide_waves_ref, points_ref, lhs_ref, sum_ref, keep_ref, part_ref, landed_ref,
    y_ref, phase_ref, rhs_ref,
    test_sem, sum_out, sum_in, z_out, z_in, x_out, x_in, y_out, y_in, core_out, core_in,
):
    pt, md = lax.axis_index("pt"), lax.axis_index("md")
    rows = own_ref.shape[0]
    step, width = cast_ref.shape[1], cast_ref.shape[2]
    modes = mine_ref.shape[0]
    core, x, y = pt % 2, (pt // 2) % 2, pt // 4
    core_pt, x_pt, y_pt = pt + 1 - 2 * core, pt + 2 - 4 * x, pt + 4 - 8 * y
    xy_pt = x_pt + 4 - 8 * y
    inner, upper = (md + 1) // 2 % 2, md // 2
    partner, cross = md + 1 - 2 * (md % 2), 3 - md
    pieces = [md, partner, upper * 3 + (1 - 2 * upper) * 2, upper * 3 + (1 - 2 * upper) * 3]

    def remote(source, target, out_sem, in_sem, to_pt, to_md):
        return pltpu.make_async_remote_copy(
            src_ref=source, dst_ref=target, send_sem=out_sem, recv_sem=in_sem,
            device_id=(to_pt, to_md), device_id_type=pl.DeviceIdType.MESH,
        )

    def place(slab, c, part):
        base, size = CHUNKS[c]
        first = pl.multiple_of(slab * rows + base + part * (size // 4), 32)
        return y_ref.at[pl.ds(first, size // 4), :]

    def fetch(index):
        return pltpu.make_async_copy(
            test_ref.at[pl.ds(pl.multiple_of(index * step, step), step), :], stage_ref.at[index], test_sem.at[index]
        )

    for index in range(cast_ref.shape[0]):
        fetch(index).start()
    barrier = pltpu.get_barrier_semaphore()
    for d in range(1, 4):
        pl.semaphore_signal(
            barrier, inc=1, device_id=(pt, (md + d) % 4), device_id_type=pl.DeviceIdType.MESH
        )
    for other in (core_pt, x_pt, y_pt):
        pl.semaphore_signal(barrier, inc=1, device_id=(other, md), device_id_type=pl.DeviceIdType.MESH)

    tall_ref[...] = jnp.zeros_like(tall_ref)
    tall_ref[pl.ds(0, 3), :] = waves_ref[...].astype(jnp.float32) * (1.0 / PERIOD)
    wide_waves_ref[...] = jnp.zeros_like(wide_waves_ref)
    wide_waves_ref[pl.ds(0, 16), :] = tall_ref[...].astype(jnp.bfloat16)
    mine = tall_ref[:, pl.ds(pl.multiple_of(pt * modes, modes), modes)]
    mine = jnp.concatenate([mine, jnp.zeros((DEPTH - 16, modes), jnp.float32)], axis=0)
    mine_ref[...] = mine.T.astype(jnp.bfloat16)
    points_ref[...] = jnp.zeros_like(points_ref)
    points_ref[pl.ds(0, 16), :] = jnp.concatenate(
        [packed_ref[...], jnp.zeros_like(packed_ref)], axis=0
    ).astype(jnp.bfloat16)
    out_ref[...] = jnp.zeros_like(out_ref)

    def at_step(index, events):
        for when, event in events:
            pl.when(index == when)(event)

    def sketch(c, events):
        base, size = CHUNKS[c]
        here = pl.ds(0, size)
        sum_ref[here, :] = jnp.zeros((size, 2 * width), jnp.float32)

        def body(index, carry):
            if c == 0:
                fetch(index).wait()
                cast_ref[index] = stage_ref[index].astype(jnp.float32).astype(jnp.bfloat16)
            for k in range(step // CHUNK):
                cols = pl.ds(pl.multiple_of(index * step + k * CHUNK, CHUNK), CHUNK)
                points = own_ref[pl.ds(base, size), :]
                turns = jnp.dot(points, wide_waves_ref[:, cols], preferred_element_type=jnp.float32)
                for at in range(0, size, STRIP):
                    re, im = phases(turns[at : at + STRIP])
                    lhs_ref[pl.ds(at, STRIP), pl.ds(k * CHUNK, CHUNK)] = re.astype(jnp.bfloat16)
                    lhs_ref[pl.ds(size + at, STRIP), pl.ds(k * CHUNK, CHUNK)] = im.astype(jnp.bfloat16)
            total = jnp.dot(lhs_ref[pl.ds(0, 2 * size), :], cast_ref[index], preferred_element_type=jnp.float32)
            sum_ref[here, pl.ds(0, width)] += total[:size]
            sum_ref[here, pl.ds(width, width)] += total[size:]
            at_step(index, events)
            return carry

        lax.fori_loop(0, cast_ref.shape[0], body, 0)

    def sums(c, d):
        here = pl.ds(0, CHUNKS[c][1] // 4)
        return remote(
            part_ref.at[c, d - 1, here], landed_ref.at[c, d - 1, here], sum_out.at[c, d - 1], sum_in.at[c, d - 1],
            pt, (md + d) % 4,
        )

    def share_out(c):
        quarter = CHUNKS[c][1] // 4
        here = pl.ds(0, quarter)
        for d in (2, 1, 3):
            rows_of = pl.ds(pl.multiple_of((md + d) % 4 * quarter, 16), quarter)
            part_ref[c, d - 1, here, :] = sum_ref[rows_of, :].astype(jnp.bfloat16)
            sums(c, d).start()
        keep_ref[c, here, :] = sum_ref[pl.ds(pl.multiple_of(md * quarter, 16), quarter), :]

    def up(c):
        here = place(pt, c, md)
        return remote(here, here, z_out.at[c, 0], z_in.at[c, 0], pt, partner)

    def relay(c, d):
        here = place(pt, c, pieces[d])
        landing = (1, 2, 1, 2)[d]
        return remote(here, here, z_out.at[c, 1 + d], z_in.at[c, landing], pt, cross if d < 2 else partner)

    def over(c, d, axis):
        here = place(pt, c, pieces[d])
        out_sem, in_sem, to = ((x_out, x_in, x_pt), (y_out, y_in, y_pt), (core_out, core_in, core_pt))[axis]
        return remote(here, here, out_sem.at[c, d], in_sem.at[c, d], to, md)

    def forward(c, d):
        if d < 2:
            here = place(x_pt, c, pieces[d])
            return remote(here, here, y_out.at[c, 4 + d], y_in.at[c, 4 + d], y_pt, md)
        here = place(y_pt, c, pieces[d])
        return remote(here, here, x_out.at[c, 2 + d], x_in.at[c, 2 + d], x_pt, md)

    def across(c, d, n):
        here = place((pt, x_pt, y_pt, xy_pt)[n], c, pieces[d])
        return remote(here, here, core_out.at[c, 4 * n + d], core_in.at[c, 4 * n + d], core_pt, md)

    def begin(c):
        def event():
            here = pl.ds(0, CHUNKS[c][1] // 4)
            for n in (1, 2, 3):
                sums(c, n).wait_recv()
            total = keep_ref[c, here, :]
            for n in range(3):
                total = total + landed_ref[c, n, here, :].astype(jnp.float32)
            place(pt, c, md)[...] = (total * mask_ref[c, here, :1]).astype(jnp.bfloat16)
            up(c).start()

            @pl.when(inner == 1)
            def _():
                relay(c, 0).start()

            for axis in range(3):
                over(c, 0, axis).start()

        return event

    def landed(c, d):
        piece = place(pt, c, pieces[d])
        return remote(piece, piece, z_out.at[c, 0], z_in.at[c, d - 1], pt, partner)

    def hop(c, d):
        def event():
            @pl.when(inner == 1)
            def _():
                landed(c, d).wait_recv()
                relay(c, d).start()

        return event

    def spread(c, d):
        def event():
            @pl.when(inner == 0)
            def _():
                landed(c, d).wait_recv()

            for axis in range(3):
                over(c, d, axis).start()

        return event

    def pass_on(c, d):
        def event():
            over(c, d, 0).wait_recv()
            if d < 2:
                forward(c, d).start()
            across(c, d, 1).start()
            over(c, d, 1).wait_recv()
            if d >= 2:
                forward(c, d).start()
            across(c, d, 2).start()

        return event

    def corner(c, d):
        def event():
            forward(c, d).wait_recv()
            across(c, d, 3).start()

        return event

    def gathered(c, n):
        def event():
            for d in range(4):
                across(c, d, n).wait_recv()

        return event

    def pair_of(nth):
        return (x + nth) % 2 + 2 * ((y + nth // 2) % 2)

    def make(events):
        per = 2 * rows // (2 * BLOCK)

        def body(nth, carry):
            index = pair_of(nth // per) * per + nth % per
            start = pl.multiple_of(index * 2 * BLOCK, 2 * BLOCK)
            coords = points_ref[:, pl.ds(start, 2 * BLOCK)]
            for k in range(modes // TILE):
                turns = jnp.dot(
                    mine_ref[pl.ds(k * TILE, TILE), :], coords, preferred_element_type=jnp.float32
                )
                for j in range(TILE // STRIP):
                    re, im = phases(turns[j * STRIP : (j + 1) * STRIP])
                    re, im = re.astype(jnp.bfloat16), im.astype(jnp.bfloat16)
                    at = pl.ds(k * TILE + j * STRIP, STRIP)
                    for h in range(2):
                        cols = slice(h * BLOCK, (h + 1) * BLOCK)
                        phase_ref[2 * index + h, at, pl.ds(0, BLOCK)] = re[:, cols]
                        phase_ref[2 * index + h, at, pl.ds(BLOCK, BLOCK)] = im[:, cols]
            at_step(nth, events)
            return carry

        lax.fori_loop(0, 4 * per, body, 0)

    def multiply(c, last, events):
        base, size = CHUNKS[c]

        def body(nth, carry):
            at_step(nth, events)
            terms = []
            for h in range(2):
                slab = 2 * pair_of(nth) + h
                for b in range(size // BLOCK):
                    block = y_ref[pl.ds(pl.multiple_of(slab * rows + base + b * BLOCK, BLOCK), BLOCK), :]
                    at = 2 * BLOCK * len(terms)
                    rhs_ref[pl.ds(at, BLOCK), :] = block
                    rhs_ref[pl.ds(at + BLOCK, BLOCK), pl.ds(0, width)] = block[:, width:]
                    rhs_ref[pl.ds(at + BLOCK, BLOCK), pl.ds(width, width)] = -block[:, :width]
                    terms.append(phase_ref[slab * (rows // BLOCK) + base // BLOCK + b])
            total = jnp.dot(
                jnp.concatenate(terms, axis=1), rhs_ref[pl.ds(0, 4 * size), :], preferred_element_type=jnp.float32
            )
            if last:
                out_ref[...] = (out_ref[...] + total) * jnp.where(nth == 3, scale, 1.0)
            else:
                out_ref[...] += total
            return carry

        lax.fori_loop(0, 4, body, 0)

    sketch(0, [])
    pl.semaphore_wait(barrier, 6)
    share_out(0)
    sketch(1, [(3, begin(0))])
    share_out(1)
    sketch(2, [(3, hop(0, 1)), (3, hop(0, 2)), (3, spread(0, 1)), (3, pass_on(0, 0))])
    share_out(2)
    make([
        (3, hop(0, 3)), (3, spread(0, 2)), (3, corner(0, 0)), (4, pass_on(0, 1)), (6, begin(1)), (7, spread(0, 3)),
        (7, pass_on(0, 2)), (8, corner(0, 1)), (9, begin(2)), (10, hop(1, 1)), (10, hop(1, 2)), (10, spread(1, 1)),
        (10, pass_on(1, 0)), (11, pass_on(0, 3)), (11, corner(0, 2)), (13, hop(2, 1)), (13, hop(2, 2)), (13, spread(2, 1)),
        (13, pass_on(2, 0)), (14, hop(1, 3)), (14, spread(1, 2)), (14, corner(1, 0)), (14, pass_on(1, 1)), (15, corner(0, 3)),
        (16, hop(2, 3)), (16, spread(2, 2)), (16, corner(2, 0)), (17, pass_on(2, 1)), (18, spread(1, 3)), (18, pass_on(1, 2)),
        (18, corner(1, 1)), (19, spread(2, 3)), (19, pass_on(2, 2)), (19, corner(2, 1)),
    ])
    multiply(0, False, [
        (0, pass_on(1, 3)), (0, corner(1, 2)), (0, gathered(0, 0)), (1, pass_on(2, 3)), (1, corner(2, 2)),
        (1, gathered(0, 1)), (2, corner(1, 3)), (2, gathered(0, 2)), (3, corner(2, 3)), (3, gathered(0, 3)),
    ])
    multiply(1, False, [(n, gathered(1, n)) for n in range(4)])
    multiply(2, True, [(n, gathered(2, n)) for n in range(4)])
    for c in range(len(CHUNKS)):
        for d in (1, 2, 3):
            sums(c, d).wait_send()
        up(c).wait_send()
        for d in range(4):
            for axis in range(3):
                over(c, d, axis).wait_send()
            forward(c, d).wait_send()
            for n in (1, 2, 3):
                across(c, d, n).wait_send()

        @pl.when(inner == 1)
        def _(c=c):
            for d in range(4):
                relay(c, d).wait_send()


def fused(scale, own, packed, mask, waves, test_block):
    rows, modes, width = own.shape[0], waves.shape[1] // 8, test_block.shape[1]
    chunks, share, _ = mask.shape
    total, step = packed.shape[1], SKETCH[0]
    steps = test_block.shape[0] // step
    return pl.pallas_call(
        functools.partial(fused_kernel, scale),
        out_shape=jax.ShapeDtypeStruct((modes, 2 * width), jnp.float32),
        in_specs=[pl.BlockSpec(memory_space=pltpu.VMEM)] * 4 + [pl.BlockSpec(memory_space=pl.ANY)],
        out_specs=pl.BlockSpec(memory_space=pltpu.VMEM),
        scratch_shapes=[
            pltpu.VMEM((16, waves.shape[1]), jnp.float32),
            pltpu.VMEM((modes, DEPTH), jnp.bfloat16),
            pltpu.VMEM((steps, step, width), jnp.int32),
            pltpu.VMEM((steps, step, width), jnp.bfloat16),
            pltpu.VMEM((DEPTH, waves.shape[1]), jnp.bfloat16),
            pltpu.VMEM((DEPTH, total), jnp.bfloat16),
            pltpu.VMEM((2 * LARGEST, step), jnp.bfloat16),
            pltpu.VMEM((LARGEST, 2 * width), jnp.float32),
            pltpu.VMEM((chunks, share, 2 * width), jnp.float32),
            pltpu.VMEM((chunks, 3, share, 2 * width), jnp.bfloat16),
            pltpu.VMEM((chunks, 3, share, 2 * width), jnp.bfloat16),
            pltpu.VMEM((total, 2 * width), jnp.bfloat16),
            pltpu.VMEM((total // BLOCK, modes, 2 * BLOCK), jnp.bfloat16),
            pltpu.VMEM((4 * LARGEST, 2 * width), jnp.bfloat16),
            pltpu.SemaphoreType.DMA((steps,)),
        ]
        + [pltpu.SemaphoreType.DMA((chunks, n)) for n in (3, 3, 5, 3, 6, 6, 6, 6, 16, 16)],
        compiler_params=pltpu.CompilerParams(
            collective_id=2, has_side_effects=True, vmem_limit_bytes=60 * 2**20
        ),
    )(own, packed, mask, waves, test_block)


def padded(rows, factor):
    rows = rows.astype(jnp.float32) * factor
    return jnp.pad(rows, ((0, DEPTH - rows.shape[0]), (0, 0))).astype(jnp.bfloat16)


def sketch_part(count, points, waves, test_block, dtype):
    rows, modes, width = points.shape[0], waves.shape[1], test_block.shape[1]
    step, tile, chunk = SKETCH
    return pl.pallas_call(
        functools.partial(sketch_kernel, dtype),
        out_shape=jax.ShapeDtypeStruct((rows, 2 * width), dtype),
        grid=(modes // step,),
        in_specs=[
            pl.BlockSpec(memory_space=pltpu.SMEM),
            pl.BlockSpec((rows, DEPTH), lambda m: (0, 0)),
            pl.BlockSpec((DEPTH, step), lambda m: (0, m)),
            pl.BlockSpec((step, width), lambda m: (m, 0)),
        ],
        out_specs=pl.BlockSpec((rows, 2 * width), lambda m: (0, 0)),
        scratch_shapes=[
            pltpu.VMEM((step // chunk, tile, chunk), jnp.float32),
            pltpu.VMEM((2 * tile, step), jnp.bfloat16),
            pltpu.VMEM((rows, 2 * width), jnp.float32),
            pltpu.VMEM((step, width), jnp.bfloat16),
        ],
        compiler_params=pltpu.CompilerParams(vmem_limit_bytes=40 * 2**20),
        cost_estimate=pl.CostEstimate(
            flops=4 * rows * modes * width, bytes_accessed=4 * modes * width, transcendentals=0
        ),
    )(count, points, waves, test_block)


def adjoint_part(scale, counts, waves, points, sketch, capacity):
    modes, slots, width = waves.shape[0], points.shape[1], sketch.shape[1]
    return pl.pallas_call(
        functools.partial(adjoint_kernel, scale),
        out_shape=jax.ShapeDtypeStruct((modes, width), jnp.float32),
        grid=(slots // capacity,),
        in_specs=[
            pl.BlockSpec(memory_space=pltpu.SMEM),
            pl.BlockSpec((modes, DEPTH), lambda p: (0, 0)),
            pl.BlockSpec((DEPTH, capacity), lambda p: (0, p)),
            pl.BlockSpec((capacity, width), lambda p: (p, 0)),
        ],
        out_specs=pl.BlockSpec((modes, width), lambda p: (0, 0)),
        scratch_shapes=[
            pltpu.VMEM((modes // TILE, TILE, TILE), jnp.float32),
            pltpu.VMEM((modes // TILE, TILE, 2 * TILE), jnp.bfloat16),
            pltpu.VMEM((2 * TILE, width), jnp.bfloat16),
        ],
        compiler_params=pltpu.CompilerParams(vmem_limit_bytes=40 * 2**20),
        cost_estimate=pl.CostEstimate(
            flops=4 * modes * slots * width, bytes_accessed=2 * slots * width, transcendentals=0
        ),
    )(counts, waves, points, sketch)


def exchange_kernel(
    scale, part_ref, info_ref, waves_ref, out_ref, all_ref, phase_ref, landed_ref, points_ref, turns_ref, made_ref, made_sem,
    sum_out, sum_in, z_out, z_in, x_out, x_in, y_out, y_in, core_out, core_in, info_out, info_in,
):
    pt, md = lax.axis_index("pt"), lax.axis_index("md")
    rows = part_ref.shape[0]
    quarter = rows // 4
    core, x, y = pt % 2, (pt // 2) % 2, pt // 4
    core_pt, x_pt, y_pt = pt + 1 - 2 * core, pt + 2 - 4 * x, pt + 4 - 8 * y
    xy_pt = x_pt + 4 - 8 * y

    def send(source, target, out_sem, in_sem, to_pt, to_md):
        copy = pltpu.make_async_remote_copy(
            src_ref=source, dst_ref=target, send_sem=out_sem, recv_sem=in_sem,
            device_id=(to_pt, to_md), device_id_type=pl.DeviceIdType.MESH,
        )
        copy.start()
        return copy

    def place(slab, part):
        return out_ref.at[pl.ds(pl.multiple_of(slab * rows + part * quarter, quarter), quarter), :]

    barrier = pltpu.get_barrier_semaphore()
    for d in range(1, 4):
        pl.semaphore_signal(
            barrier, inc=1, device_id=(pt, (md + d) % 4), device_id_type=pl.DeviceIdType.MESH
        )
    for d in range(1, 8):
        pl.semaphore_signal(
            barrier, inc=1, device_id=((pt + d) % 8, md), device_id_type=pl.DeviceIdType.MESH
        )
    pl.semaphore_wait(barrier, 10)

    sums = []
    for d in (2, 1, 3):
        to = (md + d) % 4
        source = part_ref.at[pl.ds(pl.multiple_of(to * quarter, quarter), quarter), :]
        sums.append(send(source, landed_ref.at[d - 1], sum_out.at[d - 1], sum_in.at[d - 1], pt, to))
    others = [
        send(info_ref, all_ref.at[pt], info_out.at[d - 1], info_in.at[d - 1], (pt + d) % 8, md)
        for d in range(1, 8)
    ]
    all_ref[pt] = info_ref[...]
    for copy in others:
        copy.wait_recv()
    points_ref[...] = jnp.zeros_like(points_ref)
    for slab in range(8):
        points_ref[pl.ds(0, 8), pl.ds(slab * rows, rows)] = all_ref[slab].astype(jnp.float32)

    def keep(index):
        slot = index % 2
        return pltpu.make_async_copy(made_ref.at[slot], phase_ref.at[index], made_sem.at[slot])

    def make(first, last):
        def body(index, carry):
            slot = index % 2
            start = pl.multiple_of(index * TILE, TILE)
            coords = points_ref[:, pl.ds(start, TILE)].astype(jnp.bfloat16)

            if first >= 2:
                keep(index - 2).wait()
            for k in range(waves_ref.shape[0] // TILE):
                turns_ref[k] = jnp.dot(
                    waves_ref[pl.ds(k * TILE, TILE), :], coords, preferred_element_type=jnp.float32
                )
                for j in range(TILE // STRIP):
                    re, im = phases(turns_ref[k, pl.ds(j * STRIP, STRIP), :])
                    at = pl.ds(k * TILE + j * STRIP, STRIP)
                    made_ref[slot, at, pl.ds(0, TILE)] = re.astype(jnp.bfloat16)
                    made_ref[slot, at, pl.ds(TILE, TILE)] = im.astype(jnp.bfloat16)
            keep(index).start()
            return carry

        lax.fori_loop(first, last, body, 0)

    make(0, 2)
    make(2, MARKS[0])
    for copy in sums:
        copy.wait_recv()
    total = part_ref[pl.ds(pl.multiple_of(md * quarter, quarter), quarter), :].astype(jnp.float32)
    for d in range(3):
        total = total + landed_ref[d].astype(jnp.float32)
    place(pt, md)[...] = (total * scale).astype(jnp.bfloat16)

    own = place(pt, md)
    ups = [send(own, own, z_out.at[d - 1], z_in.at[d - 1], pt, (md + d) % 4) for d in (1, 2, 3)]
    pieces = [md, (md + 3) % 4, (md + 2) % 4, (md + 1) % 4]
    over_x, over_y, over_core = [], [], []
    for d in range(4):
        if d:
            ups[d - 1].wait_recv()
        here = place(pt, pieces[d])
        over_x.append(send(here, here, x_out.at[d], x_in.at[d], x_pt, md))
        over_y.append(send(here, here, y_out.at[d], y_in.at[d], y_pt, md))
        over_core.append(send(here, here, core_out.at[d], core_in.at[d], core_pt, md))
        make(MARKS[d], MARKS[d + 1])
    forward_x, forward_y = [], []
    for d in range(4):
        over_x[d].wait_recv()
        here = place(x_pt, pieces[d])
        if d < 2:
            forward_y.append(send(here, here, y_out.at[4 + d], y_in.at[4 + d], y_pt, md))
        over_core.append(send(here, here, core_out.at[4 + d], core_in.at[4 + d], core_pt, md))
        over_y[d].wait_recv()
        here = place(y_pt, pieces[d])
        if d >= 2:
            forward_x.append(send(here, here, x_out.at[2 + d], x_in.at[2 + d], x_pt, md))
        over_core.append(send(here, here, core_out.at[8 + d], core_in.at[8 + d], core_pt, md))
        make(MARKS[4 + d], MARKS[5 + d])
    for d in range(4):
        (forward_y[d] if d < 2 else forward_x[d - 2]).wait_recv()
        here = place(xy_pt, pieces[d])
        over_core.append(send(here, here, core_out.at[12 + d], core_in.at[12 + d], core_pt, md))
    make(MARKS[8], phase_ref.shape[0])
    keep(phase_ref.shape[0] - 2).wait()
    keep(phase_ref.shape[0] - 1).wait()
    for copy in over_core:
        copy.wait_recv()
    for copy in sums + others + ups + over_x + over_y + over_core + forward_x + forward_y:
        copy.wait_send()


def exchange(scale, part, info, waves):
    rows, width = part.shape
    modes = waves.shape[0]
    sems = [n for n in (3, 3, 6, 6, 16, 7) for _ in range(2)]
    return pl.pallas_call(
        functools.partial(exchange_kernel, scale),
        out_shape=(
            jax.ShapeDtypeStruct((8 * rows, width), jnp.bfloat16),
            jax.ShapeDtypeStruct((8,) + info.shape, info.dtype),
            jax.ShapeDtypeStruct((8 * rows // TILE, modes, 2 * TILE), jnp.bfloat16),
        ),
        in_specs=[pl.BlockSpec(memory_space=pltpu.VMEM)] * 3,
        out_specs=(pl.BlockSpec(memory_space=pltpu.VMEM),) * 2 + (pl.BlockSpec(memory_space=pl.ANY),),
        scratch_shapes=[
            pltpu.VMEM((3, rows // 4, width), jnp.bfloat16),
            pltpu.VMEM((DEPTH, 8 * rows), jnp.float32),
            pltpu.VMEM((modes // TILE, TILE, TILE), jnp.float32),
            pltpu.VMEM((2, modes, 2 * TILE), jnp.bfloat16),
            pltpu.SemaphoreType.DMA((2,)),
        ]
        + [pltpu.SemaphoreType.DMA((n,)) for n in sems],
        compiler_params=pltpu.CompilerParams(
            collective_id=0, has_side_effects=True, vmem_limit_bytes=32 * 2**20
        ),
    )(part, info, waves)


def per_device(grid_index, wavenumbers, test_block, slab_counts):
    capacity = grid_index.shape[1]
    n_pt, n_md = lax.axis_size("pt"), lax.axis_size("md")
    y_scale = 1.0 / (32.0 * math.sqrt(M))
    w_scale = 1.0 / math.sqrt(capacity * n_pt)
    own = wavenumbers.shape[1] // n_pt
    first = lax.axis_index("pt") * own

    def as_given():
        points = padded(grid_index, 1.0)
        waves = padded(wavenumbers, 1.0 / PERIOD)
        mine = lax.dynamic_slice_in_dim(waves, first, own, 1)
        part = sketch_part(slab_counts, points.T, waves, test_block, jnp.bfloat16)
        info = jnp.concatenate(
            [grid_index, jnp.broadcast_to(slab_counts[:, None], (5, capacity))], axis=0
        )
        sketch, gathered, phase = exchange(y_scale, part, info, mine.T)
        per_slab = (gathered[:, 3, 0] + TILE - 1) // TILE
        ends = jnp.sum(jnp.where(jnp.arange(8)[:, None] <= jnp.arange(8)[None, :], per_slab[:, None], 0), axis=0)
        nth = jnp.minimum(jnp.arange(phase.shape[0], dtype=jnp.int32), ends[7] - 1)
        past = (ends[None, :] <= nth[:, None]).astype(jnp.int32)
        slab = jnp.sum(past, axis=1)
        order = slab * (capacity // TILE) + nth - jnp.sum(past * per_slab[None, :], axis=1)
        return product(w_scale, ends[7:], order.astype(jnp.int32), phase, sketch)

    if (n_pt, n_md) == (8, 4):
        everyone, counts, fits = gather(slab_counts, grid_index, 8 * sum(size for _, size in CHUNKS))

        def packed_rows():
            packed, share, mask = compact(y_scale, counts, everyone, capacity)
            return fused(w_scale, share, packed, mask, wavenumbers, test_block)

        return lax.switch(fits[0], (as_given, packed_rows))
    points = padded(grid_index, 1.0)
    waves = padded(wavenumbers, 1.0 / PERIOD)
    mine = lax.dynamic_slice_in_dim(waves, first, own, 1)
    counts = lax.all_gather(slab_counts, "pt", tiled=True)
    all_points = lax.all_gather(grid_index, "pt", axis=1, tiled=True)
    part = sketch_part(slab_counts, points.T, waves, test_block, jnp.float32)
    share = lax.psum_scatter(part, "md", scatter_dimension=0, tiled=True)
    share = (share * y_scale).astype(jnp.bfloat16)
    sketch = lax.all_gather(share, ("pt", "md"), tiled=True)
    return adjoint_part(w_scale, counts, mine.T, padded(all_points, 1.0), sketch, capacity)


def solution(mesh):
    placed = (P(None, "pt"), P(None, "md"), P("md", None), P("pt"))
    return jax.shard_map(
        per_device, mesh=mesh, in_specs=placed, out_specs=P(("md", "pt"), None), check_vma=False
    )
```

```python
import functools
import math

import jax
import jax.numpy as jnp
from jax import lax
from jax.experimental import pallas as pl
from jax.experimental.pallas import tpu as pltpu
from jax.sharding import PartitionSpec as P

M = 32768
PERIOD = 512
DEPTH = 128
TILE = 256
STRIP = 32
SKETCH = (2048, 512, 512)
MARKS = (10, 11, 13, 15, 17, 20, 23, 26, 29)
BLOCK = 128
CHUNK = 512
CHUNKS = ((0, 256), (256, 256), (512, 128))
LARGEST = 256

S = (7.3193808, -3.6889591, 22.557636)
C = (4.03692, -3.305112, 12.524202, 1.7281804)


def phases(whole_turns):
    r = whole_turns - jnp.round(whole_turns)
    z = r * r
    y = z * z
    s = ((y + S[0]) * (z + S[1]) + S[2]) * r
    c = ((y + C[0]) * (z + C[1]) + C[2]) * C[3]
    return 1.0 - s * s, s * c


def sketch_kernel(
    dtype, count_ref, points_ref, waves_ref, test_ref, result_ref, turns_ref, lhs_ref, out_ref, cast_ref
):
    width, tile, step = test_ref.shape[1], turns_ref.shape[1], test_ref.shape[0]
    chunk = turns_ref.shape[2]

    @pl.when(pl.program_id(0) == 0)
    def _():
        out_ref[...] = jnp.zeros_like(out_ref)

    cast_ref[...] = test_ref[...].astype(jnp.float32).astype(jnp.bfloat16)

    def block(index, carry):
        first = pl.multiple_of(index * tile, tile)
        for k in range(step // chunk):
            cols = pl.ds(k * chunk, chunk)
            turns_ref[k] = jnp.dot(
                points_ref[pl.ds(first, tile), :], waves_ref[:, cols], preferred_element_type=jnp.float32
            )
            for j in range(tile // STRIP):
                re, im = phases(turns_ref[k, pl.ds(j * STRIP, STRIP), :])
                lhs_ref[pl.ds(j * STRIP, STRIP), cols] = re.astype(jnp.bfloat16)
                lhs_ref[pl.ds(tile + j * STRIP, STRIP), cols] = im.astype(jnp.bfloat16)
        total = jnp.dot(lhs_ref[...], cast_ref[...], preferred_element_type=jnp.float32)
        out_ref[pl.ds(first, tile), pl.ds(0, width)] += total[:tile]
        out_ref[pl.ds(first, tile), pl.ds(width, width)] += total[tile:]
        return carry

    lax.fori_loop(0, (count_ref[0] + tile - 1) // tile, block, 0)

    @pl.when(pl.program_id(0) == pl.num_programs(0) - 1)
    def _():
        slot = lax.broadcasted_iota(jnp.int32, out_ref.shape, 0)
        result_ref[...] = jnp.where(slot < count_ref[0], out_ref[...], 0.0).astype(dtype)


def adjoint_kernel(scale, counts_ref, waves_ref, points_ref, sketch_ref, out_ref, turns_ref, lhs_ref, rhs_ref):
    modes, width = out_ref.shape[0], sketch_ref.shape[1] // 2
    slab = pl.program_id(0)

    @pl.when(slab == 0)
    def _():
        out_ref[...] = jnp.zeros_like(out_ref)

    def block(index, carry):
        first = pl.multiple_of(index * TILE, TILE)
        rhs_ref[pl.ds(0, TILE), :] = sketch_ref[pl.ds(first, TILE), :]
        rhs_ref[pl.ds(TILE, TILE), pl.ds(0, width)] = sketch_ref[pl.ds(first, TILE), pl.ds(width, width)]
        rhs_ref[pl.ds(TILE, TILE), pl.ds(width, width)] = -sketch_ref[pl.ds(first, TILE), pl.ds(0, width)]
        for k in range(modes // TILE):
            rows = pl.ds(k * TILE, TILE)
            turns_ref[k] = jnp.dot(
                waves_ref[rows, :], points_ref[:, pl.ds(first, TILE)], preferred_element_type=jnp.float32
            )
            for j in range(TILE // STRIP):
                re, im = phases(turns_ref[k, pl.ds(j * STRIP, STRIP), :])
                lhs_ref[k, pl.ds(j * STRIP, STRIP), pl.ds(0, TILE)] = re.astype(jnp.bfloat16)
                lhs_ref[k, pl.ds(j * STRIP, STRIP), pl.ds(TILE, TILE)] = im.astype(jnp.bfloat16)
            out_ref[rows, :] += jnp.dot(lhs_ref[k], rhs_ref[...], preferred_element_type=jnp.float32)
        return carry

    lax.fori_loop(0, (counts_ref[slab] + TILE - 1) // TILE, block, 0)

    @pl.when(slab == pl.num_programs(0) - 1)
    def _():
        out_ref[...] = out_ref[...] * scale


def product_kernel(scale, live_ref, first_ref, second_ref, upper_ref, lower_ref, out_ref, rhs_ref):
    width = upper_ref.shape[1] // 2
    step = pl.program_id(0)

    @pl.when(step == 0)
    def _():
        out_ref[...] = jnp.zeros_like(out_ref)

    @pl.when(2 * step < live_ref[0])
    def _():
        upper, lower = upper_ref[...], lower_ref[...]
        lower = jnp.where(2 * step + 1 < live_ref[0], lower, jnp.zeros_like(lower))
        for g, rows in enumerate((upper, lower)):
            rhs_ref[pl.ds(2 * g * TILE, TILE), :] = rows
            rhs_ref[pl.ds((2 * g + 1) * TILE, TILE), pl.ds(0, width)] = rows[:, width:]
            rhs_ref[pl.ds((2 * g + 1) * TILE, TILE), pl.ds(width, width)] = -rows[:, :width]
        lhs = jnp.concatenate([first_ref[0], second_ref[0]], axis=1)
        out_ref[...] += jnp.dot(lhs, rhs_ref[...], preferred_element_type=jnp.float32)

    @pl.when(step == pl.num_programs(0) - 1)
    def _():
        out_ref[...] = out_ref[...] * scale


def product(scale, live, order, phase, sketch):
    blocks, modes, _ = phase.shape
    width = sketch.shape[1]
    return pl.pallas_call(
        lambda live_ref, order_ref, *refs: product_kernel(scale, live_ref, *refs),
        out_shape=jax.ShapeDtypeStruct((modes, width), jnp.float32),
        grid_spec=pltpu.PrefetchScalarGridSpec(
            num_scalar_prefetch=2,
            grid=(blocks // 2,),
            in_specs=[
                pl.BlockSpec((1, modes, 2 * TILE), lambda b, live, order: (order[2 * b], 0, 0)),
                pl.BlockSpec((1, modes, 2 * TILE), lambda b, live, order: (order[2 * b + 1], 0, 0)),
                pl.BlockSpec((TILE, width), lambda b, live, order: (order[2 * b], 0)),
                pl.BlockSpec((TILE, width), lambda b, live, order: (order[2 * b + 1], 0)),
            ],
            out_specs=pl.BlockSpec((modes, width), lambda b, live, order: (0, 0)),
            scratch_shapes=[pltpu.VMEM((4 * TILE, width), jnp.bfloat16)],
        ),
        compiler_params=pltpu.CompilerParams(vmem_limit_bytes=30 * 2**20),
    )(live, order, phase, phase, sketch, sketch)


def gather_kernel(limit, count_ref, grid_ref, all_ref, counts_ref, fits_ref, info_ref, info_out, info_in):
    pt, md = lax.axis_index("pt"), lax.axis_index("md")
    barrier = pltpu.get_barrier_semaphore()
    for d in range(1, 8):
        pl.semaphore_signal(
            barrier, inc=1, device_id=((pt + d) % 8, md), device_id_type=pl.DeviceIdType.MESH
        )
    blocks = grid_ref.shape[1] // 128
    lines = [grid_ref[d : d + 1, j * 128 : (j + 1) * 128] for d in range(3) for j in range(blocks)]
    lines += [jnp.full((1, 128), count_ref[0] // 32, jnp.int32), jnp.full((1, 128), count_ref[0] % 32, jnp.int32)]
    lines += [jnp.zeros((info_ref.shape[0] - len(lines), 128), jnp.int32)]
    info_ref[...] = jnp.concatenate(lines, axis=0).astype(jnp.float32).astype(jnp.bfloat16)
    pl.semaphore_wait(barrier, 7)
    copies = []
    for d in range(1, 8):
        copy = pltpu.make_async_remote_copy(
            src_ref=info_ref, dst_ref=all_ref.at[pt], send_sem=info_out.at[d - 1], recv_sem=info_in.at[d - 1],
            device_id=((pt + d) % 8, md), device_id_type=pl.DeviceIdType.MESH,
        )
        copy.start()
        copies.append(copy)
    all_ref[pt] = info_ref[...]
    for copy in copies:
        copy.wait()
    digits = [all_ref[slab, 16:32, :].astype(jnp.float32) for slab in range(8)]
    counts = [jnp.max(digit[8:9] * 32.0 + digit[9:10]).astype(jnp.int32) for digit in digits]
    for slab in range(8):
        counts_ref[slab] = counts[slab]
    fits_ref[0] = jnp.where(sum(counts) <= limit, 1, 0)


def gather(count, grid_index, limit):
    shape = (32, 128)
    return pl.pallas_call(
        functools.partial(gather_kernel, limit),
        out_shape=(
            jax.ShapeDtypeStruct((8,) + shape, jnp.bfloat16),
            jax.ShapeDtypeStruct((8,), jnp.int32),
            jax.ShapeDtypeStruct((1,), jnp.int32),
        ),
        in_specs=[pl.BlockSpec(memory_space=pltpu.SMEM), pl.BlockSpec(memory_space=pltpu.VMEM)],
        out_specs=(pl.BlockSpec(memory_space=pltpu.VMEM),) + (pl.BlockSpec(memory_space=pltpu.SMEM),) * 2,
        scratch_shapes=[
            pltpu.VMEM(shape, jnp.bfloat16), pltpu.SemaphoreType.DMA((7,)), pltpu.SemaphoreType.DMA((7,))
        ],
        compiler_params=pltpu.CompilerParams(collective_id=1, has_side_effects=True),
    )(count, grid_index)


def compact_kernel(scale, counts_ref, all_ref, packed_ref, own_ref, mask_ref, wide_ref, line_ref):
    slots = line_ref.shape[1] - 128
    rows = own_ref.shape[0]
    pt, md = lax.axis_index("pt"), lax.axis_index("md")
    wide_ref[...] = jnp.zeros_like(wide_ref)
    line_ref[...] = jnp.zeros_like(line_ref)
    lane = lax.broadcasted_iota(jnp.int32, line_ref.shape, 1)
    start = jnp.int32(0)
    for slab in range(all_ref.shape[0]):
        base = pl.multiple_of((start // 128) * 128, 128)
        shift = start - base
        here = pl.ds(base, slots + 128)
        lines = all_ref[slab].astype(jnp.float32)
        for j in range(slots // 128):
            for d in range(3):
                at = d * (slots // 128) + j
                line_ref[d : d + 1, j * 128 : (j + 1) * 128] = lines[at : at + 1]
        wide_ref[:, here] = jnp.where(lane < shift, wide_ref[:, here], pltpu.roll(line_ref[...], shift, 1))
        start = start + counts_ref[slab]
    packed_ref[...] = wide_ref[:, : packed_ref.shape[1]]
    share = wide_ref[:, pl.ds(pl.multiple_of(pt * rows, 128), rows)]
    tall = jnp.concatenate([share, jnp.zeros((DEPTH - 8, rows), jnp.float32)], axis=0)
    own_ref[...] = tall.T.astype(jnp.bfloat16)
    slot = lax.broadcasted_iota(jnp.int32, mask_ref.shape[1:], 0) + pt * rows
    for c, (base, size) in enumerate(CHUNKS):
        mask_ref[c] = jnp.where(slot + base + md * (size // 4) < start, scale, 0.0)


def compact(scale, counts, everyone, slots):
    rows = sum(size for _, size in CHUNKS)
    total = 8 * rows
    return pl.pallas_call(
        functools.partial(compact_kernel, scale),
        out_shape=(
            jax.ShapeDtypeStruct((8, total), jnp.float32),
            jax.ShapeDtypeStruct((rows, DEPTH), jnp.bfloat16),
            jax.ShapeDtypeStruct((len(CHUNKS), LARGEST // 4, 128), jnp.float32),
        ),
        in_specs=[pl.BlockSpec(memory_space=pltpu.SMEM), pl.BlockSpec(memory_space=pltpu.VMEM)],
        out_specs=(pl.BlockSpec(memory_space=pltpu.VMEM),) * 3,
        scratch_shapes=[
            pltpu.VMEM((8, total + slots + 128), jnp.float32), pltpu.VMEM((8, slots + 128), jnp.float32)
        ],
    )(counts, everyone)


def fused_kernel(
    scale, own_ref, packed_ref, mask_ref, waves_ref, test_ref, out_ref,
    tall_ref, mine_ref, stage_ref, cast_ref, wide_waves_ref, points_ref, lhs_ref, sum_ref, keep_ref, part_ref, landed_ref,
    y_ref, phase_ref, rhs_ref,
    test_sem, sum_out, sum_in, z_out, z_in, x_out, x_in, y_out, y_in, core_out, core_in,
):
    pt, md = lax.axis_index("pt"), lax.axis_index("md")
    rows = own_ref.shape[0]
    step, width = cast_ref.shape[1], cast_ref.shape[2]
    modes = mine_ref.shape[0]
    core, x, y = pt % 2, (pt // 2) % 2, pt // 4
    core_pt, x_pt, y_pt = pt + 1 - 2 * core, pt + 2 - 4 * x, pt + 4 - 8 * y
    xy_pt = x_pt + 4 - 8 * y
    inner, upper = (md + 1) // 2 % 2, md // 2
    partner, cross = md + 1 - 2 * (md % 2), 3 - md
    pieces = [md, partner, upper * 3 + (1 - 2 * upper) * 2, upper * 3 + (1 - 2 * upper) * 3]

    def remote(source, target, out_sem, in_sem, to_pt, to_md):
        return pltpu.make_async_remote_copy(
            src_ref=source, dst_ref=target, send_sem=out_sem, recv_sem=in_sem,
            device_id=(to_pt, to_md), device_id_type=pl.DeviceIdType.MESH,
        )

    def place(slab, c, part):
        base, size = CHUNKS[c]
        first = pl.multiple_of(slab * rows + base + part * (size // 4), 32)
        return y_ref.at[pl.ds(first, size // 4), :]

    def fetch(index):
        return pltpu.make_async_copy(
            test_ref.at[pl.ds(pl.multiple_of(index * step, step), step), :], stage_ref.at[index], test_sem.at[index]
        )

    for index in range(cast_ref.shape[0]):
        fetch(index).start()
    barrier = pltpu.get_barrier_semaphore()
    for d in range(1, 4):
        pl.semaphore_signal(
            barrier, inc=1, device_id=(pt, (md + d) % 4), device_id_type=pl.DeviceIdType.MESH
        )
    for other in (core_pt, x_pt, y_pt):
        pl.semaphore_signal(barrier, inc=1, device_id=(other, md), device_id_type=pl.DeviceIdType.MESH)

    tall_ref[...] = jnp.zeros_like(tall_ref)
    tall_ref[pl.ds(0, 3), :] = waves_ref[...].astype(jnp.float32) * (1.0 / PERIOD)
    wide_waves_ref[...] = jnp.zeros_like(wide_waves_ref)
    wide_waves_ref[pl.ds(0, 16), :] = tall_ref[...].astype(jnp.bfloat16)
    mine = tall_ref[:, pl.ds(pl.multiple_of(pt * modes, modes), modes)]
    mine = jnp.concatenate([mine, jnp.zeros((DEPTH - 16, modes), jnp.float32)], axis=0)
    mine_ref[...] = mine.T.astype(jnp.bfloat16)
    points_ref[...] = jnp.zeros_like(points_ref)
    points_ref[pl.ds(0, 16), :] = jnp.concatenate(
        [packed_ref[...], jnp.zeros_like(packed_ref)], axis=0
    ).astype(jnp.bfloat16)
    out_ref[...] = jnp.zeros_like(out_ref)

    def at_step(index, events):
        for step_of in sorted({when for when, _ in events}):

            @pl.when(index == step_of)
            def _(step_of=step_of):
                for when, event in events:
                    if when == step_of:
                        event()

    def sketch(c):
        base, size = CHUNKS[c]
        here = pl.ds(0, size)
        sum_ref[here, :] = jnp.zeros((size, 2 * width), jnp.float32)

        def body(index, carry):
            if c == 0:
                fetch(index).wait()
                cast_ref[index] = stage_ref[index].astype(jnp.float32).astype(jnp.bfloat16)
            for k in range(step // CHUNK):
                cols = pl.ds(pl.multiple_of(index * step + k * CHUNK, CHUNK), CHUNK)
                points = own_ref[pl.ds(base, size), :]
                turns = jnp.dot(points, wide_waves_ref[:, cols], preferred_element_type=jnp.float32)
                for at in range(0, size, STRIP):
                    re, im = phases(turns[at : at + STRIP])
                    lhs_ref[pl.ds(at, STRIP), pl.ds(k * CHUNK, CHUNK)] = re.astype(jnp.bfloat16)
                    lhs_ref[pl.ds(size + at, STRIP), pl.ds(k * CHUNK, CHUNK)] = im.astype(jnp.bfloat16)
            total = jnp.dot(lhs_ref[pl.ds(0, 2 * size), :], cast_ref[index], preferred_element_type=jnp.float32)
            sum_ref[here, pl.ds(0, width)] += total[:size]
            sum_ref[here, pl.ds(width, width)] += total[size:]
            return carry

        lax.fori_loop(0, cast_ref.shape[0], body, 0)

    def sums(c, d):
        here = pl.ds(0, CHUNKS[c][1] // 4)
        return remote(
            part_ref.at[c, d - 1, here], landed_ref.at[c, d - 1, here], sum_out.at[c, d - 1], sum_in.at[c, d - 1],
            pt, (md + d) % 4,
        )

    def share_out(c):
        quarter = CHUNKS[c][1] // 4
        here = pl.ds(0, quarter)
        for d in (2, 1, 3):
            rows_of = pl.ds(pl.multiple_of((md + d) % 4 * quarter, 16), quarter)
            part_ref[c, d - 1, here, :] = sum_ref[rows_of, :].astype(jnp.bfloat16)
            sums(c, d).start()
        keep_ref[c, here, :] = sum_ref[pl.ds(pl.multiple_of(md * quarter, 16), quarter), :]

    def up(c):
        here = place(pt, c, md)
        return remote(here, here, z_out.at[c, 0], z_in.at[c, 0], pt, partner)

    def relay(c, d):
        here = place(pt, c, pieces[d])
        landing = (1, 2, 1, 2)[d]
        return remote(here, here, z_out.at[c, 1 + d], z_in.at[c, landing], pt, cross if d < 2 else partner)

    def over(c, d, axis):
        here = place(pt, c, pieces[d])
        out_sem, in_sem, to = ((x_out, x_in, x_pt), (y_out, y_in, y_pt))[axis]
        return remote(here, here, out_sem.at[c, d], in_sem.at[c, d], to, md)

    def forward(c, d):
        if d < 2:
            here = place(x_pt, c, pieces[d])
            return remote(here, here, y_out.at[c, 4 + d], y_in.at[c, 4 + d], y_pt, md)
        here = place(y_pt, c, pieces[d])
        return remote(here, here, x_out.at[c, 2 + d], x_in.at[c, 2 + d], x_pt, md)

    def across(c, n):
        base, size = CHUNKS[c]
        here = y_ref.at[pl.ds(pl.multiple_of((pt, x_pt, y_pt, xy_pt)[n] * rows + base, 128), size), :]
        return remote(here, here, core_out.at[c, n], core_in.at[c, n], core_pt, md)

    def begin(c):
        def event():
            here = pl.ds(0, CHUNKS[c][1] // 4)
            for n in (1, 2, 3):
                sums(c, n).wait_recv()
            total = keep_ref[c, here, :]
            for n in range(3):
                total = total + landed_ref[c, n, here, :].astype(jnp.float32)
            place(pt, c, md)[...] = (total * mask_ref[c, here, :1]).astype(jnp.bfloat16)
            up(c).start()

            @pl.when(inner == 1)
            def _():
                relay(c, 0).start()

            for axis in range(2):
                over(c, 0, axis).start()

        return event

    def landed(c, d):
        piece = place(pt, c, pieces[d])
        return remote(piece, piece, z_out.at[c, 0], z_in.at[c, d - 1], pt, partner)

    def hop(c, d):
        def event():
            @pl.when(inner == 1)
            def _():
                landed(c, d).wait_recv()
                relay(c, d).start()

        return event

    def spread(c, d):
        def event():
            @pl.when(inner == 0)
            def _():
                landed(c, d).wait_recv()

            for axis in range(2):
                over(c, d, axis).start()
            if d == 3:
                across(c, 0).start()

        return event

    def pass_on(c, d):
        def event():
            over(c, d, 0).wait_recv()
            if d < 2:
                forward(c, d).start()
            over(c, d, 1).wait_recv()
            if d >= 2:
                forward(c, d).start()
            if d == 3:
                across(c, 1).start()
                across(c, 2).start()

        return event

    def corner(c, d):
        def event():
            forward(c, d).wait_recv()
            if d == 3:
                across(c, 3).start()

        return event

    def gathered(c, n):
        def event():
            across(c, n).wait_recv()

        return event

    def pair_of(nth):
        return (x + nth) % 2 + 2 * ((y + nth // 2) % 2)

    def make(events):
        per = 2 * rows // (2 * BLOCK)

        def body(nth, carry):
            index = pair_of(nth // per) * per + nth % per
            start = pl.multiple_of(index * 2 * BLOCK, 2 * BLOCK)
            coords = points_ref[:, pl.ds(start, 2 * BLOCK)]
            for k in range(modes // TILE):
                turns = jnp.dot(
                    mine_ref[pl.ds(k * TILE, TILE), :], coords, preferred_element_type=jnp.float32
                )
                for j in range(TILE // STRIP):
                    re, im = phases(turns[j * STRIP : (j + 1) * STRIP])
                    re, im = re.astype(jnp.bfloat16), im.astype(jnp.bfloat16)
                    at = pl.ds(k * TILE + j * STRIP, STRIP)
                    for h in range(2):
                        cols = slice(h * BLOCK, (h + 1) * BLOCK)
                        phase_ref[2 * index + h, at, pl.ds(0, BLOCK)] = re[:, cols]
                        phase_ref[2 * index + h, at, pl.ds(BLOCK, BLOCK)] = im[:, cols]
            at_step(nth, events)
            return carry

        lax.fori_loop(0, 4 * per, body, 0)

    def multiply(c, last, events):
        base, size = CHUNKS[c]

        def body(nth, carry):
            at_step(nth, events)
            terms = []
            for h in range(2):
                slab = 2 * pair_of(nth) + h
                for b in range(size // BLOCK):
                    block = y_ref[pl.ds(pl.multiple_of(slab * rows + base + b * BLOCK, BLOCK), BLOCK), :]
                    at = 2 * BLOCK * len(terms)
                    rhs_ref[pl.ds(at, BLOCK), :] = block
                    rhs_ref[pl.ds(at + BLOCK, BLOCK), pl.ds(0, width)] = block[:, width:]
                    rhs_ref[pl.ds(at + BLOCK, BLOCK), pl.ds(width, width)] = -block[:, :width]
                    terms.append(phase_ref[slab * (rows // BLOCK) + base // BLOCK + b])
            total = jnp.dot(
                jnp.concatenate(terms, axis=1), rhs_ref[pl.ds(0, 4 * size), :], preferred_element_type=jnp.float32
            )
            if last:
                out_ref[...] = (out_ref[...] + total) * jnp.where(nth == 3, scale, 1.0)
            else:
                out_ref[...] += total
            return carry

        lax.fori_loop(0, 4, body, 0)

    sketch(0)
    pl.semaphore_wait(barrier, 6)
    share_out(0)
    sketch(1)
    begin(0)()
    share_out(1)
    sketch(2)
    for event in (hop(0, 1), hop(0, 2), spread(0, 1), pass_on(0, 0)):
        event()
    share_out(2)
    make([(3, corner(0, 0)), (4, pass_on(0, 1)), (6, begin(1)), (8, hop(0, 3)), (8, spread(0, 2)), (8, corner(0, 1)), (9, begin(2)), (11, hop(1, 1)), (11, hop(1, 2)), (11, spread(1, 1)), (11, pass_on(1, 0)), (12, spread(0, 3)), (12, pass_on(0, 2)), (13, hop(2, 1)), (13, hop(2, 2)), (13, spread(2, 1)), (13, pass_on(2, 0)), (15, corner(0, 2)), (15, hop(1, 3)), (15, spread(1, 2)), (15, pass_on(1, 1)), (15, corner(1, 0)), (16, pass_on(0, 3)), (17, hop(2, 3)), (17, spread(2, 2)), (17, pass_on(2, 1)), (17, corner(2, 0)), (19, spread(1, 3)), (19, pass_on(1, 2)), (19, corner(1, 1)), (19, corner(0, 3))])
    multiply(0, False, [(0, gathered(0, 0)), (1, spread(2, 3)), (1, pass_on(2, 2)), (1, corner(2, 1)), (1, gathered(0, 1)), (2, gathered(0, 2)), (3, pass_on(1, 3)), (3, corner(1, 2)), (3, gathered(0, 3))])
    multiply(1, False, [(0, pass_on(2, 3)), (0, corner(2, 2)), (0, gathered(1, 0)), (1, gathered(1, 1)), (2, corner(1, 3)), (2, gathered(1, 2)), (3, corner(2, 3)), (3, gathered(1, 3))])
    multiply(2, True, [(0, gathered(2, 0)), (1, gathered(2, 1)), (2, gathered(2, 2)), (3, gathered(2, 3))])
    for c in range(len(CHUNKS)):
        for d in (1, 2, 3):
            sums(c, d).wait_send()
        up(c).wait_send()
        for d in range(4):
            for axis in range(2):
                over(c, d, axis).wait_send()
            forward(c, d).wait_send()
            across(c, d).wait_send()

        @pl.when(inner == 1)
        def _(c=c):
            for d in range(4):
                relay(c, d).wait_send()


def fused(scale, own, packed, mask, waves, test_block):
    rows, modes, width = own.shape[0], waves.shape[1] // 8, test_block.shape[1]
    chunks, share, _ = mask.shape
    total, step = packed.shape[1], SKETCH[0]
    steps = test_block.shape[0] // step
    return pl.pallas_call(
        functools.partial(fused_kernel, scale),
        out_shape=jax.ShapeDtypeStruct((modes, 2 * width), jnp.float32),
        in_specs=[pl.BlockSpec(memory_space=pltpu.VMEM)] * 4 + [pl.BlockSpec(memory_space=pl.ANY)],
        out_specs=pl.BlockSpec(memory_space=pltpu.VMEM),
        scratch_shapes=[
            pltpu.VMEM((16, waves.shape[1]), jnp.float32),
            pltpu.VMEM((modes, DEPTH), jnp.bfloat16),
            pltpu.VMEM((steps, step, width), jnp.int32),
            pltpu.VMEM((steps, step, width), jnp.bfloat16),
            pltpu.VMEM((DEPTH, waves.shape[1]), jnp.bfloat16),
            pltpu.VMEM((DEPTH, total), jnp.bfloat16),
            pltpu.VMEM((2 * LARGEST, step), jnp.bfloat16),
            pltpu.VMEM((LARGEST, 2 * width), jnp.float32),
            pltpu.VMEM((chunks, share, 2 * width), jnp.float32),
            pltpu.VMEM((chunks, 3, share, 2 * width), jnp.bfloat16),
            pltpu.VMEM((chunks, 3, share, 2 * width), jnp.bfloat16),
            pltpu.VMEM((total, 2 * width), jnp.bfloat16),
            pltpu.VMEM((total // BLOCK, modes, 2 * BLOCK), jnp.bfloat16),
            pltpu.VMEM((4 * LARGEST, 2 * width), jnp.bfloat16),
            pltpu.SemaphoreType.DMA((steps,)),
        ]
        + [pltpu.SemaphoreType.DMA((chunks, n)) for n in (3, 3, 5, 3, 6, 6, 6, 6, 4, 4)],
        compiler_params=pltpu.CompilerParams(
            collective_id=2, has_side_effects=True, vmem_limit_bytes=60 * 2**20
        ),
    )(own, packed, mask, waves, test_block)


def padded(rows, factor):
    rows = rows.astype(jnp.float32) * factor
    return jnp.pad(rows, ((0, DEPTH - rows.shape[0]), (0, 0))).astype(jnp.bfloat16)


def sketch_part(count, points, waves, test_block, dtype):
    rows, modes, width = points.shape[0], waves.shape[1], test_block.shape[1]
    step, tile, chunk = SKETCH
    return pl.pallas_call(
        functools.partial(sketch_kernel, dtype),
        out_shape=jax.ShapeDtypeStruct((rows, 2 * width), dtype),
        grid=(modes // step,),
        in_specs=[
            pl.BlockSpec(memory_space=pltpu.SMEM),
            pl.BlockSpec((rows, DEPTH), lambda m: (0, 0)),
            pl.BlockSpec((DEPTH, step), lambda m: (0, m)),
            pl.BlockSpec((step, width), lambda m: (m, 0)),
        ],
        out_specs=pl.BlockSpec((rows, 2 * width), lambda m: (0, 0)),
        scratch_shapes=[
            pltpu.VMEM((step // chunk, tile, chunk), jnp.float32),
            pltpu.VMEM((2 * tile, step), jnp.bfloat16),
            pltpu.VMEM((rows, 2 * width), jnp.float32),
            pltpu.VMEM((step, width), jnp.bfloat16),
        ],
        compiler_params=pltpu.CompilerParams(vmem_limit_bytes=40 * 2**20),
        cost_estimate=pl.CostEstimate(
            flops=4 * rows * modes * width, bytes_accessed=4 * modes * width, transcendentals=0
        ),
    )(count, points, waves, test_block)


def adjoint_part(scale, counts, waves, points, sketch, capacity):
    modes, slots, width = waves.shape[0], points.shape[1], sketch.shape[1]
    return pl.pallas_call(
        functools.partial(adjoint_kernel, scale),
        out_shape=jax.ShapeDtypeStruct((modes, width), jnp.float32),
        grid=(slots // capacity,),
        in_specs=[
            pl.BlockSpec(memory_space=pltpu.SMEM),
            pl.BlockSpec((modes, DEPTH), lambda p: (0, 0)),
            pl.BlockSpec((DEPTH, capacity), lambda p: (0, p)),
            pl.BlockSpec((capacity, width), lambda p: (p, 0)),
        ],
        out_specs=pl.BlockSpec((modes, width), lambda p: (0, 0)),
        scratch_shapes=[
            pltpu.VMEM((modes // TILE, TILE, TILE), jnp.float32),
            pltpu.VMEM((modes // TILE, TILE, 2 * TILE), jnp.bfloat16),
            pltpu.VMEM((2 * TILE, width), jnp.bfloat16),
        ],
        compiler_params=pltpu.CompilerParams(vmem_limit_bytes=40 * 2**20),
        cost_estimate=pl.CostEstimate(
            flops=4 * modes * slots * width, bytes_accessed=2 * slots * width, transcendentals=0
        ),
    )(counts, waves, points, sketch)


def exchange_kernel(
    scale, part_ref, info_ref, waves_ref, out_ref, all_ref, phase_ref, landed_ref, points_ref, turns_ref, made_ref, made_sem,
    sum_out, sum_in, z_out, z_in, x_out, x_in, y_out, y_in, core_out, core_in, info_out, info_in,
):
    pt, md = lax.axis_index("pt"), lax.axis_index("md")
    rows = part_ref.shape[0]
    quarter = rows // 4
    core, x, y = pt % 2, (pt // 2) % 2, pt // 4
    core_pt, x_pt, y_pt = pt + 1 - 2 * core, pt + 2 - 4 * x, pt + 4 - 8 * y
    xy_pt = x_pt + 4 - 8 * y

    def send(source, target, out_sem, in_sem, to_pt, to_md):
        copy = pltpu.make_async_remote_copy(
            src_ref=source, dst_ref=target, send_sem=out_sem, recv_sem=in_sem,
            device_id=(to_pt, to_md), device_id_type=pl.DeviceIdType.MESH,
        )
        copy.start()
        return copy

    def place(slab, part):
        return out_ref.at[pl.ds(pl.multiple_of(slab * rows + part * quarter, quarter), quarter), :]

    barrier = pltpu.get_barrier_semaphore()
    for d in range(1, 4):
        pl.semaphore_signal(
            barrier, inc=1, device_id=(pt, (md + d) % 4), device_id_type=pl.DeviceIdType.MESH
        )
    for d in range(1, 8):
        pl.semaphore_signal(
            barrier, inc=1, device_id=((pt + d) % 8, md), device_id_type=pl.DeviceIdType.MESH
        )
    pl.semaphore_wait(barrier, 10)

    sums = []
    for d in (2, 1, 3):
        to = (md + d) % 4
        source = part_ref.at[pl.ds(pl.multiple_of(to * quarter, quarter), quarter), :]
        sums.append(send(source, landed_ref.at[d - 1], sum_out.at[d - 1], sum_in.at[d - 1], pt, to))
    others = [
        send(info_ref, all_ref.at[pt], info_out.at[d - 1], info_in.at[d - 1], (pt + d) % 8, md)
        for d in range(1, 8)
    ]
    all_ref[pt] = info_ref[...]
    for copy in others:
        copy.wait_recv()
    points_ref[...] = jnp.zeros_like(points_ref)
    for slab in range(8):
        points_ref[pl.ds(0, 8), pl.ds(slab * rows, rows)] = all_ref[slab].astype(jnp.float32)

    def keep(index):
        slot = index % 2
        return pltpu.make_async_copy(made_ref.at[slot], phase_ref.at[index], made_sem.at[slot])

    def make(first, last):
        def body(index, carry):
            slot = index % 2
            start = pl.multiple_of(index * TILE, TILE)
            coords = points_ref[:, pl.ds(start, TILE)].astype(jnp.bfloat16)

            if first >= 2:
                keep(index - 2).wait()
            for k in range(waves_ref.shape[0] // TILE):
                turns_ref[k] = jnp.dot(
                    waves_ref[pl.ds(k * TILE, TILE), :], coords, preferred_element_type=jnp.float32
                )
                for j in range(TILE // STRIP):
                    re, im = phases(turns_ref[k, pl.ds(j * STRIP, STRIP), :])
                    at = pl.ds(k * TILE + j * STRIP, STRIP)
                    made_ref[slot, at, pl.ds(0, TILE)] = re.astype(jnp.bfloat16)
                    made_ref[slot, at, pl.ds(TILE, TILE)] = im.astype(jnp.bfloat16)
            keep(index).start()
            return carry

        lax.fori_loop(first, last, body, 0)

    make(0, 2)
    make(2, MARKS[0])
    for copy in sums:
        copy.wait_recv()
    total = part_ref[pl.ds(pl.multiple_of(md * quarter, quarter), quarter), :].astype(jnp.float32)
    for d in range(3):
        total = total + landed_ref[d].astype(jnp.float32)
    place(pt, md)[...] = (total * scale).astype(jnp.bfloat16)

    own = place(pt, md)
    ups = [send(own, own, z_out.at[d - 1], z_in.at[d - 1], pt, (md + d) % 4) for d in (1, 2, 3)]
    pieces = [md, (md + 3) % 4, (md + 2) % 4, (md + 1) % 4]
    over_x, over_y, over_core = [], [], []
    for d in range(4):
        if d:
            ups[d - 1].wait_recv()
        here = place(pt, pieces[d])
        over_x.append(send(here, here, x_out.at[d], x_in.at[d], x_pt, md))
        over_y.append(send(here, here, y_out.at[d], y_in.at[d], y_pt, md))
        over_core.append(send(here, here, core_out.at[d], core_in.at[d], core_pt, md))
        make(MARKS[d], MARKS[d + 1])
    forward_x, forward_y = [], []
    for d in range(4):
        over_x[d].wait_recv()
        here = place(x_pt, pieces[d])
        if d < 2:
            forward_y.append(send(here, here, y_out.at[4 + d], y_in.at[4 + d], y_pt, md))
        over_core.append(send(here, here, core_out.at[4 + d], core_in.at[4 + d], core_pt, md))
        over_y[d].wait_recv()
        here = place(y_pt, pieces[d])
        if d >= 2:
            forward_x.append(send(here, here, x_out.at[2 + d], x_in.at[2 + d], x_pt, md))
        over_core.append(send(here, here, core_out.at[8 + d], core_in.at[8 + d], core_pt, md))
        make(MARKS[4 + d], MARKS[5 + d])
    for d in range(4):
        (forward_y[d] if d < 2 else forward_x[d - 2]).wait_recv()
        here = place(xy_pt, pieces[d])
        over_core.append(send(here, here, core_out.at[12 + d], core_in.at[12 + d], core_pt, md))
    make(MARKS[8], phase_ref.shape[0])
    keep(phase_ref.shape[0] - 2).wait()
    keep(phase_ref.shape[0] - 1).wait()
    for copy in over_core:
        copy.wait_recv()
    for copy in sums + others + ups + over_x + over_y + over_core + forward_x + forward_y:
        copy.wait_send()


def exchange(scale, part, info, waves):
    rows, width = part.shape
    modes = waves.shape[0]
    sems = [n for n in (3, 3, 6, 6, 16, 7) for _ in range(2)]
    return pl.pallas_call(
        functools.partial(exchange_kernel, scale),
        out_shape=(
            jax.ShapeDtypeStruct((8 * rows, width), jnp.bfloat16),
            jax.ShapeDtypeStruct((8,) + info.shape, info.dtype),
            jax.ShapeDtypeStruct((8 * rows // TILE, modes, 2 * TILE), jnp.bfloat16),
        ),
        in_specs=[pl.BlockSpec(memory_space=pltpu.VMEM)] * 3,
        out_specs=(pl.BlockSpec(memory_space=pltpu.VMEM),) * 2 + (pl.BlockSpec(memory_space=pl.ANY),),
        scratch_shapes=[
            pltpu.VMEM((3, rows // 4, width), jnp.bfloat16),
            pltpu.VMEM((DEPTH, 8 * rows), jnp.float32),
            pltpu.VMEM((modes // TILE, TILE, TILE), jnp.float32),
            pltpu.VMEM((2, modes, 2 * TILE), jnp.bfloat16),
            pltpu.SemaphoreType.DMA((2,)),
        ]
        + [pltpu.SemaphoreType.DMA((n,)) for n in sems],
        compiler_params=pltpu.CompilerParams(
            collective_id=0, has_side_effects=True, vmem_limit_bytes=32 * 2**20
        ),
    )(part, info, waves)


def per_device(grid_index, wavenumbers, test_block, slab_counts):
    capacity = grid_index.shape[1]
    n_pt, n_md = lax.axis_size("pt"), lax.axis_size("md")
    y_scale = 1.0 / (32.0 * math.sqrt(M))
    w_scale = 1.0 / math.sqrt(capacity * n_pt)
    own = wavenumbers.shape[1] // n_pt
    first = lax.axis_index("pt") * own

    def as_given():
        points = padded(grid_index, 1.0)
        waves = padded(wavenumbers, 1.0 / PERIOD)
        mine = lax.dynamic_slice_in_dim(waves, first, own, 1)
        part = sketch_part(slab_counts, points.T, waves, test_block, jnp.bfloat16)
        info = jnp.concatenate(
            [grid_index, jnp.broadcast_to(slab_counts[:, None], (5, capacity))], axis=0
        )
        sketch, gathered, phase = exchange(y_scale, part, info, mine.T)
        per_slab = (gathered[:, 3, 0] + TILE - 1) // TILE
        ends = jnp.sum(jnp.where(jnp.arange(8)[:, None] <= jnp.arange(8)[None, :], per_slab[:, None], 0), axis=0)
        nth = jnp.minimum(jnp.arange(phase.shape[0], dtype=jnp.int32), ends[7] - 1)
        past = (ends[None, :] <= nth[:, None]).astype(jnp.int32)
        slab = jnp.sum(past, axis=1)
        order = slab * (capacity // TILE) + nth - jnp.sum(past * per_slab[None, :], axis=1)
        return product(w_scale, ends[7:], order.astype(jnp.int32), phase, sketch)

    if (n_pt, n_md) == (8, 4):
        everyone, counts, fits = gather(slab_counts, grid_index, 8 * sum(size for _, size in CHUNKS))

        def packed_rows():
            packed, share, mask = compact(y_scale, counts, everyone, capacity)
            return fused(w_scale, share, packed, mask, wavenumbers, test_block)

        return lax.switch(fits[0], (as_given, packed_rows))
    points = padded(grid_index, 1.0)
    waves = padded(wavenumbers, 1.0 / PERIOD)
    mine = lax.dynamic_slice_in_dim(waves, first, own, 1)
    counts = lax.all_gather(slab_counts, "pt", tiled=True)
    all_points = lax.all_gather(grid_index, "pt", axis=1, tiled=True)
    part = sketch_part(slab_counts, points.T, waves, test_block, jnp.float32)
    share = lax.psum_scatter(part, "md", scatter_dimension=0, tiled=True)
    share = (share * y_scale).astype(jnp.bfloat16)
    sketch = lax.all_gather(share, ("pt", "md"), tiled=True)
    return adjoint_part(w_scale, counts, mine.T, padded(all_points, 1.0), sketch, capacity)


def solution(mesh):
    placed = (P(None, "pt"), P(None, "md"), P("md", None), P("pt"))
    return jax.shard_map(
        per_device, mesh=mesh, in_specs=placed, out_specs=P(("md", "pt"), None), check_vma=False
    )
```

```python
import functools
import math

import jax
import jax.numpy as jnp
from jax import lax
from jax.experimental import pallas as pl
from jax.experimental.pallas import tpu as pltpu
from jax.sharding import PartitionSpec as P

M = 32768
PERIOD = 512
DEPTH = 128
TILE = 256
STRIP = 32
SKETCH = (2048, 512, 512)
MARKS = (10, 11, 13, 15, 17, 20, 23, 26, 29)
BLOCK = 128
CHUNK = 512
CHUNKS = ((0, 256), (256, 256), (512, 128))
LARGEST = 256

S = (7.3193808, -3.6889591, 22.557636)
C = (4.03692, -3.305112, 12.524202, 1.7281804)


def phases(whole_turns):
    r = whole_turns - jnp.round(whole_turns)
    z = r * r
    y = z * z
    s = ((y + S[0]) * (z + S[1]) + S[2]) * r
    c = ((y + C[0]) * (z + C[1]) + C[2]) * C[3]
    return 1.0 - s * s, s * c


def sketch_kernel(
    dtype, count_ref, points_ref, waves_ref, test_ref, result_ref, turns_ref, lhs_ref, out_ref, cast_ref
):
    width, tile, step = test_ref.shape[1], turns_ref.shape[1], test_ref.shape[0]
    chunk = turns_ref.shape[2]

    @pl.when(pl.program_id(0) == 0)
    def _():
        out_ref[...] = jnp.zeros_like(out_ref)

    cast_ref[...] = test_ref[...].astype(jnp.float32).astype(jnp.bfloat16)

    def block(index, carry):
        first = pl.multiple_of(index * tile, tile)
        for k in range(step // chunk):
            cols = pl.ds(k * chunk, chunk)
            turns_ref[k] = jnp.dot(
                points_ref[pl.ds(first, tile), :], waves_ref[:, cols], preferred_element_type=jnp.float32
            )
            for j in range(tile // STRIP):
                re, im = phases(turns_ref[k, pl.ds(j * STRIP, STRIP), :])
                lhs_ref[pl.ds(j * STRIP, STRIP), cols] = re.astype(jnp.bfloat16)
                lhs_ref[pl.ds(tile + j * STRIP, STRIP), cols] = im.astype(jnp.bfloat16)
        total = jnp.dot(lhs_ref[...], cast_ref[...], preferred_element_type=jnp.float32)
        out_ref[pl.ds(first, tile), pl.ds(0, width)] += total[:tile]
        out_ref[pl.ds(first, tile), pl.ds(width, width)] += total[tile:]
        return carry

    lax.fori_loop(0, (count_ref[0] + tile - 1) // tile, block, 0)

    @pl.when(pl.program_id(0) == pl.num_programs(0) - 1)
    def _():
        slot = lax.broadcasted_iota(jnp.int32, out_ref.shape, 0)
        result_ref[...] = jnp.where(slot < count_ref[0], out_ref[...], 0.0).astype(dtype)


def adjoint_kernel(scale, counts_ref, waves_ref, points_ref, sketch_ref, out_ref, turns_ref, lhs_ref, rhs_ref):
    modes, width = out_ref.shape[0], sketch_ref.shape[1] // 2
    slab = pl.program_id(0)

    @pl.when(slab == 0)
    def _():
        out_ref[...] = jnp.zeros_like(out_ref)

    def block(index, carry):
        first = pl.multiple_of(index * TILE, TILE)
        rhs_ref[pl.ds(0, TILE), :] = sketch_ref[pl.ds(first, TILE), :]
        rhs_ref[pl.ds(TILE, TILE), pl.ds(0, width)] = sketch_ref[pl.ds(first, TILE), pl.ds(width, width)]
        rhs_ref[pl.ds(TILE, TILE), pl.ds(width, width)] = -sketch_ref[pl.ds(first, TILE), pl.ds(0, width)]
        for k in range(modes // TILE):
            rows = pl.ds(k * TILE, TILE)
            turns_ref[k] = jnp.dot(
                waves_ref[rows, :], points_ref[:, pl.ds(first, TILE)], preferred_element_type=jnp.float32
            )
            for j in range(TILE // STRIP):
                re, im = phases(turns_ref[k, pl.ds(j * STRIP, STRIP), :])
                lhs_ref[k, pl.ds(j * STRIP, STRIP), pl.ds(0, TILE)] = re.astype(jnp.bfloat16)
                lhs_ref[k, pl.ds(j * STRIP, STRIP), pl.ds(TILE, TILE)] = im.astype(jnp.bfloat16)
            out_ref[rows, :] += jnp.dot(lhs_ref[k], rhs_ref[...], preferred_element_type=jnp.float32)
        return carry

    lax.fori_loop(0, (counts_ref[slab] + TILE - 1) // TILE, block, 0)

    @pl.when(slab == pl.num_programs(0) - 1)
    def _():
        out_ref[...] = out_ref[...] * scale


def product_kernel(scale, live_ref, first_ref, second_ref, upper_ref, lower_ref, out_ref, rhs_ref):
    width = upper_ref.shape[1] // 2
    step = pl.program_id(0)

    @pl.when(step == 0)
    def _():
        out_ref[...] = jnp.zeros_like(out_ref)

    @pl.when(2 * step < live_ref[0])
    def _():
        upper, lower = upper_ref[...], lower_ref[...]
        lower = jnp.where(2 * step + 1 < live_ref[0], lower, jnp.zeros_like(lower))
        for g, rows in enumerate((upper, lower)):
            rhs_ref[pl.ds(2 * g * TILE, TILE), :] = rows
            rhs_ref[pl.ds((2 * g + 1) * TILE, TILE), pl.ds(0, width)] = rows[:, width:]
            rhs_ref[pl.ds((2 * g + 1) * TILE, TILE), pl.ds(width, width)] = -rows[:, :width]
        lhs = jnp.concatenate([first_ref[0], second_ref[0]], axis=1)
        out_ref[...] += jnp.dot(lhs, rhs_ref[...], preferred_element_type=jnp.float32)

    @pl.when(step == pl.num_programs(0) - 1)
    def _():
        out_ref[...] = out_ref[...] * scale


def product(scale, live, order, phase, sketch):
    blocks, modes, _ = phase.shape
    width = sketch.shape[1]
    return pl.pallas_call(
        lambda live_ref, order_ref, *refs: product_kernel(scale, live_ref, *refs),
        out_shape=jax.ShapeDtypeStruct((modes, width), jnp.float32),
        grid_spec=pltpu.PrefetchScalarGridSpec(
            num_scalar_prefetch=2,
            grid=(blocks // 2,),
            in_specs=[
                pl.BlockSpec((1, modes, 2 * TILE), lambda b, live, order: (order[2 * b], 0, 0)),
                pl.BlockSpec((1, modes, 2 * TILE), lambda b, live, order: (order[2 * b + 1], 0, 0)),
                pl.BlockSpec((TILE, width), lambda b, live, order: (order[2 * b], 0)),
                pl.BlockSpec((TILE, width), lambda b, live, order: (order[2 * b + 1], 0)),
            ],
            out_specs=pl.BlockSpec((modes, width), lambda b, live, order: (0, 0)),
            scratch_shapes=[pltpu.VMEM((4 * TILE, width), jnp.bfloat16)],
        ),
        compiler_params=pltpu.CompilerParams(vmem_limit_bytes=30 * 2**20),
    )(live, order, phase, phase, sketch, sketch)


def gather_kernel(limit, count_ref, grid_ref, all_ref, counts_ref, fits_ref, info_ref, info_out, info_in):
    pt, md = lax.axis_index("pt"), lax.axis_index("md")
    barrier = pltpu.get_barrier_semaphore()
    for d in range(1, 8):
        pl.semaphore_signal(
            barrier, inc=1, device_id=((pt + d) % 8, md), device_id_type=pl.DeviceIdType.MESH
        )
    blocks = grid_ref.shape[1] // 128
    lines = [grid_ref[d : d + 1, j * 128 : (j + 1) * 128] for d in range(3) for j in range(blocks)]
    lines += [jnp.full((1, 128), count_ref[0] // 32, jnp.int32), jnp.full((1, 128), count_ref[0] % 32, jnp.int32)]
    lines += [jnp.zeros((info_ref.shape[0] - len(lines), 128), jnp.int32)]
    info_ref[...] = jnp.concatenate(lines, axis=0).astype(jnp.float32).astype(jnp.bfloat16)
    pl.semaphore_wait(barrier, 7)
    copies = []
    for d in range(1, 8):
        copy = pltpu.make_async_remote_copy(
            src_ref=info_ref, dst_ref=all_ref.at[pt], send_sem=info_out.at[d - 1], recv_sem=info_in.at[d - 1],
            device_id=((pt + d) % 8, md), device_id_type=pl.DeviceIdType.MESH,
        )
        copy.start()
        copies.append(copy)
    all_ref[pt] = info_ref[...]
    for copy in copies:
        copy.wait()
    digits = [all_ref[slab, 16:32, :].astype(jnp.float32) for slab in range(8)]
    counts = [jnp.max(digit[8:9] * 32.0 + digit[9:10]).astype(jnp.int32) for digit in digits]
    for slab in range(8):
        counts_ref[slab] = counts[slab]
    fits_ref[0] = jnp.where(sum(counts) <= limit, 1, 0)


def gather(count, grid_index, limit):
    shape = (32, 128)
    return pl.pallas_call(
        functools.partial(gather_kernel, limit),
        out_shape=(
            jax.ShapeDtypeStruct((8,) + shape, jnp.bfloat16),
            jax.ShapeDtypeStruct((8,), jnp.int32),
            jax.ShapeDtypeStruct((1,), jnp.int32),
        ),
        in_specs=[pl.BlockSpec(memory_space=pltpu.SMEM), pl.BlockSpec(memory_space=pltpu.VMEM)],
        out_specs=(pl.BlockSpec(memory_space=pltpu.VMEM),) + (pl.BlockSpec(memory_space=pltpu.SMEM),) * 2,
        scratch_shapes=[
            pltpu.VMEM(shape, jnp.bfloat16), pltpu.SemaphoreType.DMA((7,)), pltpu.SemaphoreType.DMA((7,))
        ],
        compiler_params=pltpu.CompilerParams(collective_id=1, has_side_effects=True),
    )(count, grid_index)


def compact_kernel(scale, counts_ref, all_ref, packed_ref, own_ref, mask_ref, wide_ref, line_ref):
    slots = line_ref.shape[1] - 128
    rows = own_ref.shape[0]
    pt, md = lax.axis_index("pt"), lax.axis_index("md")
    wide_ref[...] = jnp.zeros_like(wide_ref)
    line_ref[...] = jnp.zeros_like(line_ref)
    lane = lax.broadcasted_iota(jnp.int32, line_ref.shape, 1)
    start = jnp.int32(0)
    for slab in range(all_ref.shape[0]):
        base = pl.multiple_of((start // 128) * 128, 128)
        shift = start - base
        here = pl.ds(base, slots + 128)
        lines = all_ref[slab].astype(jnp.float32)
        for j in range(slots // 128):
            for d in range(3):
                at = d * (slots // 128) + j
                line_ref[d : d + 1, j * 128 : (j + 1) * 128] = lines[at : at + 1]
        wide_ref[:, here] = jnp.where(lane < shift, wide_ref[:, here], pltpu.roll(line_ref[...], shift, 1))
        start = start + counts_ref[slab]
    packed_ref[...] = wide_ref[:, : packed_ref.shape[1]]
    share = wide_ref[:, pl.ds(pl.multiple_of(pt * rows, 128), rows)]
    tall = jnp.concatenate([share, jnp.zeros((DEPTH - 8, rows), jnp.float32)], axis=0)
    own_ref[...] = tall.T.astype(jnp.bfloat16)
    slot = lax.broadcasted_iota(jnp.int32, mask_ref.shape[1:], 0) + pt * rows
    for c, (base, size) in enumerate(CHUNKS):
        mask_ref[c] = jnp.where(slot + base + md * (size // 4) < start, scale, 0.0)


def compact(scale, counts, everyone, slots):
    rows = sum(size for _, size in CHUNKS)
    total = 8 * rows
    return pl.pallas_call(
        functools.partial(compact_kernel, scale),
        out_shape=(
            jax.ShapeDtypeStruct((8, total), jnp.float32),
            jax.ShapeDtypeStruct((rows, DEPTH), jnp.bfloat16),
            jax.ShapeDtypeStruct((len(CHUNKS), LARGEST // 4, 128), jnp.float32),
        ),
        in_specs=[pl.BlockSpec(memory_space=pltpu.SMEM), pl.BlockSpec(memory_space=pltpu.VMEM)],
        out_specs=(pl.BlockSpec(memory_space=pltpu.VMEM),) * 3,
        scratch_shapes=[
            pltpu.VMEM((8, total + slots + 128), jnp.float32), pltpu.VMEM((8, slots + 128), jnp.float32)
        ],
    )(counts, everyone)


def fused_kernel(
    scale, own_ref, packed_ref, mask_ref, waves_ref, test_ref, out_ref,
    tall_ref, mine_ref, stage_ref, cast_ref, wide_waves_ref, points_ref, lhs_ref, sum_ref, keep_ref, part_ref, landed_ref,
    y_ref, phase_ref, rhs_ref,
    test_sem, sum_out, sum_in, z_out, z_in, x_out, x_in, y_out, y_in, core_out, core_in,
):
    pt, md = lax.axis_index("pt"), lax.axis_index("md")
    rows = own_ref.shape[0]
    step, width = cast_ref.shape[1], cast_ref.shape[2]
    modes = mine_ref.shape[0]
    core, x, y = pt % 2, (pt // 2) % 2, pt // 4
    core_pt, x_pt, y_pt = pt + 1 - 2 * core, pt + 2 - 4 * x, pt + 4 - 8 * y
    xy_pt = x_pt + 4 - 8 * y
    inner, upper = (md + 1) // 2 % 2, md // 2
    partner, cross = md + 1 - 2 * (md % 2), 3 - md
    pieces = [md, partner, upper * 3 + (1 - 2 * upper) * 2, upper * 3 + (1 - 2 * upper) * 3]

    def remote(source, target, out_sem, in_sem, to_pt, to_md):
        return pltpu.make_async_remote_copy(
            src_ref=source, dst_ref=target, send_sem=out_sem, recv_sem=in_sem,
            device_id=(to_pt, to_md), device_id_type=pl.DeviceIdType.MESH,
        )

    def place(slab, c, part):
        base, size = CHUNKS[c]
        first = pl.multiple_of(slab * rows + base + part * (size // 4), 32)
        return y_ref.at[pl.ds(first, size // 4), :]

    def fetch(index):
        return pltpu.make_async_copy(
            test_ref.at[pl.ds(pl.multiple_of(index * step, step), step), :], stage_ref.at[index], test_sem.at[index]
        )

    for index in range(cast_ref.shape[0]):
        fetch(index).start()
    barrier = pltpu.get_barrier_semaphore()
    for d in range(1, 4):
        pl.semaphore_signal(
            barrier, inc=1, device_id=(pt, (md + d) % 4), device_id_type=pl.DeviceIdType.MESH
        )
    for other in (core_pt, x_pt, y_pt):
        pl.semaphore_signal(barrier, inc=1, device_id=(other, md), device_id_type=pl.DeviceIdType.MESH)

    tall_ref[...] = jnp.zeros_like(tall_ref)
    tall_ref[pl.ds(0, 3), :] = waves_ref[...].astype(jnp.float32) * (1.0 / PERIOD)
    wide_waves_ref[...] = jnp.zeros_like(wide_waves_ref)
    wide_waves_ref[pl.ds(0, 16), :] = tall_ref[...].astype(jnp.bfloat16)
    mine = tall_ref[:, pl.ds(pl.multiple_of(pt * modes, modes), modes)]
    mine = jnp.concatenate([mine, jnp.zeros((DEPTH - 16, modes), jnp.float32)], axis=0)
    mine_ref[...] = mine.T.astype(jnp.bfloat16)
    points_ref[...] = jnp.zeros_like(points_ref)
    points_ref[pl.ds(0, 16), :] = jnp.concatenate(
        [packed_ref[...], jnp.zeros_like(packed_ref)], axis=0
    ).astype(jnp.bfloat16)
    out_ref[...] = jnp.zeros_like(out_ref)

    def at_step(index, events):
        for step_of in sorted({when for when, _ in events}):

            @pl.when(index == step_of)
            def _(step_of=step_of):
                for when, event in events:
                    if when == step_of:
                        event()

    def sketch(c):
        base, size = CHUNKS[c]
        here = pl.ds(0, size)
        sum_ref[here, :] = jnp.zeros((size, 2 * width), jnp.float32)

        def body(index, carry):
            if c == 0:
                fetch(index).wait()
                cast_ref[index] = stage_ref[index].astype(jnp.float32).astype(jnp.bfloat16)
            for k in range(step // CHUNK):
                cols = pl.ds(pl.multiple_of(index * step + k * CHUNK, CHUNK), CHUNK)
                points = own_ref[pl.ds(base, size), :]
                turns = jnp.dot(points, wide_waves_ref[:, cols], preferred_element_type=jnp.float32)
                for at in range(0, size, STRIP):
                    re, im = phases(turns[at : at + STRIP])
                    lhs_ref[pl.ds(at, STRIP), pl.ds(k * CHUNK, CHUNK)] = re.astype(jnp.bfloat16)
                    lhs_ref[pl.ds(size + at, STRIP), pl.ds(k * CHUNK, CHUNK)] = im.astype(jnp.bfloat16)
            total = jnp.dot(lhs_ref[pl.ds(0, 2 * size), :], cast_ref[index], preferred_element_type=jnp.float32)
            sum_ref[here, pl.ds(0, width)] += total[:size]
            sum_ref[here, pl.ds(width, width)] += total[size:]
            return carry

        lax.fori_loop(0, cast_ref.shape[0], body, 0)

    def sums(c, d):
        here = pl.ds(0, CHUNKS[c][1] // 4)
        return remote(
            part_ref.at[c, d - 1, here], landed_ref.at[c, d - 1, here], sum_out.at[c, d - 1], sum_in.at[c, d - 1],
            pt, (md + d) % 4,
        )

    def share_out(c):
        quarter = CHUNKS[c][1] // 4
        here = pl.ds(0, quarter)
        for d in (2, 1, 3):
            rows_of = pl.ds(pl.multiple_of((md + d) % 4 * quarter, 16), quarter)
            part_ref[c, d - 1, here, :] = sum_ref[rows_of, :].astype(jnp.bfloat16)
            sums(c, d).start()
        keep_ref[c, here, :] = sum_ref[pl.ds(pl.multiple_of(md * quarter, 16), quarter), :]

    def up(c):
        here = place(pt, c, md)
        return remote(here, here, z_out.at[c, 0], z_in.at[c, 0], pt, partner)

    def relay(c, d):
        here = place(pt, c, pieces[d])
        landing = (1, 2, 1, 2)[d]
        return remote(here, here, z_out.at[c, 1 + d], z_in.at[c, landing], pt, cross if d < 2 else partner)

    def over(c, d, axis):
        here = place(pt, c, pieces[d])
        out_sem, in_sem, to = ((x_out, x_in, x_pt), (y_out, y_in, y_pt))[axis]
        return remote(here, here, out_sem.at[c, d], in_sem.at[c, d], to, md)

    def forward(c, d):
        if d < 2:
            here = place(x_pt, c, pieces[d])
            return remote(here, here, y_out.at[c, 4 + d], y_in.at[c, 4 + d], y_pt, md)
        here = place(y_pt, c, pieces[d])
        return remote(here, here, x_out.at[c, 2 + d], x_in.at[c, 2 + d], x_pt, md)

    def across(c, n):
        base, size = CHUNKS[c]
        here = y_ref.at[pl.ds(pl.multiple_of((pt, x_pt, y_pt, xy_pt)[n] * rows + base, 128), size), :]
        return remote(here, here, core_out.at[c, n], core_in.at[c, n], core_pt, md)

    def begin(c):
        def event():
            here = pl.ds(0, CHUNKS[c][1] // 4)
            for n in (1, 2, 3):
                sums(c, n).wait_recv()
            total = keep_ref[c, here, :]
            for n in range(3):
                total = total + landed_ref[c, n, here, :].astype(jnp.float32)
            place(pt, c, md)[...] = (total * mask_ref[c, here, :1]).astype(jnp.bfloat16)
            up(c).start()

            @pl.when(inner == 1)
            def _():
                relay(c, 0).start()

            for axis in range(2):
                over(c, 0, axis).start()

        return event

    def landed(c, d):
        piece = place(pt, c, pieces[d])
        return remote(piece, piece, z_out.at[c, 0], z_in.at[c, d - 1], pt, partner)

    def hop(c, d):
        def event():
            @pl.when(inner == 1)
            def _():
                landed(c, d).wait_recv()
                relay(c, d).start()

        return event

    def spread(c, d):
        def event():
            @pl.when(inner == 0)
            def _():
                landed(c, d).wait_recv()

            for axis in range(2):
                over(c, d, axis).start()
            if d == 3:
                across(c, 0).start()

        return event

    def pass_on(c, d):
        def event():
            over(c, d, 0).wait_recv()
            if d < 2:
                forward(c, d).start()
            over(c, d, 1).wait_recv()
            if d >= 2:
                forward(c, d).start()
            if d == 3:
                across(c, 1).start()
                across(c, 2).start()

        return event

    def corner(c, d):
        def event():
            forward(c, d).wait_recv()
            if d == 3:
                across(c, 3).start()

        return event

    def gathered(c, n):
        def event():
            across(c, n).wait_recv()

        return event

    def pair_of(nth):
        return (x + nth) % 2 + 2 * ((y + nth // 2) % 2)

    def make(events):
        per = 2 * rows // (2 * BLOCK)

        def body(nth, carry):
            index = pair_of(nth // per) * per + nth % per
            start = pl.multiple_of(index * 2 * BLOCK, 2 * BLOCK)
            coords = points_ref[:, pl.ds(start, 2 * BLOCK)]
            for k in range(modes // TILE):
                turns = jnp.dot(
                    mine_ref[pl.ds(k * TILE, TILE), :], coords, preferred_element_type=jnp.float32
                )
                for j in range(TILE // STRIP):
                    re, im = phases(turns[j * STRIP : (j + 1) * STRIP])
                    re, im = re.astype(jnp.bfloat16), im.astype(jnp.bfloat16)
                    at = pl.ds(k * TILE + j * STRIP, STRIP)
                    for h in range(2):
                        cols = slice(h * BLOCK, (h + 1) * BLOCK)
                        phase_ref[2 * index + h, at, pl.ds(0, BLOCK)] = re[:, cols]
                        phase_ref[2 * index + h, at, pl.ds(BLOCK, BLOCK)] = im[:, cols]
            at_step(nth, events)
            return carry

        lax.fori_loop(0, 4 * per, body, 0)

    def multiply(base, size, last, events):

        def body(nth, carry):
            at_step(nth, events)
            terms = []
            for h in range(2):
                slab = 2 * pair_of(nth) + h
                for b in range(size // BLOCK):
                    block = y_ref[pl.ds(pl.multiple_of(slab * rows + base + b * BLOCK, BLOCK), BLOCK), :]
                    at = 2 * BLOCK * len(terms)
                    rhs_ref[pl.ds(at, BLOCK), :] = block
                    rhs_ref[pl.ds(at + BLOCK, BLOCK), pl.ds(0, width)] = block[:, width:]
                    rhs_ref[pl.ds(at + BLOCK, BLOCK), pl.ds(width, width)] = -block[:, :width]
                    terms.append(phase_ref[slab * (rows // BLOCK) + base // BLOCK + b])
            total = jnp.dot(
                jnp.concatenate(terms, axis=1), rhs_ref[pl.ds(0, 4 * size), :], preferred_element_type=jnp.float32
            )
            if last:
                out_ref[...] = (out_ref[...] + total) * jnp.where(nth == 3, scale, 1.0)
            else:
                out_ref[...] += total
            return carry

        lax.fori_loop(0, 4, body, 0)

    sketch(0)
    pl.semaphore_wait(barrier, 6)
    share_out(0)
    sketch(1)
    begin(0)()
    share_out(1)
    sketch(2)
    for event in (hop(0, 1), hop(0, 2), spread(0, 1), pass_on(0, 0)):
        event()
    share_out(2)
    make([(3, corner(0, 0)), (4, pass_on(0, 1)), (6, begin(1)), (8, hop(0, 3)), (8, spread(0, 2)), (8, corner(0, 1)), (9, begin(2)), (11, hop(1, 1)), (11, hop(1, 2)), (11, spread(1, 1)), (11, pass_on(1, 0)), (12, spread(0, 3)), (12, pass_on(0, 2)), (13, hop(2, 1)), (13, hop(2, 2)), (13, spread(2, 1)), (13, pass_on(2, 0)), (15, corner(0, 2)), (15, hop(1, 3)), (15, spread(1, 2)), (15, pass_on(1, 1)), (15, corner(1, 0)), (16, pass_on(0, 3)), (17, hop(2, 3)), (17, spread(2, 2)), (17, pass_on(2, 1)), (17, corner(2, 0)), (19, spread(1, 3)), (19, pass_on(1, 2)), (19, corner(1, 1)), (19, corner(0, 3))])
    multiply(0, CHUNKS[0][1], False, [(0, gathered(0, 0)), (1, spread(2, 3)), (1, pass_on(2, 2)), (1, corner(2, 1)), (1, gathered(0, 1)), (2, gathered(0, 2)), (3, pass_on(1, 3)), (3, corner(1, 2)), (3, gathered(0, 3))])
    multiply(CHUNKS[1][0], rows - CHUNKS[1][0], True, [
        (0, pass_on(2, 3)), (0, corner(2, 2)), (0, gathered(1, 0)), (0, gathered(2, 0)),
        (1, corner(1, 3)), (1, gathered(1, 1)), (1, gathered(2, 1)),
        (2, corner(2, 3)), (2, gathered(1, 2)), (2, gathered(2, 2)), (3, gathered(1, 3)), (3, gathered(2, 3)),
    ])
    for c in range(len(CHUNKS)):
        for d in (1, 2, 3):
            sums(c, d).wait_send()
        up(c).wait_send()
        for d in range(4):
            for axis in range(2):
                over(c, d, axis).wait_send()
            forward(c, d).wait_send()
            across(c, d).wait_send()

        @pl.when(inner == 1)
        def _(c=c):
            for d in range(4):
                relay(c, d).wait_send()


def fused(scale, own, packed, mask, waves, test_block):
    rows, modes, width = own.shape[0], waves.shape[1] // 8, test_block.shape[1]
    chunks, share, _ = mask.shape
    total, step = packed.shape[1], SKETCH[0]
    steps = test_block.shape[0] // step
    return pl.pallas_call(
        functools.partial(fused_kernel, scale),
        out_shape=jax.ShapeDtypeStruct((modes, 2 * width), jnp.float32),
        in_specs=[pl.BlockSpec(memory_space=pltpu.VMEM)] * 4 + [pl.BlockSpec(memory_space=pl.ANY)],
        out_specs=pl.BlockSpec(memory_space=pltpu.VMEM),
        scratch_shapes=[
            pltpu.VMEM((16, waves.shape[1]), jnp.float32),
            pltpu.VMEM((modes, DEPTH), jnp.bfloat16),
            pltpu.VMEM((steps, step, width), jnp.int32),
            pltpu.VMEM((steps, step, width), jnp.bfloat16),
            pltpu.VMEM((DEPTH, waves.shape[1]), jnp.bfloat16),
            pltpu.VMEM((DEPTH, total), jnp.bfloat16),
            pltpu.VMEM((2 * LARGEST, step), jnp.bfloat16),
            pltpu.VMEM((LARGEST, 2 * width), jnp.float32),
            pltpu.VMEM((chunks, share, 2 * width), jnp.float32),
            pltpu.VMEM((chunks, 3, share, 2 * width), jnp.bfloat16),
            pltpu.VMEM((chunks, 3, share, 2 * width), jnp.bfloat16),
            pltpu.VMEM((total, 2 * width), jnp.bfloat16),
            pltpu.VMEM((total // BLOCK, modes, 2 * BLOCK), jnp.bfloat16),
            pltpu.VMEM((4 * (rows - LARGEST), 2 * width), jnp.bfloat16),
            pltpu.SemaphoreType.DMA((steps,)),
        ]
        + [pltpu.SemaphoreType.DMA((chunks, n)) for n in (3, 3, 5, 3, 6, 6, 6, 6, 4, 4)],
        compiler_params=pltpu.CompilerParams(
            collective_id=2, has_side_effects=True, vmem_limit_bytes=60 * 2**20
        ),
    )(own, packed, mask, waves, test_block)


def padded(rows, factor):
    rows = rows.astype(jnp.float32) * factor
    return jnp.pad(rows, ((0, DEPTH - rows.shape[0]), (0, 0))).astype(jnp.bfloat16)


def sketch_part(count, points, waves, test_block, dtype):
    rows, modes, width = points.shape[0], waves.shape[1], test_block.shape[1]
    step, tile, chunk = SKETCH
    return pl.pallas_call(
        functools.partial(sketch_kernel, dtype),
        out_shape=jax.ShapeDtypeStruct((rows, 2 * width), dtype),
        grid=(modes // step,),
        in_specs=[
            pl.BlockSpec(memory_space=pltpu.SMEM),
            pl.BlockSpec((rows, DEPTH), lambda m: (0, 0)),
            pl.BlockSpec((DEPTH, step), lambda m: (0, m)),
            pl.BlockSpec((step, width), lambda m: (m, 0)),
        ],
        out_specs=pl.BlockSpec((rows, 2 * width), lambda m: (0, 0)),
        scratch_shapes=[
            pltpu.VMEM((step // chunk, tile, chunk), jnp.float32),
            pltpu.VMEM((2 * tile, step), jnp.bfloat16),
            pltpu.VMEM((rows, 2 * width), jnp.float32),
            pltpu.VMEM((step, width), jnp.bfloat16),
        ],
        compiler_params=pltpu.CompilerParams(vmem_limit_bytes=40 * 2**20),
        cost_estimate=pl.CostEstimate(
            flops=4 * rows * modes * width, bytes_accessed=4 * modes * width, transcendentals=0
        ),
    )(count, points, waves, test_block)


def adjoint_part(scale, counts, waves, points, sketch, capacity):
    modes, slots, width = waves.shape[0], points.shape[1], sketch.shape[1]
    return pl.pallas_call(
        functools.partial(adjoint_kernel, scale),
        out_shape=jax.ShapeDtypeStruct((modes, width), jnp.float32),
        grid=(slots // capacity,),
        in_specs=[
            pl.BlockSpec(memory_space=pltpu.SMEM),
            pl.BlockSpec((modes, DEPTH), lambda p: (0, 0)),
            pl.BlockSpec((DEPTH, capacity), lambda p: (0, p)),
            pl.BlockSpec((capacity, width), lambda p: (p, 0)),
        ],
        out_specs=pl.BlockSpec((modes, width), lambda p: (0, 0)),
        scratch_shapes=[
            pltpu.VMEM((modes // TILE, TILE, TILE), jnp.float32),
            pltpu.VMEM((modes // TILE, TILE, 2 * TILE), jnp.bfloat16),
            pltpu.VMEM((2 * TILE, width), jnp.bfloat16),
        ],
        compiler_params=pltpu.CompilerParams(vmem_limit_bytes=40 * 2**20),
        cost_estimate=pl.CostEstimate(
            flops=4 * modes * slots * width, bytes_accessed=2 * slots * width, transcendentals=0
        ),
    )(counts, waves, points, sketch)


def exchange_kernel(
    scale, part_ref, info_ref, waves_ref, out_ref, all_ref, phase_ref, landed_ref, points_ref, turns_ref, made_ref, made_sem,
    sum_out, sum_in, z_out, z_in, x_out, x_in, y_out, y_in, core_out, core_in, info_out, info_in,
):
    pt, md = lax.axis_index("pt"), lax.axis_index("md")
    rows = part_ref.shape[0]
    quarter = rows // 4
    core, x, y = pt % 2, (pt // 2) % 2, pt // 4
    core_pt, x_pt, y_pt = pt + 1 - 2 * core, pt + 2 - 4 * x, pt + 4 - 8 * y
    xy_pt = x_pt + 4 - 8 * y

    def send(source, target, out_sem, in_sem, to_pt, to_md):
        copy = pltpu.make_async_remote_copy(
            src_ref=source, dst_ref=target, send_sem=out_sem, recv_sem=in_sem,
            device_id=(to_pt, to_md), device_id_type=pl.DeviceIdType.MESH,
        )
        copy.start()
        return copy

    def place(slab, part):
        return out_ref.at[pl.ds(pl.multiple_of(slab * rows + part * quarter, quarter), quarter), :]

    barrier = pltpu.get_barrier_semaphore()
    for d in range(1, 4):
        pl.semaphore_signal(
            barrier, inc=1, device_id=(pt, (md + d) % 4), device_id_type=pl.DeviceIdType.MESH
        )
    for d in range(1, 8):
        pl.semaphore_signal(
            barrier, inc=1, device_id=((pt + d) % 8, md), device_id_type=pl.DeviceIdType.MESH
        )
    pl.semaphore_wait(barrier, 10)

    sums = []
    for d in (2, 1, 3):
        to = (md + d) % 4
        source = part_ref.at[pl.ds(pl.multiple_of(to * quarter, quarter), quarter), :]
        sums.append(send(source, landed_ref.at[d - 1], sum_out.at[d - 1], sum_in.at[d - 1], pt, to))
    others = [
        send(info_ref, all_ref.at[pt], info_out.at[d - 1], info_in.at[d - 1], (pt + d) % 8, md)
        for d in range(1, 8)
    ]
    all_ref[pt] = info_ref[...]
    for copy in others:
        copy.wait_recv()
    points_ref[...] = jnp.zeros_like(points_ref)
    for slab in range(8):
        points_ref[pl.ds(0, 8), pl.ds(slab * rows, rows)] = all_ref[slab].astype(jnp.float32)

    def keep(index):
        slot = index % 2
        return pltpu.make_async_copy(made_ref.at[slot], phase_ref.at[index], made_sem.at[slot])

    def make(first, last):
        def body(index, carry):
            slot = index % 2
            start = pl.multiple_of(index * TILE, TILE)
            coords = points_ref[:, pl.ds(start, TILE)].astype(jnp.bfloat16)

            if first >= 2:
                keep(index - 2).wait()
            for k in range(waves_ref.shape[0] // TILE):
                turns_ref[k] = jnp.dot(
                    waves_ref[pl.ds(k * TILE, TILE), :], coords, preferred_element_type=jnp.float32
                )
                for j in range(TILE // STRIP):
                    re, im = phases(turns_ref[k, pl.ds(j * STRIP, STRIP), :])
                    at = pl.ds(k * TILE + j * STRIP, STRIP)
                    made_ref[slot, at, pl.ds(0, TILE)] = re.astype(jnp.bfloat16)
                    made_ref[slot, at, pl.ds(TILE, TILE)] = im.astype(jnp.bfloat16)
            keep(index).start()
            return carry

        lax.fori_loop(first, last, body, 0)

    make(0, 2)
    make(2, MARKS[0])
    for copy in sums:
        copy.wait_recv()
    total = part_ref[pl.ds(pl.multiple_of(md * quarter, quarter), quarter), :].astype(jnp.float32)
    for d in range(3):
        total = total + landed_ref[d].astype(jnp.float32)
    place(pt, md)[...] = (total * scale).astype(jnp.bfloat16)

    own = place(pt, md)
    ups = [send(own, own, z_out.at[d - 1], z_in.at[d - 1], pt, (md + d) % 4) for d in (1, 2, 3)]
    pieces = [md, (md + 3) % 4, (md + 2) % 4, (md + 1) % 4]
    over_x, over_y, over_core = [], [], []
    for d in range(4):
        if d:
            ups[d - 1].wait_recv()
        here = place(pt, pieces[d])
        over_x.append(send(here, here, x_out.at[d], x_in.at[d], x_pt, md))
        over_y.append(send(here, here, y_out.at[d], y_in.at[d], y_pt, md))
        over_core.append(send(here, here, core_out.at[d], core_in.at[d], core_pt, md))
        make(MARKS[d], MARKS[d + 1])
    forward_x, forward_y = [], []
    for d in range(4):
        over_x[d].wait_recv()
        here = place(x_pt, pieces[d])
        if d < 2:
            forward_y.append(send(here, here, y_out.at[4 + d], y_in.at[4 + d], y_pt, md))
        over_core.append(send(here, here, core_out.at[4 + d], core_in.at[4 + d], core_pt, md))
        over_y[d].wait_recv()
        here = place(y_pt, pieces[d])
        if d >= 2:
            forward_x.append(send(here, here, x_out.at[2 + d], x_in.at[2 + d], x_pt, md))
        over_core.append(send(here, here, core_out.at[8 + d], core_in.at[8 + d], core_pt, md))
        make(MARKS[4 + d], MARKS[5 + d])
    for d in range(4):
        (forward_y[d] if d < 2 else forward_x[d - 2]).wait_recv()
        here = place(xy_pt, pieces[d])
        over_core.append(send(here, here, core_out.at[12 + d], core_in.at[12 + d], core_pt, md))
    make(MARKS[8], phase_ref.shape[0])
    keep(phase_ref.shape[0] - 2).wait()
    keep(phase_ref.shape[0] - 1).wait()
    for copy in over_core:
        copy.wait_recv()
    for copy in sums + others + ups + over_x + over_y + over_core + forward_x + forward_y:
        copy.wait_send()


def exchange(scale, part, info, waves):
    rows, width = part.shape
    modes = waves.shape[0]
    sems = [n for n in (3, 3, 6, 6, 16, 7) for _ in range(2)]
    return pl.pallas_call(
        functools.partial(exchange_kernel, scale),
        out_shape=(
            jax.ShapeDtypeStruct((8 * rows, width), jnp.bfloat16),
            jax.ShapeDtypeStruct((8,) + info.shape, info.dtype),
            jax.ShapeDtypeStruct((8 * rows // TILE, modes, 2 * TILE), jnp.bfloat16),
        ),
        in_specs=[pl.BlockSpec(memory_space=pltpu.VMEM)] * 3,
        out_specs=(pl.BlockSpec(memory_space=pltpu.VMEM),) * 2 + (pl.BlockSpec(memory_space=pl.ANY),),
        scratch_shapes=[
            pltpu.VMEM((3, rows // 4, width), jnp.bfloat16),
            pltpu.VMEM((DEPTH, 8 * rows), jnp.float32),
            pltpu.VMEM((modes // TILE, TILE, TILE), jnp.float32),
            pltpu.VMEM((2, modes, 2 * TILE), jnp.bfloat16),
            pltpu.SemaphoreType.DMA((2,)),
        ]
        + [pltpu.SemaphoreType.DMA((n,)) for n in sems],
        compiler_params=pltpu.CompilerParams(
            collective_id=0, has_side_effects=True, vmem_limit_bytes=32 * 2**20
        ),
    )(part, info, waves)


def per_device(grid_index, wavenumbers, test_block, slab_counts):
    capacity = grid_index.shape[1]
    n_pt, n_md = lax.axis_size("pt"), lax.axis_size("md")
    y_scale = 1.0 / (32.0 * math.sqrt(M))
    w_scale = 1.0 / math.sqrt(capacity * n_pt)
    own = wavenumbers.shape[1] // n_pt
    first = lax.axis_index("pt") * own

    def as_given():
        points = padded(grid_index, 1.0)
        waves = padded(wavenumbers, 1.0 / PERIOD)
        mine = lax.dynamic_slice_in_dim(waves, first, own, 1)
        part = sketch_part(slab_counts, points.T, waves, test_block, jnp.bfloat16)
        info = jnp.concatenate(
            [grid_index, jnp.broadcast_to(slab_counts[:, None], (5, capacity))], axis=0
        )
        sketch, gathered, phase = exchange(y_scale, part, info, mine.T)
        per_slab = (gathered[:, 3, 0] + TILE - 1) // TILE
        ends = jnp.sum(jnp.where(jnp.arange(8)[:, None] <= jnp.arange(8)[None, :], per_slab[:, None], 0), axis=0)
        nth = jnp.minimum(jnp.arange(phase.shape[0], dtype=jnp.int32), ends[7] - 1)
        past = (ends[None, :] <= nth[:, None]).astype(jnp.int32)
        slab = jnp.sum(past, axis=1)
        order = slab * (capacity // TILE) + nth - jnp.sum(past * per_slab[None, :], axis=1)
        return product(w_scale, ends[7:], order.astype(jnp.int32), phase, sketch)

    if (n_pt, n_md) == (8, 4):
        everyone, counts, fits = gather(slab_counts, grid_index, 8 * sum(size for _, size in CHUNKS))

        def packed_rows():
            packed, share, mask = compact(y_scale, counts, everyone, capacity)
            return fused(w_scale, share, packed, mask, wavenumbers, test_block)

        return lax.switch(fits[0], (as_given, packed_rows))
    points = padded(grid_index, 1.0)
    waves = padded(wavenumbers, 1.0 / PERIOD)
    mine = lax.dynamic_slice_in_dim(waves, first, own, 1)
    counts = lax.all_gather(slab_counts, "pt", tiled=True)
    all_points = lax.all_gather(grid_index, "pt", axis=1, tiled=True)
    part = sketch_part(slab_counts, points.T, waves, test_block, jnp.float32)
    share = lax.psum_scatter(part, "md", scatter_dimension=0, tiled=True)
    share = (share * y_scale).astype(jnp.bfloat16)
    sketch = lax.all_gather(share, ("pt", "md"), tiled=True)
    return adjoint_part(w_scale, counts, mine.T, padded(all_points, 1.0), sketch, capacity)


def solution(mesh):
    placed = (P(None, "pt"), P(None, "md"), P("md", None), P("pt"))
    return jax.shard_map(
        per_device, mesh=mesh, in_specs=placed, out_specs=P(("md", "pt"), None), check_vma=False
    )
```

```python
import functools
import math

import jax
import jax.numpy as jnp
from jax import lax
from jax.experimental import pallas as pl
from jax.experimental.pallas import tpu as pltpu
from jax.sharding import PartitionSpec as P

M = 32768
PERIOD = 512
DEPTH = 128
TILE = 256
STRIP = 32
SKETCH = (2048, 512, 512)
MARKS = (10, 11, 13, 15, 17, 20, 23, 26, 29)
BLOCK = 128
CHUNK = 512
CHUNKS = ((0, 256), (256, 256), (512, 128))
LARGEST = 256

S = (7.3193808, -3.6889591, 22.557636)
C = (4.03692, -3.305112, 12.524202, 1.7281804)


def phases(whole_turns):
    r = whole_turns - jnp.round(whole_turns)
    z = r * r
    y = z * z
    s = ((y + S[0]) * (z + S[1]) + S[2]) * r
    c = ((y + C[0]) * (z + C[1]) + C[2]) * C[3]
    return 1.0 - s * s, s * c


def sketch_kernel(
    dtype, count_ref, points_ref, waves_ref, test_ref, result_ref, turns_ref, lhs_ref, out_ref, cast_ref
):
    width, tile, step = test_ref.shape[1], turns_ref.shape[1], test_ref.shape[0]
    chunk = turns_ref.shape[2]

    @pl.when(pl.program_id(0) == 0)
    def _():
        out_ref[...] = jnp.zeros_like(out_ref)

    cast_ref[...] = test_ref[...].astype(jnp.float32).astype(jnp.bfloat16)

    def block(index, carry):
        first = pl.multiple_of(index * tile, tile)
        for k in range(step // chunk):
            cols = pl.ds(k * chunk, chunk)
            turns_ref[k] = jnp.dot(
                points_ref[pl.ds(first, tile), :], waves_ref[:, cols], preferred_element_type=jnp.float32
            )
            for j in range(tile // STRIP):
                re, im = phases(turns_ref[k, pl.ds(j * STRIP, STRIP), :])
                lhs_ref[pl.ds(j * STRIP, STRIP), cols] = re.astype(jnp.bfloat16)
                lhs_ref[pl.ds(tile + j * STRIP, STRIP), cols] = im.astype(jnp.bfloat16)
        total = jnp.dot(lhs_ref[...], cast_ref[...], preferred_element_type=jnp.float32)
        out_ref[pl.ds(first, tile), pl.ds(0, width)] += total[:tile]
        out_ref[pl.ds(first, tile), pl.ds(width, width)] += total[tile:]
        return carry

    lax.fori_loop(0, (count_ref[0] + tile - 1) // tile, block, 0)

    @pl.when(pl.program_id(0) == pl.num_programs(0) - 1)
    def _():
        slot = lax.broadcasted_iota(jnp.int32, out_ref.shape, 0)
        result_ref[...] = jnp.where(slot < count_ref[0], out_ref[...], 0.0).astype(dtype)


def adjoint_kernel(scale, counts_ref, waves_ref, points_ref, sketch_ref, out_ref, turns_ref, lhs_ref, rhs_ref):
    modes, width = out_ref.shape[0], sketch_ref.shape[1] // 2
    slab = pl.program_id(0)

    @pl.when(slab == 0)
    def _():
        out_ref[...] = jnp.zeros_like(out_ref)

    def block(index, carry):
        first = pl.multiple_of(index * TILE, TILE)
        rhs_ref[pl.ds(0, TILE), :] = sketch_ref[pl.ds(first, TILE), :]
        rhs_ref[pl.ds(TILE, TILE), pl.ds(0, width)] = sketch_ref[pl.ds(first, TILE), pl.ds(width, width)]
        rhs_ref[pl.ds(TILE, TILE), pl.ds(width, width)] = -sketch_ref[pl.ds(first, TILE), pl.ds(0, width)]
        for k in range(modes // TILE):
            rows = pl.ds(k * TILE, TILE)
            turns_ref[k] = jnp.dot(
                waves_ref[rows, :], points_ref[:, pl.ds(first, TILE)], preferred_element_type=jnp.float32
            )
            for j in range(TILE // STRIP):
                re, im = phases(turns_ref[k, pl.ds(j * STRIP, STRIP), :])
                lhs_ref[k, pl.ds(j * STRIP, STRIP), pl.ds(0, TILE)] = re.astype(jnp.bfloat16)
                lhs_ref[k, pl.ds(j * STRIP, STRIP), pl.ds(TILE, TILE)] = im.astype(jnp.bfloat16)
            out_ref[rows, :] += jnp.dot(lhs_ref[k], rhs_ref[...], preferred_element_type=jnp.float32)
        return carry

    lax.fori_loop(0, (counts_ref[slab] + TILE - 1) // TILE, block, 0)

    @pl.when(slab == pl.num_programs(0) - 1)
    def _():
        out_ref[...] = out_ref[...] * scale


def product_kernel(scale, live_ref, first_ref, second_ref, upper_ref, lower_ref, out_ref, rhs_ref):
    width = upper_ref.shape[1] // 2
    step = pl.program_id(0)

    @pl.when(step == 0)
    def _():
        out_ref[...] = jnp.zeros_like(out_ref)

    @pl.when(2 * step < live_ref[0])
    def _():
        upper, lower = upper_ref[...], lower_ref[...]
        lower = jnp.where(2 * step + 1 < live_ref[0], lower, jnp.zeros_like(lower))
        for g, rows in enumerate((upper, lower)):
            rhs_ref[pl.ds(2 * g * TILE, TILE), :] = rows
            rhs_ref[pl.ds((2 * g + 1) * TILE, TILE), pl.ds(0, width)] = rows[:, width:]
            rhs_ref[pl.ds((2 * g + 1) * TILE, TILE), pl.ds(width, width)] = -rows[:, :width]
        lhs = jnp.concatenate([first_ref[0], second_ref[0]], axis=1)
        out_ref[...] += jnp.dot(lhs, rhs_ref[...], preferred_element_type=jnp.float32)

    @pl.when(step == pl.num_programs(0) - 1)
    def _():
        out_ref[...] = out_ref[...] * scale


def product(scale, live, order, phase, sketch):
    blocks, modes, _ = phase.shape
    width = sketch.shape[1]
    return pl.pallas_call(
        lambda live_ref, order_ref, *refs: product_kernel(scale, live_ref, *refs),
        out_shape=jax.ShapeDtypeStruct((modes, width), jnp.float32),
        grid_spec=pltpu.PrefetchScalarGridSpec(
            num_scalar_prefetch=2,
            grid=(blocks // 2,),
            in_specs=[
                pl.BlockSpec((1, modes, 2 * TILE), lambda b, live, order: (order[2 * b], 0, 0)),
                pl.BlockSpec((1, modes, 2 * TILE), lambda b, live, order: (order[2 * b + 1], 0, 0)),
                pl.BlockSpec((TILE, width), lambda b, live, order: (order[2 * b], 0)),
                pl.BlockSpec((TILE, width), lambda b, live, order: (order[2 * b + 1], 0)),
            ],
            out_specs=pl.BlockSpec((modes, width), lambda b, live, order: (0, 0)),
            scratch_shapes=[pltpu.VMEM((4 * TILE, width), jnp.bfloat16)],
        ),
        compiler_params=pltpu.CompilerParams(vmem_limit_bytes=30 * 2**20),
    )(live, order, phase, phase, sketch, sketch)


def gather_kernel(limit, count_ref, grid_ref, all_ref, counts_ref, fits_ref, info_ref, info_out, info_in):
    pt, md = lax.axis_index("pt"), lax.axis_index("md")
    barrier = pltpu.get_barrier_semaphore()
    for d in range(1, 8):
        pl.semaphore_signal(
            barrier, inc=1, device_id=((pt + d) % 8, md), device_id_type=pl.DeviceIdType.MESH
        )
    blocks = grid_ref.shape[1] // 128
    lines = [grid_ref[d : d + 1, j * 128 : (j + 1) * 128] for d in range(3) for j in range(blocks)]
    lines += [jnp.full((1, 128), count_ref[0] // 32, jnp.int32), jnp.full((1, 128), count_ref[0] % 32, jnp.int32)]
    lines += [jnp.zeros((info_ref.shape[0] - len(lines), 128), jnp.int32)]
    info_ref[...] = jnp.concatenate(lines, axis=0).astype(jnp.float32).astype(jnp.bfloat16)
    pl.semaphore_wait(barrier, 7)
    copies = []
    for d in range(1, 8):
        copy = pltpu.make_async_remote_copy(
            src_ref=info_ref, dst_ref=all_ref.at[pt], send_sem=info_out.at[d - 1], recv_sem=info_in.at[d - 1],
            device_id=((pt + d) % 8, md), device_id_type=pl.DeviceIdType.MESH,
        )
        copy.start()
        copies.append(copy)
    all_ref[pt] = info_ref[...]
    for copy in copies:
        copy.wait()
    digits = [all_ref[slab, 16:32, :].astype(jnp.float32) for slab in range(8)]
    counts = [jnp.max(digit[8:9] * 32.0 + digit[9:10]).astype(jnp.int32) for digit in digits]
    for slab in range(8):
        counts_ref[slab] = counts[slab]
    fits_ref[0] = jnp.where(sum(counts) <= limit, 1, 0)


def gather(count, grid_index, limit):
    shape = (32, 128)
    return pl.pallas_call(
        functools.partial(gather_kernel, limit),
        out_shape=(
            jax.ShapeDtypeStruct((8,) + shape, jnp.bfloat16),
            jax.ShapeDtypeStruct((8,), jnp.int32),
            jax.ShapeDtypeStruct((1,), jnp.int32),
        ),
        in_specs=[pl.BlockSpec(memory_space=pltpu.SMEM), pl.BlockSpec(memory_space=pltpu.VMEM)],
        out_specs=(pl.BlockSpec(memory_space=pltpu.VMEM),) + (pl.BlockSpec(memory_space=pltpu.SMEM),) * 2,
        scratch_shapes=[
            pltpu.VMEM(shape, jnp.bfloat16), pltpu.SemaphoreType.DMA((7,)), pltpu.SemaphoreType.DMA((7,))
        ],
        compiler_params=pltpu.CompilerParams(collective_id=1, has_side_effects=True),
    )(count, grid_index)


def compact_kernel(scale, counts_ref, all_ref, packed_ref, own_ref, mask_ref, wide_ref, line_ref):
    slots = line_ref.shape[1] - 128
    rows = own_ref.shape[0]
    pt, md = lax.axis_index("pt"), lax.axis_index("md")
    wide_ref[...] = jnp.zeros_like(wide_ref)
    line_ref[...] = jnp.zeros_like(line_ref)
    lane = lax.broadcasted_iota(jnp.int32, line_ref.shape, 1)
    start = jnp.int32(0)
    for slab in range(all_ref.shape[0]):
        base = pl.multiple_of((start // 128) * 128, 128)
        shift = start - base
        here = pl.ds(base, slots + 128)
        lines = all_ref[slab].astype(jnp.float32)
        for j in range(slots // 128):
            for d in range(3):
                at = d * (slots // 128) + j
                line_ref[d : d + 1, j * 128 : (j + 1) * 128] = lines[at : at + 1]
        wide_ref[:, here] = jnp.where(lane < shift, wide_ref[:, here], pltpu.roll(line_ref[...], shift, 1))
        start = start + counts_ref[slab]
    packed_ref[...] = wide_ref[:, : packed_ref.shape[1]]
    share = wide_ref[:, pl.ds(pl.multiple_of(pt * rows, 128), rows)]
    tall = jnp.concatenate([share, jnp.zeros((DEPTH - 8, rows), jnp.float32)], axis=0)
    own_ref[...] = tall.T.astype(jnp.bfloat16)
    slot = lax.broadcasted_iota(jnp.int32, mask_ref.shape[1:], 0) + pt * rows
    for c, (base, size) in enumerate(CHUNKS):
        mask_ref[c] = jnp.where(slot + base + md * (size // 4) < start, scale, 0.0)


def compact(scale, counts, everyone, slots):
    rows = sum(size for _, size in CHUNKS)
    total = 8 * rows
    return pl.pallas_call(
        functools.partial(compact_kernel, scale),
        out_shape=(
            jax.ShapeDtypeStruct((8, total), jnp.float32),
            jax.ShapeDtypeStruct((rows, DEPTH), jnp.bfloat16),
            jax.ShapeDtypeStruct((len(CHUNKS), LARGEST // 4, 128), jnp.float32),
        ),
        in_specs=[pl.BlockSpec(memory_space=pltpu.SMEM), pl.BlockSpec(memory_space=pltpu.VMEM)],
        out_specs=(pl.BlockSpec(memory_space=pltpu.VMEM),) * 3,
        scratch_shapes=[
            pltpu.VMEM((8, total + slots + 128), jnp.float32), pltpu.VMEM((8, slots + 128), jnp.float32)
        ],
    )(counts, everyone)


def fused_kernel(
    scale, own_ref, packed_ref, mask_ref, waves_ref, test_ref, out_ref,
    tall_ref, mine_ref, stage_ref, cast_ref, wide_waves_ref, points_ref, lhs_ref, sum_ref, keep_ref, part_ref, landed_ref,
    y_ref, phase_ref, rhs_ref,
    test_sem, sum_out, sum_in, z_out, z_in, x_out, x_in, y_out, y_in, core_out, core_in,
):
    pt, md = lax.axis_index("pt"), lax.axis_index("md")
    rows = own_ref.shape[0]
    step, width = cast_ref.shape[1], cast_ref.shape[2]
    modes = mine_ref.shape[0]
    core, x, y = pt % 2, (pt // 2) % 2, pt // 4
    core_pt, x_pt, y_pt = pt + 1 - 2 * core, pt + 2 - 4 * x, pt + 4 - 8 * y
    xy_pt = x_pt + 4 - 8 * y
    inner, upper = (md + 1) // 2 % 2, md // 2
    partner, cross = md + 1 - 2 * (md % 2), 3 - md
    pieces = [md, partner, upper * 3 + (1 - 2 * upper) * 2, upper * 3 + (1 - 2 * upper) * 3]

    def remote(source, target, out_sem, in_sem, to_pt, to_md):
        return pltpu.make_async_remote_copy(
            src_ref=source, dst_ref=target, send_sem=out_sem, recv_sem=in_sem,
            device_id=(to_pt, to_md), device_id_type=pl.DeviceIdType.MESH,
        )

    def place(slab, c, part):
        base, size = CHUNKS[c]
        first = pl.multiple_of(slab * rows + base + part * (size // 4), 32)
        return y_ref.at[pl.ds(first, size // 4), :]

    def fetch(index):
        return pltpu.make_async_copy(
            test_ref.at[pl.ds(pl.multiple_of(index * step, step), step), :], stage_ref.at[index], test_sem.at[index]
        )

    for index in range(cast_ref.shape[0]):
        fetch(index).start()
    barrier = pltpu.get_barrier_semaphore()
    for d in range(1, 4):
        pl.semaphore_signal(
            barrier, inc=1, device_id=(pt, (md + d) % 4), device_id_type=pl.DeviceIdType.MESH
        )
    for other in (core_pt, x_pt, y_pt):
        pl.semaphore_signal(barrier, inc=1, device_id=(other, md), device_id_type=pl.DeviceIdType.MESH)

    tall_ref[...] = jnp.zeros_like(tall_ref)
    tall_ref[pl.ds(0, 3), :] = waves_ref[...].astype(jnp.float32) * (1.0 / PERIOD)
    wide_waves_ref[...] = jnp.zeros_like(wide_waves_ref)
    wide_waves_ref[pl.ds(0, 16), :] = tall_ref[...].astype(jnp.bfloat16)

    def at_step(index, events):
        for step_of in sorted({when for when, _ in events}):

            @pl.when(index == step_of)
            def _(step_of=step_of):
                for when, event in events:
                    if when == step_of:
                        event()

    def sketch(c):
        base, size = CHUNKS[c]
        here = pl.ds(0, size)
        sum_ref[here, :] = jnp.zeros((size, 2 * width), jnp.float32)

        def body(index, carry):
            if c == 0:
                fetch(index).wait()
                cast_ref[index] = stage_ref[index].astype(jnp.float32).astype(jnp.bfloat16)
            for k in range(step // CHUNK):
                cols = pl.ds(pl.multiple_of(index * step + k * CHUNK, CHUNK), CHUNK)
                points = own_ref[pl.ds(base, size), :]
                turns = jnp.dot(points, wide_waves_ref[:, cols], preferred_element_type=jnp.float32)
                for at in range(0, size, STRIP):
                    re, im = phases(turns[at : at + STRIP])
                    lhs_ref[pl.ds(at, STRIP), pl.ds(k * CHUNK, CHUNK)] = re.astype(jnp.bfloat16)
                    lhs_ref[pl.ds(size + at, STRIP), pl.ds(k * CHUNK, CHUNK)] = im.astype(jnp.bfloat16)
            total = jnp.dot(lhs_ref[pl.ds(0, 2 * size), :], cast_ref[index], preferred_element_type=jnp.float32)
            sum_ref[here, pl.ds(0, width)] += total[:size]
            sum_ref[here, pl.ds(width, width)] += total[size:]
            return carry

        lax.fori_loop(0, cast_ref.shape[0], body, 0)

    def sums(c, d):
        here = pl.ds(0, CHUNKS[c][1] // 4)
        return remote(
            part_ref.at[c, d - 1, here], landed_ref.at[c, d - 1, here], sum_out.at[c, d - 1], sum_in.at[c, d - 1],
            pt, (md + d) % 4,
        )

    def share_out(c):
        quarter = CHUNKS[c][1] // 4
        here = pl.ds(0, quarter)
        for d in (2, 1, 3):
            rows_of = pl.ds(pl.multiple_of((md + d) % 4 * quarter, 16), quarter)
            part_ref[c, d - 1, here, :] = sum_ref[rows_of, :].astype(jnp.bfloat16)
            sums(c, d).start()
        keep_ref[c, here, :] = sum_ref[pl.ds(pl.multiple_of(md * quarter, 16), quarter), :]

    def up(c):
        here = place(pt, c, md)
        return remote(here, here, z_out.at[c, 0], z_in.at[c, 0], pt, partner)

    def relay(c, d):
        here = place(pt, c, pieces[d])
        landing = (1, 2, 1, 2)[d]
        return remote(here, here, z_out.at[c, 1 + d], z_in.at[c, landing], pt, cross if d < 2 else partner)

    def over(c, d, axis):
        here = place(pt, c, pieces[d])
        out_sem, in_sem, to = ((x_out, x_in, x_pt), (y_out, y_in, y_pt))[axis]
        return remote(here, here, out_sem.at[c, d], in_sem.at[c, d], to, md)

    def forward(c, d):
        if d < 2:
            here = place(x_pt, c, pieces[d])
            return remote(here, here, y_out.at[c, 4 + d], y_in.at[c, 4 + d], y_pt, md)
        here = place(y_pt, c, pieces[d])
        return remote(here, here, x_out.at[c, 2 + d], x_in.at[c, 2 + d], x_pt, md)

    def across(c, n):
        base, size = CHUNKS[c]
        here = y_ref.at[pl.ds(pl.multiple_of((pt, x_pt, y_pt, xy_pt)[n] * rows + base, 128), size), :]
        return remote(here, here, core_out.at[c, n], core_in.at[c, n], core_pt, md)

    def begin(c):
        def event():
            here = pl.ds(0, CHUNKS[c][1] // 4)
            for n in (1, 2, 3):
                sums(c, n).wait_recv()
            total = keep_ref[c, here, :]
            for n in range(3):
                total = total + landed_ref[c, n, here, :].astype(jnp.float32)
            place(pt, c, md)[...] = (total * mask_ref[c, here, :1]).astype(jnp.bfloat16)
            up(c).start()

            @pl.when(inner == 1)
            def _():
                relay(c, 0).start()

            for axis in range(2):
                over(c, 0, axis).start()

        return event

    def landed(c, d):
        piece = place(pt, c, pieces[d])
        return remote(piece, piece, z_out.at[c, 0], z_in.at[c, d - 1], pt, partner)

    def hop(c, d):
        def event():
            @pl.when(inner == 1)
            def _():
                landed(c, d).wait_recv()
                relay(c, d).start()

        return event

    def spread(c, d):
        def event():
            @pl.when(inner == 0)
            def _():
                landed(c, d).wait_recv()

            for axis in range(2):
                over(c, d, axis).start()
            if d == 3:
                across(c, 0).start()

        return event

    def pass_on(c, d):
        def event():
            over(c, d, 0).wait_recv()
            if d < 2:
                forward(c, d).start()
            over(c, d, 1).wait_recv()
            if d >= 2:
                forward(c, d).start()
            if d == 3:
                across(c, 1).start()
                across(c, 2).start()

        return event

    def corner(c, d):
        def event():
            forward(c, d).wait_recv()
            if d == 3:
                across(c, 3).start()

        return event

    def gathered(c, n):
        def event():
            across(c, n).wait_recv()

        return event

    def pair_of(nth):
        return (x + nth) % 2 + 2 * ((y + nth // 2) % 2)

    def make(events):
        per = 2 * rows // (2 * BLOCK)

        def body(nth, carry):
            index = pair_of(nth // per) * per + nth % per
            start = pl.multiple_of(index * 2 * BLOCK, 2 * BLOCK)
            coords = points_ref[:, pl.ds(start, 2 * BLOCK)]
            for k in range(modes // TILE):
                turns = jnp.dot(
                    mine_ref[pl.ds(k * TILE, TILE), :], coords, preferred_element_type=jnp.float32
                )
                for j in range(TILE // STRIP):
                    re, im = phases(turns[j * STRIP : (j + 1) * STRIP])
                    re, im = re.astype(jnp.bfloat16), im.astype(jnp.bfloat16)
                    at = pl.ds(k * TILE + j * STRIP, STRIP)
                    for h in range(2):
                        cols = slice(h * BLOCK, (h + 1) * BLOCK)
                        phase_ref[2 * index + h, at, pl.ds(0, BLOCK)] = re[:, cols]
                        phase_ref[2 * index + h, at, pl.ds(BLOCK, BLOCK)] = im[:, cols]
            at_step(nth, events)
            return carry

        lax.fori_loop(0, 4 * per, body, 0)

    def multiply(base, size, last, events):

        def body(nth, carry):
            at_step(nth, events)
            terms = []
            for h in range(2):
                slab = 2 * pair_of(nth) + h
                for b in range(size // BLOCK):
                    block = y_ref[pl.ds(pl.multiple_of(slab * rows + base + b * BLOCK, BLOCK), BLOCK), :]
                    at = 2 * BLOCK * len(terms)
                    rhs_ref[pl.ds(at, BLOCK), :] = block
                    rhs_ref[pl.ds(at + BLOCK, BLOCK), pl.ds(0, width)] = block[:, width:]
                    rhs_ref[pl.ds(at + BLOCK, BLOCK), pl.ds(width, width)] = -block[:, :width]
                    terms.append(phase_ref[slab * (rows // BLOCK) + base // BLOCK + b])
            total = jnp.dot(
                jnp.concatenate(terms, axis=1), rhs_ref[pl.ds(0, 4 * size), :], preferred_element_type=jnp.float32
            )
            if last:
                out_ref[...] = (out_ref[...] + total) * jnp.where(nth == 3, scale, 1.0)
            else:
                out_ref[...] += total
            return carry

        lax.fori_loop(0, 4, body, 0)

    sketch(0)
    pl.semaphore_wait(barrier, 6)
    share_out(0)
    mine = tall_ref[:, pl.ds(pl.multiple_of(pt * modes, modes), modes)]
    mine = jnp.concatenate([mine, jnp.zeros((DEPTH - 16, modes), jnp.float32)], axis=0)
    mine_ref[...] = mine.T.astype(jnp.bfloat16)
    points_ref[...] = jnp.zeros_like(points_ref)
    points_ref[pl.ds(0, 16), :] = jnp.concatenate(
        [packed_ref[...], jnp.zeros_like(packed_ref)], axis=0
    ).astype(jnp.bfloat16)
    out_ref[...] = jnp.zeros_like(out_ref)
    sketch(1)
    begin(0)()
    share_out(1)
    sketch(2)
    for event in (hop(0, 1), hop(0, 2), spread(0, 1), pass_on(0, 0)):
        event()
    share_out(2)
    make([(3, corner(0, 0)), (4, pass_on(0, 1)), (6, begin(1)), (8, hop(0, 3)), (8, spread(0, 2)), (8, corner(0, 1)), (9, begin(2)), (11, hop(1, 1)), (11, hop(1, 2)), (11, spread(1, 1)), (11, pass_on(1, 0)), (12, spread(0, 3)), (12, pass_on(0, 2)), (13, hop(2, 1)), (13, hop(2, 2)), (13, spread(2, 1)), (13, pass_on(2, 0)), (15, corner(0, 2)), (15, hop(1, 3)), (15, spread(1, 2)), (15, pass_on(1, 1)), (15, corner(1, 0)), (16, pass_on(0, 3)), (17, hop(2, 3)), (17, spread(2, 2)), (17, pass_on(2, 1)), (17, corner(2, 0)), (19, spread(1, 3)), (19, pass_on(1, 2)), (19, corner(1, 1)), (19, corner(0, 3))])
    multiply(0, CHUNKS[0][1], False, [(0, gathered(0, 0)), (1, spread(2, 3)), (1, pass_on(2, 2)), (1, corner(2, 1)), (1, gathered(0, 1)), (2, gathered(0, 2)), (3, pass_on(1, 3)), (3, corner(1, 2)), (3, gathered(0, 3))])
    multiply(CHUNKS[1][0], rows - CHUNKS[1][0], True, [
        (0, pass_on(2, 3)), (0, corner(2, 2)), (0, gathered(1, 0)), (0, gathered(2, 0)),
        (1, corner(1, 3)), (1, gathered(1, 1)), (1, gathered(2, 1)),
        (2, corner(2, 3)), (2, gathered(1, 2)), (2, gathered(2, 2)), (3, gathered(1, 3)), (3, gathered(2, 3)),
    ])
    for c in range(len(CHUNKS)):
        for d in (1, 2, 3):
            sums(c, d).wait_send()
        up(c).wait_send()
        for d in range(4):
            for axis in range(2):
                over(c, d, axis).wait_send()
            forward(c, d).wait_send()
            across(c, d).wait_send()

        @pl.when(inner == 1)
        def _(c=c):
            for d in range(4):
                relay(c, d).wait_send()


def fused(scale, own, packed, mask, waves, test_block):
    rows, modes, width = own.shape[0], waves.shape[1] // 8, test_block.shape[1]
    chunks, share, _ = mask.shape
    total, step = packed.shape[1], SKETCH[0]
    steps = test_block.shape[0] // step
    return pl.pallas_call(
        functools.partial(fused_kernel, scale),
        out_shape=jax.ShapeDtypeStruct((modes, 2 * width), jnp.float32),
        in_specs=[pl.BlockSpec(memory_space=pltpu.VMEM)] * 4 + [pl.BlockSpec(memory_space=pl.ANY)],
        out_specs=pl.BlockSpec(memory_space=pltpu.VMEM),
        scratch_shapes=[
            pltpu.VMEM((16, waves.shape[1]), jnp.float32),
            pltpu.VMEM((modes, DEPTH), jnp.bfloat16),
            pltpu.VMEM((steps, step, width), jnp.int32),
            pltpu.VMEM((steps, step, width), jnp.bfloat16),
            pltpu.VMEM((DEPTH, waves.shape[1]), jnp.bfloat16),
            pltpu.VMEM((DEPTH, total), jnp.bfloat16),
            pltpu.VMEM((2 * LARGEST, step), jnp.bfloat16),
            pltpu.VMEM((LARGEST, 2 * width), jnp.float32),
            pltpu.VMEM((chunks, share, 2 * width), jnp.float32),
            pltpu.VMEM((chunks, 3, share, 2 * width), jnp.bfloat16),
            pltpu.VMEM((chunks, 3, share, 2 * width), jnp.bfloat16),
            pltpu.VMEM((total, 2 * width), jnp.bfloat16),
            pltpu.VMEM((total // BLOCK, modes, 2 * BLOCK), jnp.bfloat16),
            pltpu.VMEM((4 * (rows - LARGEST), 2 * width), jnp.bfloat16),
            pltpu.SemaphoreType.DMA((steps,)),
        ]
        + [pltpu.SemaphoreType.DMA((chunks, n)) for n in (3, 3, 5, 3, 6, 6, 6, 6, 4, 4)],
        compiler_params=pltpu.CompilerParams(
            collective_id=2, has_side_effects=True, vmem_limit_bytes=60 * 2**20
        ),
    )(own, packed, mask, waves, test_block)


def padded(rows, factor):
    rows = rows.astype(jnp.float32) * factor
    return jnp.pad(rows, ((0, DEPTH - rows.shape[0]), (0, 0))).astype(jnp.bfloat16)


def sketch_part(count, points, waves, test_block, dtype):
    rows, modes, width = points.shape[0], waves.shape[1], test_block.shape[1]
    step, tile, chunk = SKETCH
    return pl.pallas_call(
        functools.partial(sketch_kernel, dtype),
        out_shape=jax.ShapeDtypeStruct((rows, 2 * width), dtype),
        grid=(modes // step,),
        in_specs=[
            pl.BlockSpec(memory_space=pltpu.SMEM),
            pl.BlockSpec((rows, DEPTH), lambda m: (0, 0)),
            pl.BlockSpec((DEPTH, step), lambda m: (0, m)),
            pl.BlockSpec((step, width), lambda m: (m, 0)),
        ],
        out_specs=pl.BlockSpec((rows, 2 * width), lambda m: (0, 0)),
        scratch_shapes=[
            pltpu.VMEM((step // chunk, tile, chunk), jnp.float32),
            pltpu.VMEM((2 * tile, step), jnp.bfloat16),
            pltpu.VMEM((rows, 2 * width), jnp.float32),
            pltpu.VMEM((step, width), jnp.bfloat16),
        ],
        compiler_params=pltpu.CompilerParams(vmem_limit_bytes=40 * 2**20),
        cost_estimate=pl.CostEstimate(
            flops=4 * rows * modes * width, bytes_accessed=4 * modes * width, transcendentals=0
        ),
    )(count, points, waves, test_block)


def adjoint_part(scale, counts, waves, points, sketch, capacity):
    modes, slots, width = waves.shape[0], points.shape[1], sketch.shape[1]
    return pl.pallas_call(
        functools.partial(adjoint_kernel, scale),
        out_shape=jax.ShapeDtypeStruct((modes, width), jnp.float32),
        grid=(slots // capacity,),
        in_specs=[
            pl.BlockSpec(memory_space=pltpu.SMEM),
            pl.BlockSpec((modes, DEPTH), lambda p: (0, 0)),
            pl.BlockSpec((DEPTH, capacity), lambda p: (0, p)),
            pl.BlockSpec((capacity, width), lambda p: (p, 0)),
        ],
        out_specs=pl.BlockSpec((modes, width), lambda p: (0, 0)),
        scratch_shapes=[
            pltpu.VMEM((modes // TILE, TILE, TILE), jnp.float32),
            pltpu.VMEM((modes // TILE, TILE, 2 * TILE), jnp.bfloat16),
            pltpu.VMEM((2 * TILE, width), jnp.bfloat16),
        ],
        compiler_params=pltpu.CompilerParams(vmem_limit_bytes=40 * 2**20),
        cost_estimate=pl.CostEstimate(
            flops=4 * modes * slots * width, bytes_accessed=2 * slots * width, transcendentals=0
        ),
    )(counts, waves, points, sketch)


def exchange_kernel(
    scale, part_ref, info_ref, waves_ref, out_ref, all_ref, phase_ref, landed_ref, points_ref, turns_ref, made_ref, made_sem,
    sum_out, sum_in, z_out, z_in, x_out, x_in, y_out, y_in, core_out, core_in, info_out, info_in,
):
    pt, md = lax.axis_index("pt"), lax.axis_index("md")
    rows = part_ref.shape[0]
    quarter = rows // 4
    core, x, y = pt % 2, (pt // 2) % 2, pt // 4
    core_pt, x_pt, y_pt = pt + 1 - 2 * core, pt + 2 - 4 * x, pt + 4 - 8 * y
    xy_pt = x_pt + 4 - 8 * y

    def send(source, target, out_sem, in_sem, to_pt, to_md):
        copy = pltpu.make_async_remote_copy(
            src_ref=source, dst_ref=target, send_sem=out_sem, recv_sem=in_sem,
            device_id=(to_pt, to_md), device_id_type=pl.DeviceIdType.MESH,
        )
        copy.start()
        return copy

    def place(slab, part):
        return out_ref.at[pl.ds(pl.multiple_of(slab * rows + part * quarter, quarter), quarter), :]

    barrier = pltpu.get_barrier_semaphore()
    for d in range(1, 4):
        pl.semaphore_signal(
            barrier, inc=1, device_id=(pt, (md + d) % 4), device_id_type=pl.DeviceIdType.MESH
        )
    for d in range(1, 8):
        pl.semaphore_signal(
            barrier, inc=1, device_id=((pt + d) % 8, md), device_id_type=pl.DeviceIdType.MESH
        )
    pl.semaphore_wait(barrier, 10)

    sums = []
    for d in (2, 1, 3):
        to = (md + d) % 4
        source = part_ref.at[pl.ds(pl.multiple_of(to * quarter, quarter), quarter), :]
        sums.append(send(source, landed_ref.at[d - 1], sum_out.at[d - 1], sum_in.at[d - 1], pt, to))
    others = [
        send(info_ref, all_ref.at[pt], info_out.at[d - 1], info_in.at[d - 1], (pt + d) % 8, md)
        for d in range(1, 8)
    ]
    all_ref[pt] = info_ref[...]
    for copy in others:
        copy.wait_recv()
    points_ref[...] = jnp.zeros_like(points_ref)
    for slab in range(8):
        points_ref[pl.ds(0, 8), pl.ds(slab * rows, rows)] = all_ref[slab].astype(jnp.float32)

    def keep(index):
        slot = index % 2
        return pltpu.make_async_copy(made_ref.at[slot], phase_ref.at[index], made_sem.at[slot])

    def make(first, last):
        def body(index, carry):
            slot = index % 2
            start = pl.multiple_of(index * TILE, TILE)
            coords = points_ref[:, pl.ds(start, TILE)].astype(jnp.bfloat16)

            if first >= 2:
                keep(index - 2).wait()
            for k in range(waves_ref.shape[0] // TILE):
                turns_ref[k] = jnp.dot(
                    waves_ref[pl.ds(k * TILE, TILE), :], coords, preferred_element_type=jnp.float32
                )
                for j in range(TILE // STRIP):
                    re, im = phases(turns_ref[k, pl.ds(j * STRIP, STRIP), :])
                    at = pl.ds(k * TILE + j * STRIP, STRIP)
                    made_ref[slot, at, pl.ds(0, TILE)] = re.astype(jnp.bfloat16)
                    made_ref[slot, at, pl.ds(TILE, TILE)] = im.astype(jnp.bfloat16)
            keep(index).start()
            return carry

        lax.fori_loop(first, last, body, 0)

    make(0, 2)
    make(2, MARKS[0])
    for copy in sums:
        copy.wait_recv()
    total = part_ref[pl.ds(pl.multiple_of(md * quarter, quarter), quarter), :].astype(jnp.float32)
    for d in range(3):
        total = total + landed_ref[d].astype(jnp.float32)
    place(pt, md)[...] = (total * scale).astype(jnp.bfloat16)

    own = place(pt, md)
    ups = [send(own, own, z_out.at[d - 1], z_in.at[d - 1], pt, (md + d) % 4) for d in (1, 2, 3)]
    pieces = [md, (md + 3) % 4, (md + 2) % 4, (md + 1) % 4]
    over_x, over_y, over_core = [], [], []
    for d in range(4):
        if d:
            ups[d - 1].wait_recv()
        here = place(pt, pieces[d])
        over_x.append(send(here, here, x_out.at[d], x_in.at[d], x_pt, md))
        over_y.append(send(here, here, y_out.at[d], y_in.at[d], y_pt, md))
        over_core.append(send(here, here, core_out.at[d], core_in.at[d], core_pt, md))
        make(MARKS[d], MARKS[d + 1])
    forward_x, forward_y = [], []
    for d in range(4):
        over_x[d].wait_recv()
        here = place(x_pt, pieces[d])
        if d < 2:
            forward_y.append(send(here, here, y_out.at[4 + d], y_in.at[4 + d], y_pt, md))
        over_core.append(send(here, here, core_out.at[4 + d], core_in.at[4 + d], core_pt, md))
        over_y[d].wait_recv()
        here = place(y_pt, pieces[d])
        if d >= 2:
            forward_x.append(send(here, here, x_out.at[2 + d], x_in.at[2 + d], x_pt, md))
        over_core.append(send(here, here, core_out.at[8 + d], core_in.at[8 + d], core_pt, md))
        make(MARKS[4 + d], MARKS[5 + d])
    for d in range(4):
        (forward_y[d] if d < 2 else forward_x[d - 2]).wait_recv()
        here = place(xy_pt, pieces[d])
        over_core.append(send(here, here, core_out.at[12 + d], core_in.at[12 + d], core_pt, md))
    make(MARKS[8], phase_ref.shape[0])
    keep(phase_ref.shape[0] - 2).wait()
    keep(phase_ref.shape[0] - 1).wait()
    for copy in over_core:
        copy.wait_recv()
    for copy in sums + others + ups + over_x + over_y + over_core + forward_x + forward_y:
        copy.wait_send()


def exchange(scale, part, info, waves):
    rows, width = part.shape
    modes = waves.shape[0]
    sems = [n for n in (3, 3, 6, 6, 16, 7) for _ in range(2)]
    return pl.pallas_call(
        functools.partial(exchange_kernel, scale),
        out_shape=(
            jax.ShapeDtypeStruct((8 * rows, width), jnp.bfloat16),
            jax.ShapeDtypeStruct((8,) + info.shape, info.dtype),
            jax.ShapeDtypeStruct((8 * rows // TILE, modes, 2 * TILE), jnp.bfloat16),
        ),
        in_specs=[pl.BlockSpec(memory_space=pltpu.VMEM)] * 3,
        out_specs=(pl.BlockSpec(memory_space=pltpu.VMEM),) * 2 + (pl.BlockSpec(memory_space=pl.ANY),),
        scratch_shapes=[
            pltpu.VMEM((3, rows // 4, width), jnp.bfloat16),
            pltpu.VMEM((DEPTH, 8 * rows), jnp.float32),
            pltpu.VMEM((modes // TILE, TILE, TILE), jnp.float32),
            pltpu.VMEM((2, modes, 2 * TILE), jnp.bfloat16),
            pltpu.SemaphoreType.DMA((2,)),
        ]
        + [pltpu.SemaphoreType.DMA((n,)) for n in sems],
        compiler_params=pltpu.CompilerParams(
            collective_id=0, has_side_effects=True, vmem_limit_bytes=32 * 2**20
        ),
    )(part, info, waves)


def per_device(grid_index, wavenumbers, test_block, slab_counts):
    capacity = grid_index.shape[1]
    n_pt, n_md = lax.axis_size("pt"), lax.axis_size("md")
    y_scale = 1.0 / (32.0 * math.sqrt(M))
    w_scale = 1.0 / math.sqrt(capacity * n_pt)
    own = wavenumbers.shape[1] // n_pt
    first = lax.axis_index("pt") * own

    def as_given():
        points = padded(grid_index, 1.0)
        waves = padded(wavenumbers, 1.0 / PERIOD)
        mine = lax.dynamic_slice_in_dim(waves, first, own, 1)
        part = sketch_part(slab_counts, points.T, waves, test_block, jnp.bfloat16)
        info = jnp.concatenate(
            [grid_index, jnp.broadcast_to(slab_counts[:, None], (5, capacity))], axis=0
        )
        sketch, gathered, phase = exchange(y_scale, part, info, mine.T)
        per_slab = (gathered[:, 3, 0] + TILE - 1) // TILE
        ends = jnp.sum(jnp.where(jnp.arange(8)[:, None] <= jnp.arange(8)[None, :], per_slab[:, None], 0), axis=0)
        nth = jnp.minimum(jnp.arange(phase.shape[0], dtype=jnp.int32), ends[7] - 1)
        past = (ends[None, :] <= nth[:, None]).astype(jnp.int32)
        slab = jnp.sum(past, axis=1)
        order = slab * (capacity // TILE) + nth - jnp.sum(past * per_slab[None, :], axis=1)
        return product(w_scale, ends[7:], order.astype(jnp.int32), phase, sketch)

    if (n_pt, n_md) == (8, 4):
        everyone, counts, fits = gather(slab_counts, grid_index, 8 * sum(size for _, size in CHUNKS))

        def packed_rows():
            packed, share, mask = compact(y_scale, counts, everyone, capacity)
            return fused(w_scale, share, packed, mask, wavenumbers, test_block)

        return lax.switch(fits[0], (as_given, packed_rows))
    points = padded(grid_index, 1.0)
    waves = padded(wavenumbers, 1.0 / PERIOD)
    mine = lax.dynamic_slice_in_dim(waves, first, own, 1)
    counts = lax.all_gather(slab_counts, "pt", tiled=True)
    all_points = lax.all_gather(grid_index, "pt", axis=1, tiled=True)
    part = sketch_part(slab_counts, points.T, waves, test_block, jnp.float32)
    share = lax.psum_scatter(part, "md", scatter_dimension=0, tiled=True)
    share = (share * y_scale).astype(jnp.bfloat16)
    sketch = lax.all_gather(share, ("pt", "md"), tiled=True)
    return adjoint_part(w_scale, counts, mine.T, padded(all_points, 1.0), sketch, capacity)


def solution(mesh):
    placed = (P(None, "pt"), P(None, "md"), P("md", None), P("pt"))
    return jax.shard_map(
        per_device, mesh=mesh, in_specs=placed, out_specs=P(("md", "pt"), None), check_vma=False
    )
```
